512 devices in a mesh: lat: 32 (over y, x), lon: 16 (over z, core).
Axes of the slice: x: 4, y: 8, z: 8, core: 2. Of those that a mesh axis runs over, the one named last changes fastest.
Arguments:
- tracers: float32 [2, 2880, 24576], P(None, 'lon', 'lat'), may hold values from -6 to 6
- wind_field: float32 [2, 2, 1024, 2880], P(None, None, 'lat', 'lon'), may hold values from -4 to 4
Outputs:
- advected: float32 [2, 2880, 24576], P(None, 'lon', 'lat')
- smoothed_winds: float32 [2, 2, 1024, 2880], P(None, None, 'lat', 'lon')
The draws below stay inside these ranges and needn't reach their ends.
All inputs are finite; a program needn't handle non-finite values.
Results may differ from the reference program's by a relative error of at most 0.00007.
Values sent between devices are 32-bit elements; how exact they have to be, the bound alone decides.
A program may use at most 64 MiB of HBM per device.

```python
import math
import jax
import jax.numpy as jnp
from jax import lax

NTR = 24
NLON = 2880
LEV = 2
NLAT = 1024


def steps_of(rng, shape, split, low, top_value):
    loudness, own = 1.0, jax.random.fold_in(rng, 6)
    for dim, parts in split:
        steps = jnp.exp(jax.random.uniform(jax.random.fold_in(own, dim), (parts,), jnp.float32, low / len(split), top_value / len(split)))
        loudness = loudness * jnp.repeat(steps, shape[dim] // parts).reshape([-1 if axis == dim else 1 for axis in range(len(shape))])
    return loudness


def centred(rng, extent, scale, reach, pieces=(), kind=jnp.bfloat16):
    factor_of = steps_of(rng, extent, pieces, -0.22, 0.18) if pieces else 1.0
    values = jax.random.normal(rng, extent, jnp.float32) * scale * factor_of
    return jnp.minimum(jnp.maximum(values, -reach), reach).astype(kind)


def setup_inputs(seed: int = 0) -> dict:
    splits = jax.random.split(jax.random.key(seed), 3)
    tracers = centred(splits[0], (LEV, NLON, NLAT * NTR), 1.0, 6.0, ((1, 16), (2, 32)), jnp.float32)
    wind_field = centred(splits[1], (2, LEV, NLAT, NLON), 1.0, 4.0, ((2, 32), (3, 16)), jnp.float32)
    return {"tracers": tracers, "wind_field": wind_field}


COURANT = 0.3
COS_FLOOR = 0.5


def damping(row_cosine, wavenumber, lon_total):
    sine = jnp.sin(wavenumber.astype(jnp.float32) * (math.pi / lon_total))
    divisor = jnp.where(wavenumber == 0, 1.0, sine * sine)
    scaled = (row_cosine / COS_FLOOR) ** 2
    scaled = scaled.reshape(scaled.shape + (1,) * wavenumber.ndim)
    return jnp.where(wavenumber == 0, 1.0, jnp.minimum(1.0, scaled / divisor))


def face_values(padded, axis, cells):
    def offset_cells(offset):
        return lax.slice_in_dim(padded, offset, offset + cells + 1, axis=axis)
    left = (2.0 * offset_cells(0) - 13.0 * offset_cells(1) + 47.0 * offset_cells(2) + 27.0 * offset_cells(3) - 3.0 * offset_cells(4)) / 60.0
    right = (2.0 * offset_cells(5) - 13.0 * offset_cells(4) + 47.0 * offset_cells(3) + 27.0 * offset_cells(2) - 3.0 * offset_cells(1)) / 60.0
    return left, right


def upwind(speed, left, right):
    return jnp.maximum(speed, 0.0) * left + jnp.minimum(speed, 0.0) * right


def reference(tracers, wind_field):
    levels, lon_total, merged = tracers.shape
    lat_total = wind_field.shape[2]
    tracer_count = merged // lat_total
    fields = tracers.reshape(levels, lon_total, lat_total, tracer_count).transpose(3, 0, 2, 1)
    row_ids = jnp.arange(lat_total, dtype=jnp.int32)
    row_cosine = jnp.cos((row_ids.astype(jnp.float32) + 0.5) * (math.pi / lat_total) - 0.5 * math.pi)
    wavenumber = jnp.arange(lon_total, dtype=jnp.int32)
    factor = damping(row_cosine, wavenumber, lon_total)
    spectra = jnp.fft.fft(wind_field, axis=-1)
    smoothed = jnp.real(jnp.fft.ifft(spectra * factor[None, None], axis=-1)).astype(jnp.float32)
    east_pad = jnp.pad(smoothed[0], ((0, 0), (0, 0), (3, 3)), mode="wrap")
    zonal_speed = 0.5 * (east_pad[:, :, 2:lon_total + 3] + east_pad[:, :, 3:lon_total + 4])
    north_pad = jnp.pad(smoothed[1], ((0, 0), (3, 3), (0, 0)))
    face_ids = jnp.arange(lat_total + 1, dtype=jnp.int32)
    face_cosine = jnp.cos(face_ids.astype(jnp.float32) * (math.pi / lat_total) - 0.5 * math.pi)
    face_cosine = jnp.where((face_ids == 0) | (face_ids == lat_total), 0.0, face_cosine)
    merid_speed = 0.5 * (north_pad[:, 2:lat_total + 3] + north_pad[:, 3:lat_total + 4]) * face_cosine[None, :, None]
    metric = 1.0 / jnp.maximum(row_cosine, COS_FLOOR)

    def advance(field):
        zonal_pad = jnp.pad(field, ((0, 0), (0, 0), (3, 3)), mode="wrap")
        left_x, right_x = face_values(zonal_pad, 2, lon_total)
        zonal_flux = upwind(zonal_speed, left_x, right_x)
        merid_pad = jnp.pad(field, ((0, 0), (3, 3), (0, 0)))
        left_y, right_y = face_values(merid_pad, 1, lat_total)
        merid_flux = upwind(merid_speed, left_y, right_y)
        change = COURANT * (zonal_flux[:, :, 1:] - zonal_flux[:, :, :-1]) + COURANT * (merid_flux[:, 1:] - merid_flux[:, :-1])
        return field - metric[None, :, None] * change

    advected = lax.map(advance, fields)
    advected = advected.transpose(1, 3, 2, 0).reshape(levels, lon_total, lat_total * tracer_count)
    return advected, smoothed
```

```python
import functools
import math

import jax
import jax.numpy as jnp
from jax import lax
from jax.experimental import pallas as pl
from jax.experimental.pallas import tpu as pltpu
from jax.sharding import PartitionSpec as P

MESH = pl.DeviceIdType.MESH

COURANT = 0.3
COS_FLOOR = 0.5
EXACT_MODE = lax.Precision.HIGHEST


def extended(array, sides, width, wrap):
    for axis, dim in sides:
        devices, length = (lax.axis_size(axis), array.shape[dim])
        up = [(i, (i + 1) % devices) for i in range(devices if wrap else devices - 1)]
        down = [(j, i) for i, j in up]
        last = lax.slice_in_dim(array, length - width, length, axis=dim)
        first = lax.slice_in_dim(array, 0, width, axis=dim)
        before = lax.ppermute(last, axis, up)
        after = lax.ppermute(first, axis, down)
        array = jnp.concatenate([before, array, after], axis=dim)
    return array


def damping(row_cosine, wavenumber, lon_total):
    sine = jnp.sin(wavenumber.astype(jnp.float32) * (math.pi / lon_total))
    divisor = jnp.where(wavenumber == 0, 1.0, sine * sine)
    scaled = (row_cosine / COS_FLOOR) ** 2
    scaled = scaled.reshape(scaled.shape + (1,) * wavenumber.ndim)
    return jnp.where(wavenumber == 0, 1.0, jnp.minimum(1.0, scaled / divisor))


def face_values(padded, axis, cells, stride):

    def offset_cells(offset):
        return lax.slice_in_dim(padded, offset * stride, (offset + cells + 1) * stride, axis=axis)

    left = (
        2.0 * offset_cells(0)
        - 13.0 * offset_cells(1)
        + 47.0 * offset_cells(2)
        + 27.0 * offset_cells(3)
        - 3.0 * offset_cells(4)
    ) / 60.0
    right = (
        2.0 * offset_cells(5)
        - 13.0 * offset_cells(4)
        + 47.0 * offset_cells(3)
        + 27.0 * offset_cells(2)
        - 3.0 * offset_cells(1)
    ) / 60.0
    return (left, right)


def upwind(speed, left, right):
    return jnp.maximum(speed, 0.0) * left + jnp.minimum(speed, 0.0) * right


def apply_table(values, table):
    return jnp.einsum("rkm,mb->rkb", values, table, precision=EXACT_MODE)


def filter_modes(real_part, imag_part, lon_block, row_cosine, lon_total):
    columns = real_part.shape[-1]
    blocks = lon_total // columns
    column_ids = jnp.arange(columns, dtype=jnp.int32)
    twist = (
        2.0
        * math.pi
        * (column_ids[None, :] * lon_block[:, None] % lon_total).astype(jnp.float32)
        / lon_total
    )
    twist_cos = jnp.cos(twist)
    twist_sin = jnp.sin(twist)
    shifted_re = real_part * twist_cos + imag_part * twist_sin
    shifted_im = imag_part * twist_cos - real_part * twist_sin
    table_turn = (
        2.0
        * math.pi
        * (column_ids[:, None] * column_ids[None, :] % columns).astype(jnp.float32)
        / columns
    )
    table_cos = jnp.cos(table_turn)
    table_sin = jnp.sin(table_turn)
    modes_re = apply_table(shifted_re, table_cos) + apply_table(shifted_im, table_sin)
    modes_im = apply_table(shifted_im, table_cos) - apply_table(shifted_re, table_sin)
    wavenumber = lon_block[:, None] + blocks * column_ids[None, :]
    factor = damping(row_cosine, wavenumber, lon_total)
    modes_re = modes_re * factor
    modes_im = modes_im * factor
    back_re = apply_table(modes_re, table_cos) - apply_table(modes_im, table_sin)
    back_im = apply_table(modes_im, table_cos) + apply_table(modes_re, table_sin)
    return (back_re * twist_cos - back_im * twist_sin, back_im * twist_cos + back_re * twist_sin)


def exchange_kernel(n, x_ref, o_ref, send_sem, recv_sem):
    me = lax.axis_index("lon")
    band = lax.axis_index("lat")
    barrier = pltpu.get_barrier_semaphore()
    for k in range(1, n):
        peer = lax.rem(me + k, n)
        pl.semaphore_signal(barrier, inc=1, device_id=(band, peer), device_id_type=MESH)
    pl.semaphore_wait(barrier, n - 1)
    sends = []
    for k in range(1, n):
        peer = lax.rem(me + k, n)
        copy = pltpu.make_async_remote_copy(
            src_ref=x_ref.at[peer],
            dst_ref=o_ref.at[me],
            send_sem=send_sem.at[peer],
            recv_sem=recv_sem.at[me],
            device_id=(band, peer),
            device_id_type=MESH,
        )
        copy.start()
        sends.append(copy)
    o_ref[me] = x_ref[me]
    for k in range(1, n):
        source = lax.rem(me + n - k, n)
        pltpu.make_async_remote_copy(
            src_ref=x_ref.at[source],
            dst_ref=o_ref.at[source],
            send_sem=send_sem.at[source],
            recv_sem=recv_sem.at[source],
            device_id=(band, source),
            device_id_type=MESH,
        ).wait_recv()
    for copy in sends:
        copy.wait_send()


def exchange(blocks, collective):
    n = blocks.shape[0]
    return pl.pallas_call(
        functools.partial(exchange_kernel, n),
        out_shape=jax.ShapeDtypeStruct(blocks.shape, blocks.dtype),
        in_specs=[pl.BlockSpec(memory_space=pltpu.VMEM)],
        out_specs=pl.BlockSpec(memory_space=pltpu.VMEM),
        scratch_shapes=[pltpu.SemaphoreType.DMA((n,)), pltpu.SemaphoreType.DMA((n,))],
        compiler_params=pltpu.CompilerParams(collective_id=collective, has_side_effects=True),
    )(blocks)


def spectral(flat_winds, row_cosine, lon_total):
    flat_rows, columns = flat_winds.shape
    lon_count = lax.axis_size("lon")
    lon_index = lax.axis_index("lon")
    row_share = flat_rows // lon_count
    gathered = exchange(flat_winds.reshape(lon_count, row_share, columns), 0)
    own_cosine = lax.dynamic_slice_in_dim(row_cosine, lon_index * row_share, row_share, 0)
    block_ids = jnp.arange(lon_count, dtype=jnp.int32)
    phase_angle = (
        2.0
        * math.pi
        * (block_ids[:, None] * block_ids[None, :] % lon_count).astype(jnp.float32)
        / lon_count
    )
    phase_cos = jnp.cos(phase_angle)
    phase_sin = jnp.sin(phase_angle)
    real_part = jnp.einsum("prm,pk->rkm", gathered, phase_cos, precision=EXACT_MODE)
    imag_part = -jnp.einsum("prm,pk->rkm", gathered, phase_sin, precision=EXACT_MODE)
    out_re, out_im = filter_modes(real_part, imag_part, block_ids, own_cosine, lon_total)
    restored = (
        jnp.einsum("rkm,kp->prm", out_re, phase_cos, precision=EXACT_MODE)
        - jnp.einsum("rkm,kp->prm", out_im, phase_sin, precision=EXACT_MODE)
    ) / lon_total
    return exchange(restored, 1).reshape(flat_rows, columns)


def local(tracers, wind_field):
    levels, lon_cols, merged = tracers.shape
    lat_rows = wind_field.shape[2]
    tracer_count = merged // lat_rows
    lon_total = lon_cols * lax.axis_size("lon")
    lat_total = lat_rows * lax.axis_size("lat")
    first_row = lax.axis_index("lat") * lat_rows
    row_ids = first_row + jnp.arange(lat_rows, dtype=jnp.int32)
    row_cosine = jnp.cos(
        (row_ids.astype(jnp.float32) + 0.5) * (math.pi / lat_total) - 0.5 * math.pi
    )
    flat_winds = wind_field.reshape(2 * levels * lat_rows, lon_cols)
    flat_cosine = jnp.tile(row_cosine, 2 * levels)
    smoothed = spectral(flat_winds, flat_cosine, lon_total)
    smoothed = smoothed.reshape(2, levels, lat_rows, lon_cols)
    east_turned = jnp.transpose(smoothed[0], (0, 2, 1))
    north_turned = jnp.transpose(smoothed[1], (0, 2, 1))
    zonal_stack = jnp.concatenate([tracers, east_turned], axis=2)
    zonal_pad = extended(zonal_stack, (("lon", 1),), 3, True)
    east_wind = zonal_pad[:, :, merged:]
    zonal_speed = 0.5 * (east_wind[:, 2 : lon_cols + 3] + east_wind[:, 3 : lon_cols + 4])
    zonal_speed = jnp.repeat(zonal_speed, tracer_count, axis=2)
    left_x, right_x = face_values(zonal_pad[:, :, :merged], 1, lon_cols, 1)
    zonal_flux = upwind(zonal_speed, left_x, right_x)
    slot_count = tracer_count + 1
    merid_stack = jnp.concatenate(
        [tracers.reshape(levels, lon_cols, lat_rows, tracer_count), north_turned[..., None]], axis=3
    )
    merid_stack = merid_stack.reshape(levels, lon_cols, lat_rows * slot_count)
    merid_pad = extended(merid_stack, (("lat", 2),), 3 * slot_count, False)
    merid_pad = merid_pad.reshape(levels, lon_cols, lat_rows + 6, slot_count)
    north_wind = merid_pad[..., tracer_count]
    tracer_pad = merid_pad[..., :tracer_count].reshape(
        levels, lon_cols, (lat_rows + 6) * tracer_count
    )
    face_ids = first_row + jnp.arange(lat_rows + 1, dtype=jnp.int32)
    face_cosine = jnp.cos(face_ids.astype(jnp.float32) * (math.pi / lat_total) - 0.5 * math.pi)
    face_cosine = jnp.where((face_ids == 0) | (face_ids == lat_total), 0.0, face_cosine)
    merid_speed = (
        0.5
        * (north_wind[:, :, 2 : lat_rows + 3] + north_wind[:, :, 3 : lat_rows + 4])
        * face_cosine[None, None, :]
    )
    merid_speed = jnp.repeat(merid_speed, tracer_count, axis=2)
    left_y, right_y = face_values(tracer_pad, 2, lat_rows, tracer_count)
    merid_flux = upwind(merid_speed, left_y, right_y)
    metric = jnp.repeat(1.0 / jnp.maximum(row_cosine, COS_FLOOR), tracer_count)
    change = COURANT * (zonal_flux[:, 1:] - zonal_flux[:, :-1]) + COURANT * (
        merid_flux[:, :, tracer_count:] - merid_flux[:, :, :-tracer_count]
    )
    advected = tracers - metric[None, None, :] * change
    return (advected, smoothed)


def solution(mesh):
    placed = (P(None, "lon", "lat"), P(None, None, "lat", "lon"))
    return jax.shard_map(
        local,
        mesh=mesh,
        in_specs=placed,
        out_specs=(P(None, "lon", "lat"), P(None, None, "lat", "lon")),
        check_vma=False,
    )
```

```python
import functools
import math

import jax
import jax.numpy as jnp
from jax import lax
from jax.experimental import pallas as pl
from jax.experimental.pallas import tpu as pltpu
from jax.sharding import PartitionSpec as P

MESH = pl.DeviceIdType.MESH

COURANT = 0.3
COS_FLOOR = 0.5
EXACT_MODE = lax.Precision.HIGHEST


def extended(array, sides, width, wrap):
    for axis, dim in sides:
        devices, length = (lax.axis_size(axis), array.shape[dim])
        up = [(i, (i + 1) % devices) for i in range(devices if wrap else devices - 1)]
        down = [(j, i) for i, j in up]
        last = lax.slice_in_dim(array, length - width, length, axis=dim)
        first = lax.slice_in_dim(array, 0, width, axis=dim)
        before = lax.ppermute(last, axis, up)
        after = lax.ppermute(first, axis, down)
        array = jnp.concatenate([before, array, after], axis=dim)
    return array


def damping(row_cosine, wavenumber, lon_total):
    sine = jnp.sin(wavenumber.astype(jnp.float32) * (math.pi / lon_total))
    divisor = jnp.where(wavenumber == 0, 1.0, sine * sine)
    scaled = (row_cosine / COS_FLOOR) ** 2
    scaled = scaled.reshape(scaled.shape + (1,) * wavenumber.ndim)
    return jnp.where(wavenumber == 0, 1.0, jnp.minimum(1.0, scaled / divisor))


def face_values(padded, axis, cells, stride):

    def offset_cells(offset):
        return lax.slice_in_dim(padded, offset * stride, (offset + cells + 1) * stride, axis=axis)

    left = (
        2.0 * offset_cells(0)
        - 13.0 * offset_cells(1)
        + 47.0 * offset_cells(2)
        + 27.0 * offset_cells(3)
        - 3.0 * offset_cells(4)
    ) / 60.0
    right = (
        2.0 * offset_cells(5)
        - 13.0 * offset_cells(4)
        + 47.0 * offset_cells(3)
        + 27.0 * offset_cells(2)
        - 3.0 * offset_cells(1)
    ) / 60.0
    return (left, right)


def upwind(speed, left, right):
    return jnp.maximum(speed, 0.0) * left + jnp.minimum(speed, 0.0) * right


def apply_table(values, table):
    return jnp.einsum("rkm,mb->rkb", values, table, precision=EXACT_MODE)


def filter_modes(real_part, imag_part, lon_block, row_cosine, lon_total):
    columns = real_part.shape[-1]
    blocks = lon_total // columns
    column_ids = jnp.arange(columns, dtype=jnp.int32)
    twist = (
        2.0
        * math.pi
        * (column_ids[None, :] * lon_block[:, None] % lon_total).astype(jnp.float32)
        / lon_total
    )
    twist_cos = jnp.cos(twist)
    twist_sin = jnp.sin(twist)
    shifted_re = real_part * twist_cos + imag_part * twist_sin
    shifted_im = imag_part * twist_cos - real_part * twist_sin
    table_turn = (
        2.0
        * math.pi
        * (column_ids[:, None] * column_ids[None, :] % columns).astype(jnp.float32)
        / columns
    )
    table_cos = jnp.cos(table_turn)
    table_sin = jnp.sin(table_turn)
    modes_re = apply_table(shifted_re, table_cos) + apply_table(shifted_im, table_sin)
    modes_im = apply_table(shifted_im, table_cos) - apply_table(shifted_re, table_sin)
    wavenumber = lon_block[:, None] + blocks * column_ids[None, :]
    factor = damping(row_cosine, wavenumber, lon_total)
    modes_re = modes_re * factor
    modes_im = modes_im * factor
    back_re = apply_table(modes_re, table_cos) - apply_table(modes_im, table_sin)
    back_im = apply_table(modes_im, table_cos) + apply_table(modes_re, table_sin)
    return (back_re * twist_cos - back_im * twist_sin, back_im * twist_cos + back_re * twist_sin)


def exchange_kernel(n, x_ref, o_ref, send_sem, recv_sem):
    me = lax.axis_index("lon")
    band = lax.axis_index("lat")
    barrier = pltpu.get_barrier_semaphore()
    for k in range(1, n):
        peer = lax.rem(me + k, n)
        pl.semaphore_signal(barrier, inc=1, device_id=(band, peer), device_id_type=MESH)
    pl.semaphore_wait(barrier, n - 1)
    sends = []
    for k in range(1, n):
        peer = lax.rem(me + k, n)
        copy = pltpu.make_async_remote_copy(
            src_ref=x_ref.at[peer],
            dst_ref=o_ref.at[me],
            send_sem=send_sem.at[peer],
            recv_sem=recv_sem.at[me],
            device_id=(band, peer),
            device_id_type=MESH,
        )
        copy.start()
        sends.append(copy)
    o_ref[me] = x_ref[me]
    for k in range(1, n):
        source = lax.rem(me + n - k, n)
        pltpu.make_async_remote_copy(
            src_ref=x_ref.at[source],
            dst_ref=o_ref.at[source],
            send_sem=send_sem.at[source],
            recv_sem=recv_sem.at[source],
            device_id=(band, source),
            device_id_type=MESH,
        ).wait_recv()
    for copy in sends:
        copy.wait_send()


def exchange(blocks, collective):
    n = blocks.shape[0]
    return pl.pallas_call(
        functools.partial(exchange_kernel, n),
        out_shape=jax.ShapeDtypeStruct(blocks.shape, blocks.dtype),
        in_specs=[pl.BlockSpec(memory_space=pltpu.VMEM)],
        out_specs=pl.BlockSpec(memory_space=pltpu.VMEM),
        scratch_shapes=[pltpu.SemaphoreType.DMA((n,)), pltpu.SemaphoreType.DMA((n,))],
        compiler_params=pltpu.CompilerParams(collective_id=collective, has_side_effects=True),
    )(blocks)


def spectral(flat_winds, row_cosine, lon_total):
    flat_rows, columns = flat_winds.shape
    lon_count = lax.axis_size("lon")
    lon_index = lax.axis_index("lon")
    row_share = flat_rows // lon_count
    gathered = exchange(flat_winds.reshape(lon_count, row_share, columns), 0)
    own_cosine = lax.dynamic_slice_in_dim(row_cosine, lon_index * row_share, row_share, 0)
    block_ids = jnp.arange(lon_count, dtype=jnp.int32)
    phase_angle = (
        2.0
        * math.pi
        * (block_ids[:, None] * block_ids[None, :] % lon_count).astype(jnp.float32)
        / lon_count
    )
    phase_cos = jnp.cos(phase_angle)
    phase_sin = jnp.sin(phase_angle)
    real_part = jnp.einsum("prm,pk->rkm", gathered, phase_cos, precision=EXACT_MODE)
    imag_part = -jnp.einsum("prm,pk->rkm", gathered, phase_sin, precision=EXACT_MODE)
    out_re, out_im = filter_modes(real_part, imag_part, block_ids, own_cosine, lon_total)
    restored = (
        jnp.einsum("rkm,kp->prm", out_re, phase_cos, precision=EXACT_MODE)
        - jnp.einsum("rkm,kp->prm", out_im, phase_sin, precision=EXACT_MODE)
    ) / lon_total
    return exchange(restored, 1).reshape(flat_rows, columns)


def halo(array, axis, dim, width, wrap):
    devices, length = (lax.axis_size(axis), array.shape[dim])
    up = [(i, (i + 1) % devices) for i in range(devices if wrap else devices - 1)]
    down = [(j, i) for i, j in up]
    before = lax.ppermute(lax.slice_in_dim(array, length - width, length, axis=dim), axis, up)
    after = lax.ppermute(lax.slice_in_dim(array, 0, width, axis=dim), axis, down)
    return before, after


def stencil(padded, dim, faces, stride):

    def offset_cells(offset):
        return lax.slice_in_dim(padded, offset * stride, (offset + faces) * stride, axis=dim)

    left = (
        2.0 * offset_cells(0)
        - 13.0 * offset_cells(1)
        + 47.0 * offset_cells(2)
        + 27.0 * offset_cells(3)
        - 3.0 * offset_cells(4)
    ) / 60.0
    right = (
        2.0 * offset_cells(5)
        - 13.0 * offset_cells(4)
        + 47.0 * offset_cells(3)
        + 27.0 * offset_cells(2)
        - 3.0 * offset_cells(1)
    ) / 60.0
    return left, right


def spread(values, rows, tracer_count):
    lanes = jnp.arange(rows * tracer_count, dtype=jnp.int32) // tracer_count
    pick = (jnp.arange(rows, dtype=jnp.int32)[:, None] == lanes[None, :]).astype(jnp.float32)
    return jnp.einsum("ljc,jm->lcm", values, pick, precision=EXACT_MODE)


def local(tracers, wind_field):
    levels, lon_cols, merged = tracers.shape
    lat_rows = wind_field.shape[2]
    tracer_count = merged // lat_rows
    lon_total = lon_cols * lax.axis_size("lon")
    lat_total = lat_rows * lax.axis_size("lat")
    first_row = lax.axis_index("lat") * lat_rows
    west, east = halo(tracers, "lon", 1, 3, True)
    south, north = halo(tracers, "lat", 2, 3 * tracer_count, False)
    row_ids = first_row + jnp.arange(lat_rows, dtype=jnp.int32)
    row_cosine = jnp.cos(
        (row_ids.astype(jnp.float32) + 0.5) * (math.pi / lat_total) - 0.5 * math.pi
    )
    flat_winds = wind_field.reshape(2 * levels * lat_rows, lon_cols)
    flat_cosine = jnp.tile(row_cosine, 2 * levels)
    smoothed = spectral(flat_winds, flat_cosine, lon_total)
    smoothed = smoothed.reshape(2, levels, lat_rows, lon_cols)
    east_wind, north_wind = smoothed[0], smoothed[1]
    u_west, u_east = halo(east_wind, "lon", 2, 1, True)
    v_south, v_north = halo(north_wind, "lat", 1, 1, False)
    u_pad = jnp.concatenate([u_west, east_wind, u_east], axis=2)
    zonal_speed = 0.5 * (u_pad[:, :, : lon_cols + 1] + u_pad[:, :, 1:])
    v_pad = jnp.concatenate([v_south, north_wind, v_north], axis=1)
    face_ids = first_row + jnp.arange(lat_rows + 1, dtype=jnp.int32)
    face_cosine = jnp.cos(face_ids.astype(jnp.float32) * (math.pi / lat_total) - 0.5 * math.pi)
    face_cosine = jnp.where((face_ids == 0) | (face_ids == lat_total), 0.0, face_cosine)
    merid_speed = 0.5 * (v_pad[:, : lat_rows + 1] + v_pad[:, 1:]) * face_cosine[None, :, None]
    zonal_rep = spread(zonal_speed, lat_rows, tracer_count)
    merid_rep = spread(merid_speed, lat_rows + 1, tracer_count)
    zonal_pad = jnp.concatenate([west, tracers, east], axis=1)
    left_x, right_x = stencil(zonal_pad, 1, lon_cols + 1, 1)
    zonal_flux = upwind(zonal_rep, left_x, right_x)
    merid_pad = jnp.concatenate([south, tracers, north], axis=2)
    left_y, right_y = stencil(merid_pad, 2, lat_rows + 1, tracer_count)
    merid_flux = upwind(merid_rep, left_y, right_y)
    metric = jnp.repeat(1.0 / jnp.maximum(row_cosine, COS_FLOOR), tracer_count)
    change = COURANT * (zonal_flux[:, 1:] - zonal_flux[:, :-1]) + COURANT * (
        merid_flux[:, :, tracer_count:] - merid_flux[:, :, :-tracer_count]
    )
    advected = tracers - metric[None, None, :] * change
    return (advected, smoothed)


def solution(mesh):
    placed = (P(None, "lon", "lat"), P(None, None, "lat", "lon"))
    return jax.shard_map(
        local,
        mesh=mesh,
        in_specs=placed,
        out_specs=(P(None, "lon", "lat"), P(None, None, "lat", "lon")),
        check_vma=False,
    )
```

```python
import functools
import math

import jax
import jax.numpy as jnp
from jax import lax
from jax.experimental import pallas as pl
from jax.experimental.pallas import tpu as pltpu
from jax.sharding import PartitionSpec as P

MESH = pl.DeviceIdType.MESH

COURANT = 0.3
COS_FLOOR = 0.5
EXACT_MODE = lax.Precision.HIGHEST


def extended(array, sides, width, wrap):
    for axis, dim in sides:
        devices, length = (lax.axis_size(axis), array.shape[dim])
        up = [(i, (i + 1) % devices) for i in range(devices if wrap else devices - 1)]
        down = [(j, i) for i, j in up]
        last = lax.slice_in_dim(array, length - width, length, axis=dim)
        first = lax.slice_in_dim(array, 0, width, axis=dim)
        before = lax.ppermute(last, axis, up)
        after = lax.ppermute(first, axis, down)
        array = jnp.concatenate([before, array, after], axis=dim)
    return array


def damping(row_cosine, wavenumber, lon_total):
    sine = jnp.sin(wavenumber.astype(jnp.float32) * (math.pi / lon_total))
    divisor = jnp.where(wavenumber == 0, 1.0, sine * sine)
    scaled = (row_cosine / COS_FLOOR) ** 2
    scaled = scaled.reshape(scaled.shape + (1,) * wavenumber.ndim)
    return jnp.where(wavenumber == 0, 1.0, jnp.minimum(1.0, scaled / divisor))


def face_values(padded, axis, cells, stride):

    def offset_cells(offset):
        return lax.slice_in_dim(padded, offset * stride, (offset + cells + 1) * stride, axis=axis)

    left = (
        2.0 * offset_cells(0)
        - 13.0 * offset_cells(1)
        + 47.0 * offset_cells(2)
        + 27.0 * offset_cells(3)
        - 3.0 * offset_cells(4)
    ) / 60.0
    right = (
        2.0 * offset_cells(5)
        - 13.0 * offset_cells(4)
        + 47.0 * offset_cells(3)
        + 27.0 * offset_cells(2)
        - 3.0 * offset_cells(1)
    ) / 60.0
    return (left, right)


def upwind(speed, left, right):
    return jnp.maximum(speed, 0.0) * left + jnp.minimum(speed, 0.0) * right


def filter_kernel(n, rows, winds_ref, kc_ref, ks_ref, tc_ref, ts_ref, c_ref, s_ref, factor_ref,
                  out_ref, gathered, restored, send_a, recv_a, send_b, recv_b):
    me = lax.axis_index("lon")
    band = lax.axis_index("lat")
    barrier = pltpu.get_barrier_semaphore()
    for k in range(1, n):
        peer = lax.rem(me + k, n)
        pl.semaphore_signal(barrier, inc=1, device_id=(band, peer), device_id_type=MESH)
    pl.semaphore_wait(barrier, n - 1)

    def block(ref, index):
        return ref.at[pl.ds(pl.multiple_of(index * rows, rows), rows)]

    def swap(source, target, send_sem, recv_sem):
        sends = []
        for k in range(1, n):
            peer = lax.rem(me + k, n)
            copy = pltpu.make_async_remote_copy(
                src_ref=block(source, peer),
                dst_ref=block(target, me),
                send_sem=send_sem.at[peer],
                recv_sem=recv_sem.at[me],
                device_id=(band, peer),
                device_id_type=MESH,
            )
            copy.start()
            sends.append(copy)
        block(target, me)[...] = block(source, me)[...]
        for k in range(1, n):
            origin = lax.rem(me + n - k, n)
            pltpu.make_async_remote_copy(
                src_ref=block(source, origin),
                dst_ref=block(target, origin),
                send_sem=send_sem.at[origin],
                recv_sem=recv_sem.at[origin],
                device_id=(band, origin),
                device_id_type=MESH,
            ).wait_recv()
        for copy in sends:
            copy.wait_send()

    swap(winds_ref, gathered, send_a, recv_a)

    def mm(a, b):
        return jnp.dot(a, b, precision=EXACT_MODE, preferred_element_type=jnp.float32)

    x = gathered[...]
    kc, ks = kc_ref[...], ks_ref[...]
    tc, ts = tc_ref[...], ts_ref[...]
    c, s = c_ref[...], s_ref[...]
    re = mm(kc, x)
    im = -mm(ks, x)
    shifted_re = re * tc + im * ts
    shifted_im = im * tc - re * ts
    modes_re = mm(shifted_re, c) + mm(shifted_im, s)
    modes_im = mm(shifted_im, c) - mm(shifted_re, s)
    factor = factor_ref[...]
    modes_re = modes_re * factor
    modes_im = modes_im * factor
    back_re = mm(modes_re, c) - mm(modes_im, s)
    back_im = mm(modes_im, c) + mm(modes_re, s)
    out_re = back_re * tc - back_im * ts
    out_im = back_im * tc + back_re * ts
    restored[...] = (mm(kc, out_re) - mm(ks, out_im)) / (n * x.shape[1])
    swap(restored, out_ref, send_b, recv_b)


def spectral(flat_winds, row_cosine, lon_total):
    flat_rows, columns = flat_winds.shape
    n = lax.axis_size("lon")
    lon_index = lax.axis_index("lon")
    rows = flat_rows // n
    own_cosine = lax.dynamic_slice_in_dim(row_cosine, lon_index * rows, rows, 0)
    block_ids = jnp.arange(n, dtype=jnp.int32)
    phase = 2.0 * math.pi * (block_ids[:, None] * block_ids[None, :] % n).astype(jnp.float32) / n
    eye = jnp.eye(rows, dtype=jnp.float32)
    kron_cos = jnp.kron(jnp.cos(phase), eye)
    kron_sin = jnp.kron(jnp.sin(phase), eye)
    column_ids = jnp.arange(columns, dtype=jnp.int32)
    twist = (
        2.0
        * math.pi
        * (column_ids[None, :] * block_ids[:, None] % lon_total).astype(jnp.float32)
        / lon_total
    )
    twist_cos = jnp.repeat(jnp.cos(twist), rows, axis=0)
    twist_sin = jnp.repeat(jnp.sin(twist), rows, axis=0)
    table_turn = (
        2.0
        * math.pi
        * (column_ids[:, None] * column_ids[None, :] % columns).astype(jnp.float32)
        / columns
    )
    wavenumber = block_ids[:, None] + n * column_ids[None, :]
    factor = damping(own_cosine, wavenumber, lon_total)
    factor = jnp.transpose(factor, (1, 0, 2)).reshape(n * rows, columns)
    vmem = pl.BlockSpec(memory_space=pltpu.VMEM)
    return pl.pallas_call(
        functools.partial(filter_kernel, n, rows),
        out_shape=jax.ShapeDtypeStruct(flat_winds.shape, flat_winds.dtype),
        in_specs=[vmem] * 8,
        out_specs=vmem,
        scratch_shapes=[
            pltpu.VMEM(flat_winds.shape, jnp.float32),
            pltpu.VMEM(flat_winds.shape, jnp.float32),
            pltpu.SemaphoreType.DMA((n,)),
            pltpu.SemaphoreType.DMA((n,)),
            pltpu.SemaphoreType.DMA((n,)),
            pltpu.SemaphoreType.DMA((n,)),
        ],
        compiler_params=pltpu.CompilerParams(collective_id=0, has_side_effects=True),
    )(
        flat_winds,
        kron_cos,
        kron_sin,
        twist_cos,
        twist_sin,
        jnp.cos(table_turn),
        jnp.sin(table_turn),
        factor,
    )


def local(tracers, wind_field):
    levels, lon_cols, merged = tracers.shape
    lat_rows = wind_field.shape[2]
    tracer_count = merged // lat_rows
    lon_total = lon_cols * lax.axis_size("lon")
    lat_total = lat_rows * lax.axis_size("lat")
    first_row = lax.axis_index("lat") * lat_rows
    row_ids = first_row + jnp.arange(lat_rows, dtype=jnp.int32)
    row_cosine = jnp.cos(
        (row_ids.astype(jnp.float32) + 0.5) * (math.pi / lat_total) - 0.5 * math.pi
    )
    flat_winds = wind_field.reshape(2 * levels * lat_rows, lon_cols)
    flat_cosine = jnp.tile(row_cosine, 2 * levels)
    smoothed = spectral(flat_winds, flat_cosine, lon_total)
    smoothed = smoothed.reshape(2, levels, lat_rows, lon_cols)
    east_turned = jnp.transpose(smoothed[0], (0, 2, 1))
    north_turned = jnp.transpose(smoothed[1], (0, 2, 1))
    zonal_stack = jnp.concatenate([tracers, east_turned], axis=2)
    zonal_pad = extended(zonal_stack, (("lon", 1),), 3, True)
    east_wind = zonal_pad[:, :, merged:]
    zonal_speed = 0.5 * (east_wind[:, 2 : lon_cols + 3] + east_wind[:, 3 : lon_cols + 4])
    zonal_speed = jnp.repeat(zonal_speed, tracer_count, axis=2)
    left_x, right_x = face_values(zonal_pad[:, :, :merged], 1, lon_cols, 1)
    zonal_flux = upwind(zonal_speed, left_x, right_x)
    slot_count = tracer_count + 1
    merid_stack = jnp.concatenate(
        [tracers.reshape(levels, lon_cols, lat_rows, tracer_count), north_turned[..., None]], axis=3
    )
    merid_stack = merid_stack.reshape(levels, lon_cols, lat_rows * slot_count)
    merid_pad = extended(merid_stack, (("lat", 2),), 3 * slot_count, False)
    merid_pad = merid_pad.reshape(levels, lon_cols, lat_rows + 6, slot_count)
    north_wind = merid_pad[..., tracer_count]
    tracer_pad = merid_pad[..., :tracer_count].reshape(
        levels, lon_cols, (lat_rows + 6) * tracer_count
    )
    face_ids = first_row + jnp.arange(lat_rows + 1, dtype=jnp.int32)
    face_cosine = jnp.cos(face_ids.astype(jnp.float32) * (math.pi / lat_total) - 0.5 * math.pi)
    face_cosine = jnp.where((face_ids == 0) | (face_ids == lat_total), 0.0, face_cosine)
    merid_speed = (
        0.5
        * (north_wind[:, :, 2 : lat_rows + 3] + north_wind[:, :, 3 : lat_rows + 4])
        * face_cosine[None, None, :]
    )
    merid_speed = jnp.repeat(merid_speed, tracer_count, axis=2)
    left_y, right_y = face_values(tracer_pad, 2, lat_rows, tracer_count)
    merid_flux = upwind(merid_speed, left_y, right_y)
    metric = jnp.repeat(1.0 / jnp.maximum(row_cosine, COS_FLOOR), tracer_count)
    change = COURANT * (zonal_flux[:, 1:] - zonal_flux[:, :-1]) + COURANT * (
        merid_flux[:, :, tracer_count:] - merid_flux[:, :, :-tracer_count]
    )
    advected = tracers - metric[None, None, :] * change
    return (advected, smoothed)


def solution(mesh):
    placed = (P(None, "lon", "lat"), P(None, None, "lat", "lon"))
    return jax.shard_map(
        local,
        mesh=mesh,
        in_specs=placed,
        out_specs=(P(None, "lon", "lat"), P(None, None, "lat", "lon")),
        check_vma=False,
    )
```

```python
import functools
import math

import jax
import numpy as np
import jax.numpy as jnp
from jax import lax
from jax.experimental import pallas as pl
from jax.experimental.pallas import tpu as pltpu
from jax.sharding import PartitionSpec as P

MESH = pl.DeviceIdType.MESH

COURANT = 0.3
COS_FLOOR = 0.5
EXACT_MODE = lax.Precision.HIGHEST


def extended(array, sides, width, wrap):
    for axis, dim in sides:
        devices, length = (lax.axis_size(axis), array.shape[dim])
        up = [(i, (i + 1) % devices) for i in range(devices if wrap else devices - 1)]
        down = [(j, i) for i, j in up]
        last = lax.slice_in_dim(array, length - width, length, axis=dim)
        first = lax.slice_in_dim(array, 0, width, axis=dim)
        before = lax.ppermute(last, axis, up)
        after = lax.ppermute(first, axis, down)
        array = jnp.concatenate([before, array, after], axis=dim)
    return array


def damping(row_cosine, wavenumber, lon_total):
    sine = jnp.sin(wavenumber.astype(jnp.float32) * (math.pi / lon_total))
    divisor = jnp.where(wavenumber == 0, 1.0, sine * sine)
    scaled = (row_cosine / COS_FLOOR) ** 2
    scaled = scaled.reshape(scaled.shape + (1,) * wavenumber.ndim)
    return jnp.where(wavenumber == 0, 1.0, jnp.minimum(1.0, scaled / divisor))


def face_values(padded, axis, cells, stride):

    def offset_cells(offset):
        return lax.slice_in_dim(padded, offset * stride, (offset + cells + 1) * stride, axis=axis)

    left = (
        2.0 * offset_cells(0)
        - 13.0 * offset_cells(1)
        + 47.0 * offset_cells(2)
        + 27.0 * offset_cells(3)
        - 3.0 * offset_cells(4)
    ) / 60.0
    right = (
        2.0 * offset_cells(5)
        - 13.0 * offset_cells(4)
        + 47.0 * offset_cells(3)
        + 27.0 * offset_cells(2)
        - 3.0 * offset_cells(1)
    ) / 60.0
    return (left, right)


def upwind(speed, left, right):
    return jnp.maximum(speed, 0.0) * left + jnp.minimum(speed, 0.0) * right


def filter_kernel(n, rows, winds_ref, scaled_ref, kc_ref, ks_ref, tc_ref, ts_ref, c_ref, s_ref,
                  divisor_ref, zero_ref, out_ref, gathered, restored, send_a, recv_a, send_b, recv_b):
    me = lax.axis_index("lon")
    band = lax.axis_index("lat")
    barrier = pltpu.get_barrier_semaphore()
    for k in range(1, n):
        peer = lax.rem(me + k, n)
        pl.semaphore_signal(barrier, inc=1, device_id=(band, peer), device_id_type=MESH)
    pl.semaphore_wait(barrier, n - 1)

    def block(ref, index):
        return ref.at[pl.ds(pl.multiple_of(index * rows, rows), rows)]

    def swap(source, target, send_sem, recv_sem):
        sends = []
        for k in range(1, n):
            peer = lax.rem(me + k, n)
            copy = pltpu.make_async_remote_copy(
                src_ref=block(source, peer),
                dst_ref=block(target, me),
                send_sem=send_sem.at[peer],
                recv_sem=recv_sem.at[me],
                device_id=(band, peer),
                device_id_type=MESH,
            )
            copy.start()
            sends.append(copy)
        block(target, me)[...] = block(source, me)[...]
        for k in range(1, n):
            origin = lax.rem(me + n - k, n)
            pltpu.make_async_remote_copy(
                src_ref=block(source, origin),
                dst_ref=block(target, origin),
                send_sem=send_sem.at[origin],
                recv_sem=recv_sem.at[origin],
                device_id=(band, origin),
                device_id_type=MESH,
            ).wait_recv()
        for copy in sends:
            copy.wait_send()

    swap(winds_ref, gathered, send_a, recv_a)

    def mm(a, b):
        return jnp.dot(a, b, precision=EXACT_MODE, preferred_element_type=jnp.float32)

    x = gathered[...]
    kc, ks = kc_ref[...], ks_ref[...]
    tc, ts = tc_ref[...], ts_ref[...]
    c, s = c_ref[...], s_ref[...]
    re = mm(kc, x)
    im = -mm(ks, x)
    shifted_re = re * tc + im * ts
    shifted_im = im * tc - re * ts
    modes_re = mm(shifted_re, c) + mm(shifted_im, s)
    modes_im = mm(shifted_im, c) - mm(shifted_re, s)
    factor = jnp.where(
        zero_ref[...] > 0.0, 1.0, jnp.minimum(1.0, scaled_ref[...] / divisor_ref[...])
    )
    modes_re = modes_re * factor
    modes_im = modes_im * factor
    back_re = mm(modes_re, c) - mm(modes_im, s)
    back_im = mm(modes_im, c) + mm(modes_re, s)
    out_re = back_re * tc - back_im * ts
    out_im = back_im * tc + back_re * ts
    restored[...] = (mm(kc, out_re) - mm(ks, out_im)) / (n * x.shape[1])
    swap(restored, out_ref, send_b, recv_b)


def spectral_tables(n, rows, columns):
    lon_total = n * columns
    blocks = np.arange(n)
    phase = 2.0 * np.pi * (np.outer(blocks, blocks) % n) / n
    eye = np.eye(rows)
    column_ids = np.arange(columns)
    twist = 2.0 * np.pi * (np.outer(blocks, column_ids) % lon_total) / lon_total
    turn = 2.0 * np.pi * (np.outer(column_ids, column_ids) % columns) / columns
    wavenumber = blocks[:, None] + n * column_ids[None, :]
    sine = np.sin(wavenumber.astype(np.float32) * np.float32(math.pi / lon_total))
    divisor = np.where(wavenumber == 0, np.float32(1.0), sine * sine).astype(np.float32)
    zero_mode = (wavenumber == 0).astype(np.float32)
    tables = (
        np.kron(np.cos(phase), eye),
        np.kron(np.sin(phase), eye),
        np.repeat(np.cos(twist), rows, axis=0),
        np.repeat(np.sin(twist), rows, axis=0),
        np.cos(turn),
        np.sin(turn),
        np.repeat(divisor, rows, axis=0),
        np.repeat(zero_mode, rows, axis=0),
    )
    return [jnp.asarray(t.astype(np.float32)) for t in tables]


def spectral(flat_winds, row_cosine, lon_total):
    flat_rows, columns = flat_winds.shape
    n = lax.axis_size("lon")
    lon_index = lax.axis_index("lon")
    rows = flat_rows // n
    own_cosine = lax.dynamic_slice_in_dim(row_cosine, lon_index * rows, rows, 0)
    scaled = (own_cosine / COS_FLOOR) ** 2
    scaled = jnp.tile(scaled, n).reshape(n * rows, 1)
    vmem = pl.BlockSpec(memory_space=pltpu.VMEM)
    return pl.pallas_call(
        functools.partial(filter_kernel, n, rows),
        out_shape=jax.ShapeDtypeStruct(flat_winds.shape, flat_winds.dtype),
        in_specs=[vmem] * 10,
        out_specs=vmem,
        scratch_shapes=[
            pltpu.VMEM(flat_winds.shape, jnp.float32),
            pltpu.VMEM(flat_winds.shape, jnp.float32),
            pltpu.SemaphoreType.DMA((n,)),
            pltpu.SemaphoreType.DMA((n,)),
            pltpu.SemaphoreType.DMA((n,)),
            pltpu.SemaphoreType.DMA((n,)),
        ],
        compiler_params=pltpu.CompilerParams(collective_id=0, has_side_effects=True),
    )(flat_winds, scaled, *spectral_tables(n, rows, columns))


def local(tracers, wind_field):
    levels, lon_cols, merged = tracers.shape
    lat_rows = wind_field.shape[2]
    tracer_count = merged // lat_rows
    lon_total = lon_cols * lax.axis_size("lon")
    lat_total = lat_rows * lax.axis_size("lat")
    first_row = lax.axis_index("lat") * lat_rows
    row_ids = first_row + jnp.arange(lat_rows, dtype=jnp.int32)
    row_cosine = jnp.cos(
        (row_ids.astype(jnp.float32) + 0.5) * (math.pi / lat_total) - 0.5 * math.pi
    )
    flat_winds = wind_field.reshape(2 * levels * lat_rows, lon_cols)
    flat_cosine = jnp.tile(row_cosine, 2 * levels)
    smoothed = spectral(flat_winds, flat_cosine, lon_total)
    smoothed = smoothed.reshape(2, levels, lat_rows, lon_cols)
    east_turned = jnp.transpose(smoothed[0], (0, 2, 1))
    north_turned = jnp.transpose(smoothed[1], (0, 2, 1))
    zonal_stack = jnp.concatenate([tracers, east_turned], axis=2)
    zonal_pad = extended(zonal_stack, (("lon", 1),), 3, True)
    east_wind = zonal_pad[:, :, merged:]
    zonal_speed = 0.5 * (east_wind[:, 2 : lon_cols + 3] + east_wind[:, 3 : lon_cols + 4])
    zonal_speed = jnp.repeat(zonal_speed, tracer_count, axis=2)
    left_x, right_x = face_values(zonal_pad[:, :, :merged], 1, lon_cols, 1)
    zonal_flux = upwind(zonal_speed, left_x, right_x)
    slot_count = tracer_count + 1
    merid_stack = jnp.concatenate(
        [tracers.reshape(levels, lon_cols, lat_rows, tracer_count), north_turned[..., None]], axis=3
    )
    merid_stack = merid_stack.reshape(levels, lon_cols, lat_rows * slot_count)
    merid_pad = extended(merid_stack, (("lat", 2),), 3 * slot_count, False)
    merid_pad = merid_pad.reshape(levels, lon_cols, lat_rows + 6, slot_count)
    north_wind = merid_pad[..., tracer_count]
    tracer_pad = merid_pad[..., :tracer_count].reshape(
        levels, lon_cols, (lat_rows + 6) * tracer_count
    )
    face_ids = first_row + jnp.arange(lat_rows + 1, dtype=jnp.int32)
    face_cosine = jnp.cos(face_ids.astype(jnp.float32) * (math.pi / lat_total) - 0.5 * math.pi)
    face_cosine = jnp.where((face_ids == 0) | (face_ids == lat_total), 0.0, face_cosine)
    merid_speed = (
        0.5
        * (north_wind[:, :, 2 : lat_rows + 3] + north_wind[:, :, 3 : lat_rows + 4])
        * face_cosine[None, None, :]
    )
    merid_speed = jnp.repeat(merid_speed, tracer_count, axis=2)
    left_y, right_y = face_values(tracer_pad, 2, lat_rows, tracer_count)
    merid_flux = upwind(merid_speed, left_y, right_y)
    metric = jnp.repeat(1.0 / jnp.maximum(row_cosine, COS_FLOOR), tracer_count)
    change = COURANT * (zonal_flux[:, 1:] - zonal_flux[:, :-1]) + COURANT * (
        merid_flux[:, :, tracer_count:] - merid_flux[:, :, :-tracer_count]
    )
    advected = tracers - metric[None, None, :] * change
    return (advected, smoothed)


def solution(mesh):
    placed = (P(None, "lon", "lat"), P(None, None, "lat", "lon"))
    return jax.shard_map(
        local,
        mesh=mesh,
        in_specs=placed,
        out_specs=(P(None, "lon", "lat"), P(None, None, "lat", "lon")),
        check_vma=False,
    )
```

```python
import functools
import math

import jax
import numpy as np
import jax.numpy as jnp
from jax import lax
from jax.experimental import pallas as pl
from jax.experimental.pallas import tpu as pltpu
from jax.sharding import PartitionSpec as P

MESH = pl.DeviceIdType.MESH

COURANT = 0.3
COS_FLOOR = 0.5
EXACT_MODE = lax.Precision.HIGHEST


def extended(array, sides, width, wrap):
    for axis, dim in sides:
        devices, length = (lax.axis_size(axis), array.shape[dim])
        up = [(i, (i + 1) % devices) for i in range(devices if wrap else devices - 1)]
        down = [(j, i) for i, j in up]
        last = lax.slice_in_dim(array, length - width, length, axis=dim)
        first = lax.slice_in_dim(array, 0, width, axis=dim)
        before = lax.ppermute(last, axis, up)
        after = lax.ppermute(first, axis, down)
        array = jnp.concatenate([before, array, after], axis=dim)
    return array


def damping(row_cosine, wavenumber, lon_total):
    sine = jnp.sin(wavenumber.astype(jnp.float32) * (math.pi / lon_total))
    divisor = jnp.where(wavenumber == 0, 1.0, sine * sine)
    scaled = (row_cosine / COS_FLOOR) ** 2
    scaled = scaled.reshape(scaled.shape + (1,) * wavenumber.ndim)
    return jnp.where(wavenumber == 0, 1.0, jnp.minimum(1.0, scaled / divisor))


def face_values(padded, axis, cells, stride):

    def offset_cells(offset):
        return lax.slice_in_dim(padded, offset * stride, (offset + cells + 1) * stride, axis=axis)

    left = (
        2.0 * offset_cells(0)
        - 13.0 * offset_cells(1)
        + 47.0 * offset_cells(2)
        + 27.0 * offset_cells(3)
        - 3.0 * offset_cells(4)
    ) / 60.0
    right = (
        2.0 * offset_cells(5)
        - 13.0 * offset_cells(4)
        + 47.0 * offset_cells(3)
        + 27.0 * offset_cells(2)
        - 3.0 * offset_cells(1)
    ) / 60.0
    return (left, right)


def upwind(speed, left, right):
    return jnp.maximum(speed, 0.0) * left + jnp.minimum(speed, 0.0) * right


def filter_kernel(n, rows, winds_ref, scaled_ref, kc_ref, ks_ref, tc_ref, ts_ref, c_ref, s_ref,
                  divisor_ref, zero_ref, widen_ref, prev_ref, next_ref, tracers_ref,
                  out_ref, west_ref, east_ref, south_ref, north_ref, vsouth_ref, vnorth_ref,
                  gathered, restored, send_a, recv_a, send_b, recv_b, halo_send, halo_recv, local_sem):
    me = lax.axis_index("lon")
    band = lax.axis_index("lat")
    bands = lax.axis_size("lat")
    up, down = lax.rem(band + 1, bands), lax.rem(band + bands - 1, bands)
    east_peer, west_peer = lax.rem(me + 1, n), lax.rem(me + n - 1, n)
    barrier = pltpu.get_barrier_semaphore()
    for k in range(1, n):
        peer = lax.rem(me + k, n)
        pl.semaphore_signal(barrier, inc=1, device_id=(band, peer), device_id_type=MESH)
    for other in (up, down):
        pl.semaphore_signal(barrier, inc=1, device_id=(other, me), device_id_type=MESH)
    pl.semaphore_wait(barrier, n + 1)

    cols, merged = tracers_ref.shape[1], tracers_ref.shape[2]
    lane_depth = south_ref.shape[2]
    flat_rows = out_ref.shape[0]
    level_rows = flat_rows // 4
    halo_plan = [
        (tracers_ref.at[:, pl.ds(cols - west_ref.shape[1], west_ref.shape[1]), :], west_ref, (band, east_peer)),
        (tracers_ref.at[:, pl.ds(0, east_ref.shape[1]), :], east_ref, (band, west_peer)),
        (tracers_ref.at[:, :, pl.ds(merged - lane_depth, lane_depth)], south_ref, (up, me)),
        (tracers_ref.at[:, :, pl.ds(0, lane_depth)], north_ref, (down, me)),
    ]
    for level in range(2):
        first = 2 * level_rows + level * level_rows
        halo_plan.append(
            (out_ref.at[pl.ds(first + level_rows - 1, 1)], vsouth_ref.at[pl.ds(level, 1)], (up, me))
        )
    for level in range(2):
        first = 2 * level_rows + level * level_rows
        halo_plan.append((out_ref.at[pl.ds(first, 1)], vnorth_ref.at[pl.ds(level, 1)], (down, me)))

    def halo_copy(index):
        source, target, device = halo_plan[index]
        return pltpu.make_async_remote_copy(
            src_ref=source,
            dst_ref=target,
            send_sem=halo_send.at[index],
            recv_sem=halo_recv.at[index],
            device_id=device,
            device_id_type=MESH,
        )

    def block(ref, index):
        return ref.at[pl.ds(pl.multiple_of(index * rows, rows), rows)]

    def swap(source, target, send_sem, recv_sem, slot):
        sends = []
        for k in range(1, n):
            peer = lax.rem(me + k, n)
            copy = pltpu.make_async_remote_copy(
                src_ref=block(source, peer),
                dst_ref=block(target, me),
                send_sem=send_sem.at[peer],
                recv_sem=recv_sem.at[me],
                device_id=(band, peer),
                device_id_type=MESH,
            )
            copy.start()
            sends.append(copy)
        own = pltpu.make_async_copy(block(source, me), block(target, me), local_sem.at[slot])
        own.start()
        return sends, own

    def settle(source, target, send_sem, recv_sem, sends, own):
        own.wait()
        for k in range(1, n):
            origin = lax.rem(me + n - k, n)
            pltpu.make_async_remote_copy(
                src_ref=block(source, origin),
                dst_ref=block(target, origin),
                send_sem=send_sem.at[origin],
                recv_sem=recv_sem.at[origin],
                device_id=(band, origin),
                device_id_type=MESH,
            ).wait_recv()
        for copy in sends:
            copy.wait_send()

    sends, own = swap(winds_ref, gathered, send_a, recv_a, 0)
    tracer_halos = [halo_copy(i) for i in range(4)]
    for copy in tracer_halos:
        copy.start()
    settle(winds_ref, gathered, send_a, recv_a, sends, own)

    def mm(a, b):
        return jnp.dot(a, b, precision=EXACT_MODE, preferred_element_type=jnp.float32)

    x = gathered[...]
    kc, ks = kc_ref[...], ks_ref[...]
    tc, ts = tc_ref[...], ts_ref[...]
    c, s = c_ref[...], s_ref[...]
    re = mm(kc, x)
    im = -mm(ks, x)
    shifted_re = re * tc + im * ts
    shifted_im = im * tc - re * ts
    modes_re = mm(shifted_re, c) + mm(shifted_im, s)
    modes_im = mm(shifted_im, c) - mm(shifted_re, s)
    factor = jnp.where(
        zero_ref[...] > 0.0, 1.0, jnp.minimum(1.0, scaled_ref[...] / divisor_ref[...])
    )
    modes_re = modes_re * factor
    modes_im = modes_im * factor
    back_re = mm(modes_re, c) - mm(modes_im, s)
    back_im = mm(modes_im, c) + mm(modes_re, s)
    out_re = back_re * tc - back_im * ts
    out_im = back_im * tc + back_re * ts
    result = (mm(kc, out_re) - mm(ks, out_im)) / (n * x.shape[1])
    restored[...] = (
        mm(result, widen_ref[...])
        + mm(jnp.roll(result, rows, axis=0), prev_ref[...])
        + mm(jnp.roll(result, -rows, axis=0), next_ref[...])
    )
    sends, own = swap(restored, out_ref, send_b, recv_b, 1)
    settle(restored, out_ref, send_b, recv_b, sends, own)
    wind_halos = [halo_copy(i) for i in range(4, 8)]
    for copy in wind_halos:
        copy.start()
    for copy in tracer_halos + wind_halos:
        copy.wait_recv()
    for copy in tracer_halos + wind_halos:
        copy.wait_send()


def spectral_tables(n, rows, columns):
    lon_total = n * columns
    blocks = np.arange(n)
    phase = 2.0 * np.pi * (np.outer(blocks, blocks) % n) / n
    eye = np.eye(rows)
    column_ids = np.arange(columns)
    twist = 2.0 * np.pi * (np.outer(blocks, column_ids) % lon_total) / lon_total
    turn = 2.0 * np.pi * (np.outer(column_ids, column_ids) % columns) / columns
    wavenumber = blocks[:, None] + n * column_ids[None, :]
    sine = np.sin(wavenumber.astype(np.float32) * np.float32(math.pi / lon_total))
    divisor = np.where(wavenumber == 0, np.float32(1.0), sine * sine).astype(np.float32)
    zero_mode = (wavenumber == 0).astype(np.float32)
    widen = np.eye(columns, columns + 2)
    take_last = np.zeros((columns, columns + 2))
    take_last[columns - 1, columns] = 1.0
    take_first = np.zeros((columns, columns + 2))
    take_first[0, columns + 1] = 1.0
    tables = (
        np.kron(np.cos(phase), eye),
        np.kron(np.sin(phase), eye),
        np.repeat(np.cos(twist), rows, axis=0),
        np.repeat(np.sin(twist), rows, axis=0),
        np.cos(turn),
        np.sin(turn),
        np.repeat(divisor, rows, axis=0),
        np.repeat(zero_mode, rows, axis=0),
        widen,
        take_last,
        take_first,
    )
    return [jnp.asarray(t.astype(np.float32)) for t in tables]


def exchange_all(flat_winds, row_cosine, tracers):
    flat_rows, columns = flat_winds.shape
    levels, lon_cols, merged = tracers.shape
    n = lax.axis_size("lon")
    lon_index = lax.axis_index("lon")
    rows = flat_rows // n
    tracer_count = merged // row_cosine.shape[0]
    own_cosine = lax.dynamic_slice_in_dim(jnp.tile(row_cosine, flat_rows // row_cosine.shape[0]), lon_index * rows, rows, 0)
    scaled = (own_cosine / COS_FLOOR) ** 2
    scaled = jnp.tile(scaled, n).reshape(n * rows, 1)
    vmem = pl.BlockSpec(memory_space=pltpu.VMEM)
    west_cols = lon_cols - (lon_cols - 3) // 8 * 8
    lanes = -(-3 * tracer_count // 128) * 128
    shapes = [
        (flat_rows, columns + 2),
        (levels, west_cols, merged),
        (levels, 8, merged),
        (levels, lon_cols, lanes),
        (levels, lon_cols, lanes),
        (levels, columns + 2),
        (levels, columns + 2),
    ]
    return pl.pallas_call(
        functools.partial(filter_kernel, n, rows),
        out_shape=[jax.ShapeDtypeStruct(shape, jnp.float32) for shape in shapes],
        in_specs=[vmem] * 13 + [pl.BlockSpec(memory_space=pl.ANY)],
        out_specs=[vmem] * len(shapes),
        scratch_shapes=[
            pltpu.VMEM((flat_rows, columns), jnp.float32),
            pltpu.VMEM((flat_rows, columns + 2), jnp.float32),
            pltpu.SemaphoreType.DMA((n,)),
            pltpu.SemaphoreType.DMA((n,)),
            pltpu.SemaphoreType.DMA((n,)),
            pltpu.SemaphoreType.DMA((n,)),
            pltpu.SemaphoreType.DMA((8,)),
            pltpu.SemaphoreType.DMA((8,)),
            pltpu.SemaphoreType.DMA((2,)),
        ],
        compiler_params=pltpu.CompilerParams(collective_id=0, has_side_effects=True),
    )(flat_winds, scaled, *spectral_tables(n, rows, columns), tracers)


def stencil(padded, dim, faces, stride):

    def offset_cells(offset):
        return lax.slice_in_dim(padded, offset * stride, (offset + faces) * stride, axis=dim)

    left = (
        2.0 * offset_cells(0)
        - 13.0 * offset_cells(1)
        + 47.0 * offset_cells(2)
        + 27.0 * offset_cells(3)
        - 3.0 * offset_cells(4)
    ) / 60.0
    right = (
        2.0 * offset_cells(5)
        - 13.0 * offset_cells(4)
        + 47.0 * offset_cells(3)
        + 27.0 * offset_cells(2)
        - 3.0 * offset_cells(1)
    ) / 60.0
    return left, right


def spread(values, rows, tracer_count):
    lanes = jnp.arange(rows * tracer_count, dtype=jnp.int32) // tracer_count
    pick = (jnp.arange(rows, dtype=jnp.int32)[:, None] == lanes[None, :]).astype(jnp.float32)
    return jnp.einsum("ljc,jm->lcm", values, pick, precision=EXACT_MODE)


def local(tracers, wind_field):
    levels, lon_cols, merged = tracers.shape
    lat_rows = wind_field.shape[2]
    tracer_count = merged // lat_rows
    lat_total = lat_rows * lax.axis_size("lat")
    band = lax.axis_index("lat")
    first_row = band * lat_rows
    row_ids = first_row + jnp.arange(lat_rows, dtype=jnp.int32)
    row_cosine = jnp.cos(
        (row_ids.astype(jnp.float32) + 0.5) * (math.pi / lat_total) - 0.5 * math.pi
    )
    flat_winds = wind_field.reshape(2 * levels * lat_rows, lon_cols)
    wide, west, east, south, north, v_south, v_north = exchange_all(flat_winds, row_cosine, tracers)
    has_south = band > 0
    has_north = band < lax.axis_size("lat") - 1
    west = west[:, west.shape[1] - 3 :]
    east = east[:, :3]
    south = jnp.where(has_south, south[..., south.shape[2] - 3 * tracer_count :], 0.0)
    north = jnp.where(has_north, north[..., : 3 * tracer_count], 0.0)
    v_south = jnp.where(has_south, v_south[:, :lon_cols], 0.0)
    v_north = jnp.where(has_north, v_north[:, :lon_cols], 0.0)
    wide = wide.reshape(2, levels, lat_rows, lon_cols + 2)
    smoothed = wide[..., :lon_cols]
    east_wide = wide[0]
    north_wind = smoothed[1]
    u_pad = jnp.concatenate(
        [east_wide[..., lon_cols : lon_cols + 1], east_wide[..., :lon_cols], east_wide[..., lon_cols + 1 :]],
        axis=2,
    )
    zonal_speed = 0.5 * (u_pad[:, :, : lon_cols + 1] + u_pad[:, :, 1:])
    v_pad = jnp.concatenate([v_south[:, None], north_wind, v_north[:, None]], axis=1)
    face_ids = first_row + jnp.arange(lat_rows + 1, dtype=jnp.int32)
    face_cosine = jnp.cos(face_ids.astype(jnp.float32) * (math.pi / lat_total) - 0.5 * math.pi)
    face_cosine = jnp.where((face_ids == 0) | (face_ids == lat_total), 0.0, face_cosine)
    merid_speed = 0.5 * (v_pad[:, : lat_rows + 1] + v_pad[:, 1:]) * face_cosine[None, :, None]
    zonal_rep = spread(zonal_speed, lat_rows, tracer_count)
    merid_rep = spread(merid_speed, lat_rows + 1, tracer_count)
    zonal_pad = jnp.concatenate([west, tracers, east], axis=1)
    left_x, right_x = stencil(zonal_pad, 1, lon_cols + 1, 1)
    zonal_flux = upwind(zonal_rep, left_x, right_x)
    merid_pad = jnp.concatenate([south, tracers, north], axis=2)
    left_y, right_y = stencil(merid_pad, 2, lat_rows + 1, tracer_count)
    merid_flux = upwind(merid_rep, left_y, right_y)
    metric = jnp.repeat(1.0 / jnp.maximum(row_cosine, COS_FLOOR), tracer_count)
    change = COURANT * (zonal_flux[:, 1:] - zonal_flux[:, :-1]) + COURANT * (
        merid_flux[:, :, tracer_count:] - merid_flux[:, :, :-tracer_count]
    )
    advected = tracers - metric[None, None, :] * change
    return (advected, smoothed)


def solution(mesh):
    placed = (P(None, "lon", "lat"), P(None, None, "lat", "lon"))
    return jax.shard_map(
        local,
        mesh=mesh,
        in_specs=placed,
        out_specs=(P(None, "lon", "lat"), P(None, None, "lat", "lon")),
        check_vma=False,
    )
```

```python
import functools
import math

import jax
import numpy as np
import jax.numpy as jnp
from jax import lax
from jax.experimental import pallas as pl
from jax.experimental.pallas import tpu as pltpu
from jax.sharding import PartitionSpec as P

MESH = pl.DeviceIdType.MESH

COURANT = 0.3
COS_FLOOR = 0.5
EXACT_MODE = lax.Precision.HIGHEST


def extended(array, sides, width, wrap):
    for axis, dim in sides:
        devices, length = (lax.axis_size(axis), array.shape[dim])
        up = [(i, (i + 1) % devices) for i in range(devices if wrap else devices - 1)]
        down = [(j, i) for i, j in up]
        last = lax.slice_in_dim(array, length - width, length, axis=dim)
        first = lax.slice_in_dim(array, 0, width, axis=dim)
        before = lax.ppermute(last, axis, up)
        after = lax.ppermute(first, axis, down)
        array = jnp.concatenate([before, array, after], axis=dim)
    return array


def damping(row_cosine, wavenumber, lon_total):
    sine = jnp.sin(wavenumber.astype(jnp.float32) * (math.pi / lon_total))
    divisor = jnp.where(wavenumber == 0, 1.0, sine * sine)
    scaled = (row_cosine / COS_FLOOR) ** 2
    scaled = scaled.reshape(scaled.shape + (1,) * wavenumber.ndim)
    return jnp.where(wavenumber == 0, 1.0, jnp.minimum(1.0, scaled / divisor))


def face_values(padded, axis, cells, stride):

    def offset_cells(offset):
        return lax.slice_in_dim(padded, offset * stride, (offset + cells + 1) * stride, axis=axis)

    left = (
        2.0 * offset_cells(0)
        - 13.0 * offset_cells(1)
        + 47.0 * offset_cells(2)
        + 27.0 * offset_cells(3)
        - 3.0 * offset_cells(4)
    ) / 60.0
    right = (
        2.0 * offset_cells(5)
        - 13.0 * offset_cells(4)
        + 47.0 * offset_cells(3)
        + 27.0 * offset_cells(2)
        - 3.0 * offset_cells(1)
    ) / 60.0
    return (left, right)


def upwind(speed, left, right):
    return jnp.maximum(speed, 0.0) * left + jnp.minimum(speed, 0.0) * right


def filter_kernel(n, rows, winds_ref, scaled_ref, kc_ref, ks_ref, tc_ref, ts_ref, c_ref, s_ref,
                  divisor_ref, zero_ref, widen_ref, prev_ref, next_ref, tracers_ref,
                  out_ref, smooth_ref, west_ref, east_ref, south_ref, north_ref, vsouth_ref, vnorth_ref,
                  gathered, restored, send_a, recv_a, send_b, recv_b, halo_send, halo_recv, local_sem):
    me = lax.axis_index("lon")
    band = lax.axis_index("lat")
    bands = lax.axis_size("lat")
    up, down = lax.rem(band + 1, bands), lax.rem(band + bands - 1, bands)
    east_peer, west_peer = lax.rem(me + 1, n), lax.rem(me + n - 1, n)
    barrier = pltpu.get_barrier_semaphore()
    for k in range(1, n):
        peer = lax.rem(me + k, n)
        pl.semaphore_signal(barrier, inc=1, device_id=(band, peer), device_id_type=MESH)
    for other in (up, down):
        pl.semaphore_signal(barrier, inc=1, device_id=(other, me), device_id_type=MESH)
    pl.semaphore_wait(barrier, n + 1)

    cols, merged = tracers_ref.shape[0], tracers_ref.shape[2]
    depth, lane_depth = west_ref.shape[0], south_ref.shape[2]
    flat_rows = out_ref.shape[0]
    level_rows = flat_rows // 4
    halo_plan = [
        (tracers_ref.at[pl.ds(cols - depth, depth)], west_ref, (band, east_peer)),
        (tracers_ref.at[pl.ds(0, depth)], east_ref, (band, west_peer)),
        (tracers_ref.at[:, :, pl.ds(merged - lane_depth, lane_depth)], south_ref, (up, me)),
        (tracers_ref.at[:, :, pl.ds(0, lane_depth)], north_ref, (down, me)),
    ]
    for level in range(2):
        first = 2 * level_rows + level * level_rows
        halo_plan.append(
            (out_ref.at[pl.ds(first + level_rows - 1, 1)], vsouth_ref.at[pl.ds(level, 1)], (up, me))
        )
    for level in range(2):
        first = 2 * level_rows + level * level_rows
        halo_plan.append((out_ref.at[pl.ds(first, 1)], vnorth_ref.at[pl.ds(level, 1)], (down, me)))

    def halo_copy(index):
        source, target, device = halo_plan[index]
        return pltpu.make_async_remote_copy(
            src_ref=source,
            dst_ref=target,
            send_sem=halo_send.at[index],
            recv_sem=halo_recv.at[index],
            device_id=device,
            device_id_type=MESH,
        )

    def block(ref, index):
        return ref.at[pl.ds(pl.multiple_of(index * rows, rows), rows)]

    def swap(source, target, send_sem, recv_sem, slot):
        sends = []
        for k in range(1, n):
            peer = lax.rem(me + k, n)
            copy = pltpu.make_async_remote_copy(
                src_ref=block(source, peer),
                dst_ref=block(target, me),
                send_sem=send_sem.at[peer],
                recv_sem=recv_sem.at[me],
                device_id=(band, peer),
                device_id_type=MESH,
            )
            copy.start()
            sends.append(copy)
        own = pltpu.make_async_copy(block(source, me), block(target, me), local_sem.at[slot])
        own.start()
        return sends, own

    def settle(source, target, send_sem, recv_sem, sends, own):
        own.wait()
        for k in range(1, n):
            origin = lax.rem(me + n - k, n)
            pltpu.make_async_remote_copy(
                src_ref=block(source, origin),
                dst_ref=block(target, origin),
                send_sem=send_sem.at[origin],
                recv_sem=recv_sem.at[origin],
                device_id=(band, origin),
                device_id_type=MESH,
            ).wait_recv()
        for copy in sends:
            copy.wait_send()

    sends, own = swap(winds_ref, gathered, send_a, recv_a, 0)
    tracer_halos = [halo_copy(i) for i in range(4)]
    for copy in tracer_halos:
        copy.start()
    settle(winds_ref, gathered, send_a, recv_a, sends, own)

    def mm(a, b):
        return jnp.dot(a, b, precision=EXACT_MODE, preferred_element_type=jnp.float32)

    x = gathered[...]
    kc, ks = kc_ref[...], ks_ref[...]
    tc, ts = tc_ref[...], ts_ref[...]
    c, s = c_ref[...], s_ref[...]
    re = mm(kc, x)
    im = -mm(ks, x)
    shifted_re = re * tc + im * ts
    shifted_im = im * tc - re * ts
    modes_re = mm(shifted_re, c) + mm(shifted_im, s)
    modes_im = mm(shifted_im, c) - mm(shifted_re, s)
    factor = jnp.where(
        zero_ref[...] > 0.0, 1.0, jnp.minimum(1.0, scaled_ref[...] / divisor_ref[...])
    )
    modes_re = modes_re * factor
    modes_im = modes_im * factor
    back_re = mm(modes_re, c) - mm(modes_im, s)
    back_im = mm(modes_im, c) + mm(modes_re, s)
    out_re = back_re * tc - back_im * ts
    out_im = back_im * tc + back_re * ts
    result = (mm(kc, out_re) - mm(ks, out_im)) / (n * x.shape[1])
    restored[...] = (
        mm(result, widen_ref[...])
        + mm(jnp.roll(result, rows, axis=0), prev_ref[...])
        + mm(jnp.roll(result, -rows, axis=0), next_ref[...])
    )
    sends, own = swap(restored, out_ref, send_b, recv_b, 1)
    settle(restored, out_ref, send_b, recv_b, sends, own)
    wind_halos = [halo_copy(i) for i in range(4, 8)]
    for copy in wind_halos:
        copy.start()
    smooth_ref[...] = out_ref[:, : smooth_ref.shape[1]]
    for copy in tracer_halos + wind_halos:
        copy.wait_recv()
    for copy in tracer_halos + wind_halos:
        copy.wait_send()

    @pl.when(band == 0)
    def _():
        south_ref[...] = jnp.zeros(south_ref.shape, jnp.float32)
        vsouth_ref[...] = jnp.zeros(vsouth_ref.shape, jnp.float32)

    @pl.when(band == bands - 1)
    def _():
        north_ref[...] = jnp.zeros(north_ref.shape, jnp.float32)
        vnorth_ref[...] = jnp.zeros(vnorth_ref.shape, jnp.float32)


def spectral_tables(n, rows, columns):
    lon_total = n * columns
    blocks = np.arange(n)
    phase = 2.0 * np.pi * (np.outer(blocks, blocks) % n) / n
    eye = np.eye(rows)
    column_ids = np.arange(columns)
    twist = 2.0 * np.pi * (np.outer(blocks, column_ids) % lon_total) / lon_total
    turn = 2.0 * np.pi * (np.outer(column_ids, column_ids) % columns) / columns
    wavenumber = blocks[:, None] + n * column_ids[None, :]
    sine = np.sin(wavenumber.astype(np.float32) * np.float32(math.pi / lon_total))
    divisor = np.where(wavenumber == 0, np.float32(1.0), sine * sine).astype(np.float32)
    zero_mode = (wavenumber == 0).astype(np.float32)
    widen = np.eye(columns, columns + 2)
    take_last = np.zeros((columns, columns + 2))
    take_last[columns - 1, columns] = 1.0
    take_first = np.zeros((columns, columns + 2))
    take_first[0, columns + 1] = 1.0
    tables = (
        np.kron(np.cos(phase), eye),
        np.kron(np.sin(phase), eye),
        np.repeat(np.cos(twist), rows, axis=0),
        np.repeat(np.sin(twist), rows, axis=0),
        np.cos(turn),
        np.sin(turn),
        np.repeat(divisor, rows, axis=0),
        np.repeat(zero_mode, rows, axis=0),
        widen,
        take_last,
        take_first,
    )
    return [jnp.asarray(t.astype(np.float32)) for t in tables]


def exchange_all(flat_winds, row_cosine, tracers):
    flat_rows, columns = flat_winds.shape
    lon_cols, levels, merged = tracers.shape
    n = lax.axis_size("lon")
    lon_index = lax.axis_index("lon")
    rows = flat_rows // n
    tracer_count = merged // row_cosine.shape[0]
    own_cosine = lax.dynamic_slice_in_dim(jnp.tile(row_cosine, flat_rows // row_cosine.shape[0]), lon_index * rows, rows, 0)
    scaled = (own_cosine / COS_FLOOR) ** 2
    scaled = jnp.tile(scaled, n).reshape(n * rows, 1)
    vmem = pl.BlockSpec(memory_space=pltpu.VMEM)
    lanes = -(-3 * tracer_count // 128) * 128
    shapes = [
        (flat_rows, columns + 2),
        (flat_rows, columns),
        (3, levels, merged),
        (3, levels, merged),
        (lon_cols, levels, lanes),
        (lon_cols, levels, lanes),
        (levels, columns + 2),
        (levels, columns + 2),
    ]
    return pl.pallas_call(
        functools.partial(filter_kernel, n, rows),
        out_shape=[jax.ShapeDtypeStruct(shape, jnp.float32) for shape in shapes],
        in_specs=[vmem] * 13 + [pl.BlockSpec(memory_space=pl.ANY)],
        out_specs=[vmem] * len(shapes),
        scratch_shapes=[
            pltpu.VMEM((flat_rows, columns), jnp.float32),
            pltpu.VMEM((flat_rows, columns + 2), jnp.float32),
            pltpu.SemaphoreType.DMA((n,)),
            pltpu.SemaphoreType.DMA((n,)),
            pltpu.SemaphoreType.DMA((n,)),
            pltpu.SemaphoreType.DMA((n,)),
            pltpu.SemaphoreType.DMA((8,)),
            pltpu.SemaphoreType.DMA((8,)),
            pltpu.SemaphoreType.DMA((2,)),
        ],
        compiler_params=pltpu.CompilerParams(collective_id=0, has_side_effects=True),
    )(flat_winds, scaled, *spectral_tables(n, rows, columns), tracers)


def stencil(padded, dim, faces, stride):

    def offset_cells(offset):
        return lax.slice_in_dim(padded, offset * stride, (offset + faces) * stride, axis=dim)

    left = (
        2.0 * offset_cells(0)
        - 13.0 * offset_cells(1)
        + 47.0 * offset_cells(2)
        + 27.0 * offset_cells(3)
        - 3.0 * offset_cells(4)
    ) / 60.0
    right = (
        2.0 * offset_cells(5)
        - 13.0 * offset_cells(4)
        + 47.0 * offset_cells(3)
        + 27.0 * offset_cells(2)
        - 3.0 * offset_cells(1)
    ) / 60.0
    return left, right


def spread(values, rows, tracer_count):
    lanes = jnp.arange(rows * tracer_count, dtype=jnp.int32) // tracer_count
    pick = (jnp.arange(rows, dtype=jnp.int32)[:, None] == lanes[None, :]).astype(jnp.float32)
    return jnp.einsum("ljc,jm->clm", values, pick, precision=EXACT_MODE)


def local(tracers, wind_field):
    levels, lon_cols, merged = tracers.shape
    lat_rows = wind_field.shape[2]
    tracer_count = merged // lat_rows
    lat_total = lat_rows * lax.axis_size("lat")
    band = lax.axis_index("lat")
    first_row = band * lat_rows
    row_ids = first_row + jnp.arange(lat_rows, dtype=jnp.int32)
    row_cosine = jnp.cos(
        (row_ids.astype(jnp.float32) + 0.5) * (math.pi / lat_total) - 0.5 * math.pi
    )
    columns_first = jnp.transpose(tracers, (1, 0, 2))
    flat_winds = wind_field.reshape(2 * levels * lat_rows, lon_cols)
    wide, smoothed, west, east, south, north, v_south, v_north = exchange_all(
        flat_winds, row_cosine, columns_first
    )
    south = south[..., south.shape[2] - 3 * tracer_count :]
    north = north[..., : 3 * tracer_count]
    smoothed = smoothed.reshape(2, levels, lat_rows, lon_cols)
    east_wide = wide.reshape(2, levels, lat_rows, lon_cols + 2)[0]
    north_wind = smoothed[1]
    u_pad = jnp.concatenate(
        [east_wide[..., lon_cols : lon_cols + 1], smoothed[0], east_wide[..., lon_cols + 1 :]],
        axis=2,
    )
    zonal_speed = 0.5 * (u_pad[:, :, : lon_cols + 1] + u_pad[:, :, 1:])
    v_pad = jnp.concatenate(
        [v_south[:, None, :lon_cols], north_wind, v_north[:, None, :lon_cols]], axis=1
    )
    face_ids = first_row + jnp.arange(lat_rows + 1, dtype=jnp.int32)
    face_cosine = jnp.cos(face_ids.astype(jnp.float32) * (math.pi / lat_total) - 0.5 * math.pi)
    face_cosine = jnp.where((face_ids == 0) | (face_ids == lat_total), 0.0, face_cosine)
    merid_speed = 0.5 * (v_pad[:, : lat_rows + 1] + v_pad[:, 1:]) * face_cosine[None, :, None]
    zonal_rep = spread(zonal_speed, lat_rows, tracer_count)
    merid_rep = spread(merid_speed, lat_rows + 1, tracer_count)
    zonal_pad = jnp.concatenate([west, columns_first, east], axis=0)
    left_x, right_x = stencil(zonal_pad, 0, lon_cols + 1, 1)
    zonal_flux = upwind(zonal_rep, left_x, right_x)
    merid_pad = jnp.concatenate([south, columns_first, north], axis=2)
    left_y, right_y = stencil(merid_pad, 2, lat_rows + 1, tracer_count)
    merid_flux = upwind(merid_rep, left_y, right_y)
    metric = jnp.repeat(1.0 / jnp.maximum(row_cosine, COS_FLOOR), tracer_count)
    change = COURANT * (zonal_flux[1:] - zonal_flux[:-1]) + COURANT * (
        merid_flux[:, :, tracer_count:] - merid_flux[:, :, :-tracer_count]
    )
    advected = columns_first - metric[None, None, :] * change
    return (jnp.transpose(advected, (1, 0, 2)), smoothed)


def solution(mesh):
    placed = (P(None, "lon", "lat"), P(None, None, "lat", "lon"))
    return jax.shard_map(
        local,
        mesh=mesh,
        in_specs=placed,
        out_specs=(P(None, "lon", "lat"), P(None, None, "lat", "lon")),
        check_vma=False,
    )
```

```python
import functools
import math

import jax
import numpy as np
import jax.numpy as jnp
from jax import lax
from jax.experimental import pallas as pl
from jax.experimental.pallas import tpu as pltpu
from jax.sharding import PartitionSpec as P

MESH = pl.DeviceIdType.MESH

COURANT = 0.3
COS_FLOOR = 0.5
EXACT_MODE = lax.Precision.HIGHEST


def extended(array, sides, width, wrap):
    for axis, dim in sides:
        devices, length = (lax.axis_size(axis), array.shape[dim])
        up = [(i, (i + 1) % devices) for i in range(devices if wrap else devices - 1)]
        down = [(j, i) for i, j in up]
        last = lax.slice_in_dim(array, length - width, length, axis=dim)
        first = lax.slice_in_dim(array, 0, width, axis=dim)
        before = lax.ppermute(last, axis, up)
        after = lax.ppermute(first, axis, down)
        array = jnp.concatenate([before, array, after], axis=dim)
    return array


def damping(row_cosine, wavenumber, lon_total):
    sine = jnp.sin(wavenumber.astype(jnp.float32) * (math.pi / lon_total))
    divisor = jnp.where(wavenumber == 0, 1.0, sine * sine)
    scaled = (row_cosine / COS_FLOOR) ** 2
    scaled = scaled.reshape(scaled.shape + (1,) * wavenumber.ndim)
    return jnp.where(wavenumber == 0, 1.0, jnp.minimum(1.0, scaled / divisor))


def face_values(padded, axis, cells, stride):

    def offset_cells(offset):
        return lax.slice_in_dim(padded, offset * stride, (offset + cells + 1) * stride, axis=axis)

    left = (
        2.0 * offset_cells(0)
        - 13.0 * offset_cells(1)
        + 47.0 * offset_cells(2)
        + 27.0 * offset_cells(3)
        - 3.0 * offset_cells(4)
    ) / 60.0
    right = (
        2.0 * offset_cells(5)
        - 13.0 * offset_cells(4)
        + 47.0 * offset_cells(3)
        + 27.0 * offset_cells(2)
        - 3.0 * offset_cells(1)
    ) / 60.0
    return (left, right)


def upwind(speed, left, right):
    return jnp.maximum(speed, 0.0) * left + jnp.minimum(speed, 0.0) * right


def filter_kernel(n, rows, winds_ref, scaled_ref, kc_ref, ks_ref, tc_ref, ts_ref, c_ref, s_ref,
                  divisor_ref, zero_ref, widen_ref, prev_ref, next_ref, tracers_ref,
                  out_ref, smooth_ref, west_ref, east_ref, south_ref, north_ref, vsouth_ref, vnorth_ref,
                  gathered, restored, send_a, recv_a, send_b, recv_b, halo_send, halo_recv, local_sem):
    me = lax.axis_index("lon")
    band = lax.axis_index("lat")
    bands = lax.axis_size("lat")
    up, down = lax.rem(band + 1, bands), lax.rem(band + bands - 1, bands)
    east_peer, west_peer = lax.rem(me + 1, n), lax.rem(me + n - 1, n)
    barrier = pltpu.get_barrier_semaphore()
    for k in range(1, n):
        peer = lax.rem(me + k, n)
        pl.semaphore_signal(barrier, inc=1, device_id=(band, peer), device_id_type=MESH)
    for other in (up, down):
        pl.semaphore_signal(barrier, inc=1, device_id=(other, me), device_id_type=MESH)
    pl.semaphore_wait(barrier, n + 1)

    cols, merged = tracers_ref.shape[1], tracers_ref.shape[2]
    lane_depth = south_ref.shape[2]
    flat_rows = out_ref.shape[0]
    level_rows = flat_rows // 4
    halo_plan = [
        (tracers_ref.at[:, pl.ds(cols - west_ref.shape[1], west_ref.shape[1]), :], west_ref, (band, east_peer)),
        (tracers_ref.at[:, pl.ds(0, east_ref.shape[1]), :], east_ref, (band, west_peer)),
        (tracers_ref.at[:, :, pl.ds(merged - lane_depth, lane_depth)], south_ref, (up, me)),
        (tracers_ref.at[:, :, pl.ds(0, lane_depth)], north_ref, (down, me)),
    ]
    for level in range(2):
        first = 2 * level_rows + level * level_rows
        halo_plan.append(
            (out_ref.at[pl.ds(first + level_rows - 1, 1)], vsouth_ref.at[pl.ds(level, 1)], (up, me))
        )
    for level in range(2):
        first = 2 * level_rows + level * level_rows
        halo_plan.append((out_ref.at[pl.ds(first, 1)], vnorth_ref.at[pl.ds(level, 1)], (down, me)))

    def halo_copy(index):
        source, target, device = halo_plan[index]
        return pltpu.make_async_remote_copy(
            src_ref=source,
            dst_ref=target,
            send_sem=halo_send.at[index],
            recv_sem=halo_recv.at[index],
            device_id=device,
            device_id_type=MESH,
        )

    def block(ref, index):
        return ref.at[pl.ds(pl.multiple_of(index * rows, rows), rows)]

    def swap(source, target, send_sem, recv_sem, slot):
        sends = []
        for k in range(1, n):
            peer = lax.rem(me + k, n)
            copy = pltpu.make_async_remote_copy(
                src_ref=block(source, peer),
                dst_ref=block(target, me),
                send_sem=send_sem.at[peer],
                recv_sem=recv_sem.at[me],
                device_id=(band, peer),
                device_id_type=MESH,
            )
            copy.start()
            sends.append(copy)
        own = pltpu.make_async_copy(block(source, me), block(target, me), local_sem.at[slot])
        own.start()
        return sends, own

    def settle(source, target, send_sem, recv_sem, sends, own):
        own.wait()
        for k in range(1, n):
            origin = lax.rem(me + n - k, n)
            pltpu.make_async_remote_copy(
                src_ref=block(source, origin),
                dst_ref=block(target, origin),
                send_sem=send_sem.at[origin],
                recv_sem=recv_sem.at[origin],
                device_id=(band, origin),
                device_id_type=MESH,
            ).wait_recv()
        for copy in sends:
            copy.wait_send()

    sends, own = swap(winds_ref, gathered, send_a, recv_a, 0)
    tracer_halos = [halo_copy(i) for i in range(4)]
    for copy in tracer_halos:
        copy.start()
    settle(winds_ref, gathered, send_a, recv_a, sends, own)

    def mm(a, b):
        return jnp.dot(a, b, precision=EXACT_MODE, preferred_element_type=jnp.float32)

    x = gathered[...]
    kc, ks = kc_ref[...], ks_ref[...]
    tc, ts = tc_ref[...], ts_ref[...]
    c, s = c_ref[...], s_ref[...]
    re = mm(kc, x)
    im = -mm(ks, x)
    shifted_re = re * tc + im * ts
    shifted_im = im * tc - re * ts
    modes_re = mm(shifted_re, c) + mm(shifted_im, s)
    modes_im = mm(shifted_im, c) - mm(shifted_re, s)
    factor = jnp.where(
        zero_ref[...] > 0.0, 1.0, jnp.minimum(1.0, scaled_ref[...] / divisor_ref[...])
    )
    modes_re = modes_re * factor
    modes_im = modes_im * factor
    back_re = mm(modes_re, c) - mm(modes_im, s)
    back_im = mm(modes_im, c) + mm(modes_re, s)
    out_re = back_re * tc - back_im * ts
    out_im = back_im * tc + back_re * ts
    result = (mm(kc, out_re) - mm(ks, out_im)) / (n * x.shape[1])
    restored[...] = (
        mm(result, widen_ref[...])
        + mm(jnp.roll(result, rows, axis=0), prev_ref[...])
        + mm(jnp.roll(result, -rows, axis=0), next_ref[...])
    )
    sends, own = swap(restored, out_ref, send_b, recv_b, 1)
    settle(restored, out_ref, send_b, recv_b, sends, own)
    wind_halos = [halo_copy(i) for i in range(4, 8)]
    for copy in wind_halos:
        copy.start()
    smooth_ref[...] = out_ref[:, : smooth_ref.shape[1]]
    for copy in tracer_halos + wind_halos:
        copy.wait_recv()
    for copy in tracer_halos + wind_halos:
        copy.wait_send()

    @pl.when(band == 0)
    def _():
        south_ref[...] = jnp.zeros(south_ref.shape, jnp.float32)
        vsouth_ref[...] = jnp.zeros(vsouth_ref.shape, jnp.float32)

    @pl.when(band == bands - 1)
    def _():
        north_ref[...] = jnp.zeros(north_ref.shape, jnp.float32)
        vnorth_ref[...] = jnp.zeros(vnorth_ref.shape, jnp.float32)


def spectral_tables(n, rows, columns):
    lon_total = n * columns
    blocks = np.arange(n)
    phase = 2.0 * np.pi * (np.outer(blocks, blocks) % n) / n
    eye = np.eye(rows)
    column_ids = np.arange(columns)
    twist = 2.0 * np.pi * (np.outer(blocks, column_ids) % lon_total) / lon_total
    turn = 2.0 * np.pi * (np.outer(column_ids, column_ids) % columns) / columns
    wavenumber = blocks[:, None] + n * column_ids[None, :]
    sine = np.sin(wavenumber.astype(np.float32) * np.float32(math.pi / lon_total))
    divisor = np.where(wavenumber == 0, np.float32(1.0), sine * sine).astype(np.float32)
    zero_mode = (wavenumber == 0).astype(np.float32)
    widen = np.eye(columns, columns + 2)
    take_last = np.zeros((columns, columns + 2))
    take_last[columns - 1, columns] = 1.0
    take_first = np.zeros((columns, columns + 2))
    take_first[0, columns + 1] = 1.0
    tables = (
        np.kron(np.cos(phase), eye),
        np.kron(np.sin(phase), eye),
        np.repeat(np.cos(twist), rows, axis=0),
        np.repeat(np.sin(twist), rows, axis=0),
        np.cos(turn),
        np.sin(turn),
        np.repeat(divisor, rows, axis=0),
        np.repeat(zero_mode, rows, axis=0),
        widen,
        take_last,
        take_first,
    )
    return [jnp.asarray(t.astype(np.float32)) for t in tables]


def exchange_all(flat_winds, row_cosine, tracers):
    flat_rows, columns = flat_winds.shape
    levels, lon_cols, merged = tracers.shape
    n = lax.axis_size("lon")
    lon_index = lax.axis_index("lon")
    rows = flat_rows // n
    tracer_count = merged // row_cosine.shape[0]
    own_cosine = lax.dynamic_slice_in_dim(jnp.tile(row_cosine, flat_rows // row_cosine.shape[0]), lon_index * rows, rows, 0)
    scaled = (own_cosine / COS_FLOOR) ** 2
    scaled = jnp.tile(scaled, n).reshape(n * rows, 1)
    vmem = pl.BlockSpec(memory_space=pltpu.VMEM)
    west_cols = lon_cols - (lon_cols - 3) // 8 * 8
    lanes = -(-3 * tracer_count // 128) * 128
    shapes = [
        (flat_rows, columns + 2),
        (flat_rows, columns),
        (levels, west_cols, merged),
        (levels, 8, merged),
        (levels, lon_cols, lanes),
        (levels, lon_cols, lanes),
        (levels, columns + 2),
        (levels, columns + 2),
    ]
    return pl.pallas_call(
        functools.partial(filter_kernel, n, rows),
        out_shape=[jax.ShapeDtypeStruct(shape, jnp.float32) for shape in shapes],
        in_specs=[vmem] * 13 + [pl.BlockSpec(memory_space=pl.ANY)],
        out_specs=[vmem] * len(shapes),
        scratch_shapes=[
            pltpu.VMEM((flat_rows, columns), jnp.float32),
            pltpu.VMEM((flat_rows, columns + 2), jnp.float32),
            pltpu.SemaphoreType.DMA((n,)),
            pltpu.SemaphoreType.DMA((n,)),
            pltpu.SemaphoreType.DMA((n,)),
            pltpu.SemaphoreType.DMA((n,)),
            pltpu.SemaphoreType.DMA((8,)),
            pltpu.SemaphoreType.DMA((8,)),
            pltpu.SemaphoreType.DMA((2,)),
        ],
        compiler_params=pltpu.CompilerParams(collective_id=0, has_side_effects=True),
    )(flat_winds, scaled, *spectral_tables(n, rows, columns), tracers)


def stencil(padded, dim, faces, stride):

    def offset_cells(offset):
        return lax.slice_in_dim(padded, offset * stride, (offset + faces) * stride, axis=dim)

    left = (
        2.0 * offset_cells(0)
        - 13.0 * offset_cells(1)
        + 47.0 * offset_cells(2)
        + 27.0 * offset_cells(3)
        - 3.0 * offset_cells(4)
    ) / 60.0
    right = (
        2.0 * offset_cells(5)
        - 13.0 * offset_cells(4)
        + 47.0 * offset_cells(3)
        + 27.0 * offset_cells(2)
        - 3.0 * offset_cells(1)
    ) / 60.0
    return left, right


def spread(values, rows, tracer_count):
    lanes = jnp.arange(rows * tracer_count, dtype=jnp.int32) // tracer_count
    pick = (jnp.arange(rows, dtype=jnp.int32)[:, None] == lanes[None, :]).astype(jnp.float32)
    return jnp.einsum("ljc,jm->lcm", values, pick, precision=EXACT_MODE)


def local(tracers, wind_field):
    levels, lon_cols, merged = tracers.shape
    lat_rows = wind_field.shape[2]
    tracer_count = merged // lat_rows
    lat_total = lat_rows * lax.axis_size("lat")
    band = lax.axis_index("lat")
    first_row = band * lat_rows
    row_ids = first_row + jnp.arange(lat_rows, dtype=jnp.int32)
    row_cosine = jnp.cos(
        (row_ids.astype(jnp.float32) + 0.5) * (math.pi / lat_total) - 0.5 * math.pi
    )
    flat_winds = wind_field.reshape(2 * levels * lat_rows, lon_cols)
    wide, smoothed, west, east, south, north, v_south, v_north = exchange_all(
        flat_winds, row_cosine, tracers
    )
    west = west[:, west.shape[1] - 3 :]
    east = east[:, :3]
    south = south[..., south.shape[2] - 3 * tracer_count :]
    north = north[..., : 3 * tracer_count]
    v_south = v_south[:, :lon_cols]
    v_north = v_north[:, :lon_cols]
    smoothed = smoothed.reshape(2, levels, lat_rows, lon_cols)
    east_wide = wide.reshape(2, levels, lat_rows, lon_cols + 2)[0]
    north_wind = smoothed[1]
    u_pad = jnp.concatenate(
        [east_wide[..., lon_cols : lon_cols + 1], smoothed[0], east_wide[..., lon_cols + 1 :]],
        axis=2,
    )
    zonal_speed = 0.5 * (u_pad[:, :, : lon_cols + 1] + u_pad[:, :, 1:])
    v_pad = jnp.concatenate([v_south[:, None], north_wind, v_north[:, None]], axis=1)
    face_ids = first_row + jnp.arange(lat_rows + 1, dtype=jnp.int32)
    face_cosine = jnp.cos(face_ids.astype(jnp.float32) * (math.pi / lat_total) - 0.5 * math.pi)
    face_cosine = jnp.where((face_ids == 0) | (face_ids == lat_total), 0.0, face_cosine)
    merid_speed = 0.5 * (v_pad[:, : lat_rows + 1] + v_pad[:, 1:]) * face_cosine[None, :, None]
    zonal_rep = spread(zonal_speed, lat_rows, tracer_count)
    merid_rep = spread(merid_speed, lat_rows + 1, tracer_count)
    zonal_pad = jnp.concatenate([west, tracers, east], axis=1)
    left_x, right_x = stencil(zonal_pad, 1, lon_cols + 1, 1)
    zonal_flux = upwind(zonal_rep, left_x, right_x)
    merid_pad = jnp.concatenate([south, tracers, north], axis=2)
    left_y, right_y = stencil(merid_pad, 2, lat_rows + 1, tracer_count)
    merid_flux = upwind(merid_rep, left_y, right_y)
    metric = jnp.repeat(1.0 / jnp.maximum(row_cosine, COS_FLOOR), tracer_count)
    change = COURANT * (zonal_flux[:, 1:] - zonal_flux[:, :-1]) + COURANT * (
        merid_flux[:, :, tracer_count:] - merid_flux[:, :, :-tracer_count]
    )
    advected = tracers - metric[None, None, :] * change
    return (advected, smoothed)


def solution(mesh):
    placed = (P(None, "lon", "lat"), P(None, None, "lat", "lon"))
    return jax.shard_map(
        local,
        mesh=mesh,
        in_specs=placed,
        out_specs=(P(None, "lon", "lat"), P(None, None, "lat", "lon")),
        check_vma=False,
    )
```

```python
import functools
import math

import jax
import numpy as np
import jax.numpy as jnp
from jax import lax
from jax.experimental import pallas as pl
from jax.experimental.pallas import tpu as pltpu
from jax.sharding import PartitionSpec as P

MESH = pl.DeviceIdType.MESH

COURANT = 0.3
COS_FLOOR = 0.5
EXACT_MODE = lax.Precision.HIGHEST


def extended(array, sides, width, wrap):
    for axis, dim in sides:
        devices, length = (lax.axis_size(axis), array.shape[dim])
        up = [(i, (i + 1) % devices) for i in range(devices if wrap else devices - 1)]
        down = [(j, i) for i, j in up]
        last = lax.slice_in_dim(array, length - width, length, axis=dim)
        first = lax.slice_in_dim(array, 0, width, axis=dim)
        before = lax.ppermute(last, axis, up)
        after = lax.ppermute(first, axis, down)
        array = jnp.concatenate([before, array, after], axis=dim)
    return array


def damping(row_cosine, wavenumber, lon_total):
    sine = jnp.sin(wavenumber.astype(jnp.float32) * (math.pi / lon_total))
    divisor = jnp.where(wavenumber == 0, 1.0, sine * sine)
    scaled = (row_cosine / COS_FLOOR) ** 2
    scaled = scaled.reshape(scaled.shape + (1,) * wavenumber.ndim)
    return jnp.where(wavenumber == 0, 1.0, jnp.minimum(1.0, scaled / divisor))


def face_values(padded, axis, cells, stride):

    def offset_cells(offset):
        return lax.slice_in_dim(padded, offset * stride, (offset + cells + 1) * stride, axis=axis)

    left = (
        2.0 * offset_cells(0)
        - 13.0 * offset_cells(1)
        + 47.0 * offset_cells(2)
        + 27.0 * offset_cells(3)
        - 3.0 * offset_cells(4)
    ) / 60.0
    right = (
        2.0 * offset_cells(5)
        - 13.0 * offset_cells(4)
        + 47.0 * offset_cells(3)
        + 27.0 * offset_cells(2)
        - 3.0 * offset_cells(1)
    ) / 60.0
    return (left, right)


def upwind(speed, left, right):
    return jnp.maximum(speed, 0.0) * left + jnp.minimum(speed, 0.0) * right


def filter_kernel(n, rows, winds_ref, scaled_ref, kc_ref, ks_ref, tc_ref, ts_ref, c_ref, s_ref,
                  divisor_ref, zero_ref, widen_ref, prev_ref, next_ref, tracers_ref,
                  out_ref, smooth_ref, west_ref, east_ref, south_ref, north_ref, vsouth_ref, vnorth_ref,
                  stage_a, gathered, restored, stage_b, chip_send, chip_recv, pair_send, pair_recv,
                  halo_send, halo_recv, local_sem):
    me = lax.axis_index("lon")
    band = lax.axis_index("lat")
    bands = lax.axis_size("lat")
    pair = 2
    chips = n // pair
    chip, core = me // pair, me % pair
    partner = chip * pair + (1 - core)
    cross = lax.rem(me + 2 * core - 1 + n, n)
    up, down = lax.rem(band + 1, bands), lax.rem(band + bands - 1, bands)
    east_peer, west_peer = lax.rem(me + 1, n), lax.rem(me + n - 1, n)
    barrier = pltpu.get_barrier_semaphore()
    for k in range(1, chips):
        other = lax.rem(chip + k, chips) * pair + core
        pl.semaphore_signal(barrier, inc=1, device_id=(band, other), device_id_type=MESH)
    for device in ((band, partner), (band, cross), (up, me), (down, me)):
        pl.semaphore_signal(barrier, inc=1, device_id=device, device_id_type=MESH)
    pl.semaphore_wait(barrier, chips + 3)

    cols, merged = tracers_ref.shape[1], tracers_ref.shape[2]
    lane_depth = south_ref.shape[2]
    flat_rows = n * rows
    level_rows = flat_rows // 4

    def flat_row(ref, index):
        return ref.at[index // (pair * rows), (index // rows) % pair, pl.ds(index % rows, 1)]
    halo_plan = [
        (tracers_ref.at[:, pl.ds(cols - west_ref.shape[1], west_ref.shape[1]), :], west_ref, (band, east_peer)),
        (tracers_ref.at[:, pl.ds(0, east_ref.shape[1]), :], east_ref, (band, west_peer)),
        (tracers_ref.at[:, :, pl.ds(merged - lane_depth, lane_depth)], south_ref, (up, me)),
        (tracers_ref.at[:, :, pl.ds(0, lane_depth)], north_ref, (down, me)),
    ]
    for level in range(2):
        first = 2 * level_rows + level * level_rows
        halo_plan.append(
            (flat_row(out_ref, first + level_rows - 1), vsouth_ref.at[pl.ds(level, 1)], (up, me))
        )
    for level in range(2):
        first = 2 * level_rows + level * level_rows
        halo_plan.append((flat_row(out_ref, first), vnorth_ref.at[pl.ds(level, 1)], (down, me)))

    def halo_copy(index):
        source, target, device = halo_plan[index]
        return pltpu.make_async_remote_copy(
            src_ref=source,
            dst_ref=target,
            send_sem=halo_send.at[index],
            recv_sem=halo_recv.at[index],
            device_id=device,
            device_id_type=MESH,
        )

    def chip_rows(ref, index):
        return ref.at[index]

    def swap(source, stage, target, phase):
        sends = []
        for k in range(1, chips):
            other = lax.rem(chip + k, chips)
            copy = pltpu.make_async_remote_copy(
                src_ref=chip_rows(source, other),
                dst_ref=stage.at[chip],
                send_sem=chip_send.at[phase, other],
                recv_sem=chip_recv.at[phase, chip],
                device_id=(band, other * pair + core),
                device_id_type=MESH,
            )
            copy.start()
            sends.append(copy)
        own = pltpu.make_async_copy(chip_rows(source, chip), stage.at[chip], local_sem.at[phase, 0])
        own.start()
        own.wait()
        for k in range(1, chips):
            origin = lax.rem(chip + chips - k, chips)
            pltpu.make_async_remote_copy(
                src_ref=chip_rows(source, origin),
                dst_ref=stage.at[origin],
                send_sem=chip_send.at[phase, origin],
                recv_sem=chip_recv.at[phase, origin],
                device_id=(band, origin * pair + core),
                device_id_type=MESH,
            ).wait_recv()
        across = pltpu.make_async_remote_copy(
            src_ref=stage.at[:, 1 - core],
            dst_ref=target.at[:, core],
            send_sem=pair_send.at[phase],
            recv_sem=pair_recv.at[phase],
            device_id=(band, partner),
            device_id_type=MESH,
        )
        across.start()
        keep = pltpu.make_async_copy(stage.at[:, core], target.at[:, core], local_sem.at[phase, 1])
        keep.start()
        keep.wait()
        pltpu.make_async_remote_copy(
            src_ref=stage.at[:, core],
            dst_ref=target.at[:, 1 - core],
            send_sem=pair_send.at[phase],
            recv_sem=pair_recv.at[phase],
            device_id=(band, partner),
            device_id_type=MESH,
        ).wait_recv()
        for copy in sends:
            copy.wait_send()
        across.wait_send()

    tracer_halos = [halo_copy(i) for i in range(4)]
    for copy in tracer_halos:
        copy.start()
    swap(winds_ref, stage_a, gathered, 0)

    def mm(a, b):
        return jnp.dot(a, b, precision=EXACT_MODE, preferred_element_type=jnp.float32)

    x = gathered[...].reshape(flat_rows, -1)
    kc, ks = kc_ref[...], ks_ref[...]
    tc, ts = tc_ref[...], ts_ref[...]
    c, s = c_ref[...], s_ref[...]
    re = mm(kc, x)
    im = -mm(ks, x)
    shifted_re = re * tc + im * ts
    shifted_im = im * tc - re * ts
    modes_re = mm(shifted_re, c) + mm(shifted_im, s)
    modes_im = mm(shifted_im, c) - mm(shifted_re, s)
    factor = jnp.where(
        zero_ref[...] > 0.0, 1.0, jnp.minimum(1.0, scaled_ref[...] / divisor_ref[...])
    )
    modes_re = modes_re * factor
    modes_im = modes_im * factor
    back_re = mm(modes_re, c) - mm(modes_im, s)
    back_im = mm(modes_im, c) + mm(modes_re, s)
    out_re = back_re * tc - back_im * ts
    out_im = back_im * tc + back_re * ts
    result = (mm(kc, out_re) - mm(ks, out_im)) / (n * x.shape[1])
    restored[...] = (
        mm(result, widen_ref[...])
        + mm(jnp.roll(result, rows, axis=0), prev_ref[...])
        + mm(jnp.roll(result, -rows, axis=0), next_ref[...])
    ).reshape(restored.shape)
    swap(restored, stage_b, out_ref, 1)
    smooth_ref[...] = out_ref[..., : smooth_ref.shape[3]]
    wind_halos = [halo_copy(i) for i in range(4, 8)]
    for copy in wind_halos:
        copy.start()
    for copy in tracer_halos + wind_halos:
        copy.wait_recv()
    for copy in tracer_halos + wind_halos:
        copy.wait_send()

    @pl.when(band == 0)
    def _():
        south_ref[...] = jnp.zeros(south_ref.shape, jnp.float32)
        vsouth_ref[...] = jnp.zeros(vsouth_ref.shape, jnp.float32)

    @pl.when(band == bands - 1)
    def _():
        north_ref[...] = jnp.zeros(north_ref.shape, jnp.float32)
        vnorth_ref[...] = jnp.zeros(vnorth_ref.shape, jnp.float32)


def spectral_tables(n, rows, columns):
    lon_total = n * columns
    blocks = np.arange(n)
    phase = 2.0 * np.pi * (np.outer(blocks, blocks) % n) / n
    eye = np.eye(rows)
    column_ids = np.arange(columns)
    twist = 2.0 * np.pi * (np.outer(blocks, column_ids) % lon_total) / lon_total
    turn = 2.0 * np.pi * (np.outer(column_ids, column_ids) % columns) / columns
    wavenumber = blocks[:, None] + n * column_ids[None, :]
    sine = np.sin(wavenumber.astype(np.float32) * np.float32(math.pi / lon_total))
    divisor = np.where(wavenumber == 0, np.float32(1.0), sine * sine).astype(np.float32)
    zero_mode = (wavenumber == 0).astype(np.float32)
    widen = np.eye(columns, columns + 2)
    take_last = np.zeros((columns, columns + 2))
    take_last[columns - 1, columns] = 1.0
    take_first = np.zeros((columns, columns + 2))
    take_first[0, columns + 1] = 1.0
    tables = (
        np.kron(np.cos(phase), eye),
        np.kron(np.sin(phase), eye),
        np.repeat(np.cos(twist), rows, axis=0),
        np.repeat(np.sin(twist), rows, axis=0),
        np.cos(turn),
        np.sin(turn),
        np.repeat(divisor, rows, axis=0),
        np.repeat(zero_mode, rows, axis=0),
        widen,
        take_last,
        take_first,
    )
    return [jnp.asarray(t.astype(np.float32)) for t in tables]


def exchange_all(flat_winds, row_cosine, tracers):
    flat_rows, columns = flat_winds.shape
    levels, lon_cols, merged = tracers.shape
    n = lax.axis_size("lon")
    lon_index = lax.axis_index("lon")
    rows = flat_rows // n
    tracer_count = merged // row_cosine.shape[0]
    own_cosine = lax.dynamic_slice_in_dim(jnp.tile(row_cosine, flat_rows // row_cosine.shape[0]), lon_index * rows, rows, 0)
    scaled = (own_cosine / COS_FLOOR) ** 2
    scaled = jnp.tile(scaled, n).reshape(n * rows, 1)
    vmem = pl.BlockSpec(memory_space=pltpu.VMEM)
    west_cols = lon_cols - (lon_cols - 3) // 8 * 8
    lanes = -(-3 * tracer_count // 128) * 128
    shapes = [
        (n // 2, 2, rows, columns + 2),
        (n // 2, 2, rows, columns),
        (levels, west_cols, merged),
        (levels, 8, merged),
        (levels, lon_cols, lanes),
        (levels, lon_cols, lanes),
        (levels, columns + 2),
        (levels, columns + 2),
    ]
    return pl.pallas_call(
        functools.partial(filter_kernel, n, rows),
        out_shape=[jax.ShapeDtypeStruct(shape, jnp.float32) for shape in shapes],
        in_specs=[vmem] * 13 + [pl.BlockSpec(memory_space=pl.ANY)],
        out_specs=[vmem] * len(shapes),
        scratch_shapes=[
            pltpu.VMEM((n // 2, 2, rows, columns), jnp.float32),
            pltpu.VMEM((n // 2, 2, rows, columns), jnp.float32),
            pltpu.VMEM((n // 2, 2, rows, columns + 2), jnp.float32),
            pltpu.VMEM((n // 2, 2, rows, columns + 2), jnp.float32),
            pltpu.SemaphoreType.DMA((2, n // 2)),
            pltpu.SemaphoreType.DMA((2, n // 2)),
            pltpu.SemaphoreType.DMA((2,)),
            pltpu.SemaphoreType.DMA((2,)),
            pltpu.SemaphoreType.DMA((8,)),
            pltpu.SemaphoreType.DMA((8,)),
            pltpu.SemaphoreType.DMA((2, 2)),
        ],
        compiler_params=pltpu.CompilerParams(collective_id=0, has_side_effects=True),
    )(flat_winds.reshape(n // 2, 2, rows, columns), scaled, *spectral_tables(n, rows, columns), tracers)


def stencil(padded, dim, faces, stride):

    def offset_cells(offset):
        return lax.slice_in_dim(padded, offset * stride, (offset + faces) * stride, axis=dim)

    left = (
        2.0 * offset_cells(0)
        - 13.0 * offset_cells(1)
        + 47.0 * offset_cells(2)
        + 27.0 * offset_cells(3)
        - 3.0 * offset_cells(4)
    ) / 60.0
    right = (
        2.0 * offset_cells(5)
        - 13.0 * offset_cells(4)
        + 47.0 * offset_cells(3)
        + 27.0 * offset_cells(2)
        - 3.0 * offset_cells(1)
    ) / 60.0
    return left, right


def spread(values, rows, tracer_count):
    lanes = jnp.arange(rows * tracer_count, dtype=jnp.int32) // tracer_count
    pick = (jnp.arange(rows, dtype=jnp.int32)[:, None] == lanes[None, :]).astype(jnp.float32)
    return jnp.einsum("ljc,jm->lcm", values, pick, precision=EXACT_MODE)


def local(tracers, wind_field):
    levels, lon_cols, merged = tracers.shape
    lat_rows = wind_field.shape[2]
    tracer_count = merged // lat_rows
    lat_total = lat_rows * lax.axis_size("lat")
    band = lax.axis_index("lat")
    first_row = band * lat_rows
    row_ids = first_row + jnp.arange(lat_rows, dtype=jnp.int32)
    row_cosine = jnp.cos(
        (row_ids.astype(jnp.float32) + 0.5) * (math.pi / lat_total) - 0.5 * math.pi
    )
    flat_winds = wind_field.reshape(2 * levels * lat_rows, lon_cols)
    wide, smoothed, west, east, south, north, v_south, v_north = exchange_all(
        flat_winds, row_cosine, tracers
    )
    west = west[:, west.shape[1] - 3 :]
    east = east[:, :3]
    south = south[..., south.shape[2] - 3 * tracer_count :]
    north = north[..., : 3 * tracer_count]
    v_south = v_south[:, :lon_cols]
    v_north = v_north[:, :lon_cols]
    smoothed = smoothed.reshape(2, levels, lat_rows, lon_cols)
    east_wide = wide.reshape(2, levels, lat_rows, lon_cols + 2)[0]
    north_wind = smoothed[1]
    u_pad = jnp.concatenate(
        [east_wide[..., lon_cols : lon_cols + 1], smoothed[0], east_wide[..., lon_cols + 1 :]],
        axis=2,
    )
    zonal_speed = 0.5 * (u_pad[:, :, : lon_cols + 1] + u_pad[:, :, 1:])
    v_pad = jnp.concatenate([v_south[:, None], north_wind, v_north[:, None]], axis=1)
    face_ids = first_row + jnp.arange(lat_rows + 1, dtype=jnp.int32)
    face_cosine = jnp.cos(face_ids.astype(jnp.float32) * (math.pi / lat_total) - 0.5 * math.pi)
    face_cosine = jnp.where((face_ids == 0) | (face_ids == lat_total), 0.0, face_cosine)
    merid_speed = 0.5 * (v_pad[:, : lat_rows + 1] + v_pad[:, 1:]) * face_cosine[None, :, None]
    zonal_rep = spread(zonal_speed, lat_rows, tracer_count)
    merid_rep = spread(merid_speed, lat_rows + 1, tracer_count)
    zonal_pad = jnp.concatenate([west, tracers, east], axis=1)
    left_x, right_x = stencil(zonal_pad, 1, lon_cols + 1, 1)
    zonal_flux = upwind(zonal_rep, left_x, right_x)
    merid_pad = jnp.concatenate([south, tracers, north], axis=2)
    left_y, right_y = stencil(merid_pad, 2, lat_rows + 1, tracer_count)
    merid_flux = upwind(merid_rep, left_y, right_y)
    metric = jnp.repeat(1.0 / jnp.maximum(row_cosine, COS_FLOOR), tracer_count)
    change = COURANT * (zonal_flux[:, 1:] - zonal_flux[:, :-1]) + COURANT * (
        merid_flux[:, :, tracer_count:] - merid_flux[:, :, :-tracer_count]
    )
    advected = tracers - metric[None, None, :] * change
    return (advected, smoothed)


def solution(mesh):
    placed = (P(None, "lon", "lat"), P(None, None, "lat", "lon"))
    return jax.shard_map(
        local,
        mesh=mesh,
        in_specs=placed,
        out_specs=(P(None, "lon", "lat"), P(None, None, "lat", "lon")),
        check_vma=False,
    )
```

```python
import functools
import math

import jax
import numpy as np
import jax.numpy as jnp
from jax import lax
from jax.experimental import pallas as pl
from jax.experimental.pallas import tpu as pltpu
from jax.sharding import PartitionSpec as P

MESH = pl.DeviceIdType.MESH

COURANT = 0.3
COS_FLOOR = 0.5
EXACT_MODE = lax.Precision.HIGHEST


def extended(array, sides, width, wrap):
    for axis, dim in sides:
        devices, length = (lax.axis_size(axis), array.shape[dim])
        up = [(i, (i + 1) % devices) for i in range(devices if wrap else devices - 1)]
        down = [(j, i) for i, j in up]
        last = lax.slice_in_dim(array, length - width, length, axis=dim)
        first = lax.slice_in_dim(array, 0, width, axis=dim)
        before = lax.ppermute(last, axis, up)
        after = lax.ppermute(first, axis, down)
        array = jnp.concatenate([before, array, after], axis=dim)
    return array


def damping(row_cosine, wavenumber, lon_total):
    sine = jnp.sin(wavenumber.astype(jnp.float32) * (math.pi / lon_total))
    divisor = jnp.where(wavenumber == 0, 1.0, sine * sine)
    scaled = (row_cosine / COS_FLOOR) ** 2
    scaled = scaled.reshape(scaled.shape + (1,) * wavenumber.ndim)
    return jnp.where(wavenumber == 0, 1.0, jnp.minimum(1.0, scaled / divisor))


def face_values(padded, axis, cells, stride):

    def offset_cells(offset):
        return lax.slice_in_dim(padded, offset * stride, (offset + cells + 1) * stride, axis=axis)

    left = (
        2.0 * offset_cells(0)
        - 13.0 * offset_cells(1)
        + 47.0 * offset_cells(2)
        + 27.0 * offset_cells(3)
        - 3.0 * offset_cells(4)
    ) / 60.0
    right = (
        2.0 * offset_cells(5)
        - 13.0 * offset_cells(4)
        + 47.0 * offset_cells(3)
        + 27.0 * offset_cells(2)
        - 3.0 * offset_cells(1)
    ) / 60.0
    return (left, right)


def upwind(speed, left, right):
    return jnp.maximum(speed, 0.0) * left + jnp.minimum(speed, 0.0) * right


def filter_kernel(n, rows, winds_ref, scaled_ref, kc_ref, ks_ref, tc_ref, ts_ref, c_ref, s_ref,
                  divisor_ref, zero_ref, widen_ref, prev_ref, next_ref, tracers_ref,
                  out_ref, smooth_ref, west_ref, east_ref, south_ref, north_ref, vsouth_ref, vnorth_ref,
                  gathered, restored, send_a, recv_a, send_b, recv_b, halo_send, halo_recv, local_sem):
    me = lax.axis_index("lon")
    band = lax.axis_index("lat")
    bands = lax.axis_size("lat")
    up, down = lax.rem(band + 1, bands), lax.rem(band + bands - 1, bands)
    east_peer, west_peer = lax.rem(me + 1, n), lax.rem(me + n - 1, n)
    barrier = pltpu.get_barrier_semaphore()
    for k in range(1, n):
        peer = lax.rem(me + k, n)
        pl.semaphore_signal(barrier, inc=1, device_id=(band, peer), device_id_type=MESH)
    for other in (up, down):
        pl.semaphore_signal(barrier, inc=1, device_id=(other, me), device_id_type=MESH)
    pl.semaphore_wait(barrier, n + 1)

    cols, merged = tracers_ref.shape[1], tracers_ref.shape[2]
    lane_depth = south_ref.shape[2]
    flat_rows = out_ref.shape[0]
    level_rows = flat_rows // 4
    halo_plan = [
        (tracers_ref.at[:, pl.ds(cols - west_ref.shape[1], west_ref.shape[1]), :], west_ref, (band, east_peer)),
        (tracers_ref.at[:, pl.ds(0, east_ref.shape[1]), :], east_ref, (band, west_peer)),
        (tracers_ref.at[:, :, pl.ds(merged - lane_depth, lane_depth)], south_ref, (up, me)),
        (tracers_ref.at[:, :, pl.ds(0, lane_depth)], north_ref, (down, me)),
    ]
    for level in range(2):
        first = 2 * level_rows + level * level_rows
        halo_plan.append(
            (out_ref.at[pl.ds(first + level_rows - 1, 1)], vsouth_ref.at[pl.ds(level, 1)], (up, me))
        )
    for level in range(2):
        first = 2 * level_rows + level * level_rows
        halo_plan.append((out_ref.at[pl.ds(first, 1)], vnorth_ref.at[pl.ds(level, 1)], (down, me)))

    def halo_copy(index):
        source, target, device = halo_plan[index]
        return pltpu.make_async_remote_copy(
            src_ref=source,
            dst_ref=target,
            send_sem=halo_send.at[index],
            recv_sem=halo_recv.at[index],
            device_id=device,
            device_id_type=MESH,
        )

    def block(ref, index):
        return ref.at[pl.ds(pl.multiple_of(index * rows, rows), rows)]

    def swap(source, target, send_sem, recv_sem, slot):
        sends = []
        for k in range(1, n):
            peer = lax.rem(me + k, n)
            copy = pltpu.make_async_remote_copy(
                src_ref=block(source, peer),
                dst_ref=block(target, me),
                send_sem=send_sem.at[peer],
                recv_sem=recv_sem.at[me],
                device_id=(band, peer),
                device_id_type=MESH,
            )
            copy.start()
            sends.append(copy)
        own = pltpu.make_async_copy(block(source, me), block(target, me), local_sem.at[slot])
        own.start()
        return sends, own

    def settle(source, target, send_sem, recv_sem, sends, own):
        own.wait()
        for k in range(1, n):
            origin = lax.rem(me + n - k, n)
            pltpu.make_async_remote_copy(
                src_ref=block(source, origin),
                dst_ref=block(target, origin),
                send_sem=send_sem.at[origin],
                recv_sem=recv_sem.at[origin],
                device_id=(band, origin),
                device_id_type=MESH,
            ).wait_recv()
        for copy in sends:
            copy.wait_send()

    sends, own = swap(winds_ref, gathered, send_a, recv_a, 0)
    tracer_halos = [halo_copy(i) for i in range(4)]
    for copy in tracer_halos:
        copy.start()
    settle(winds_ref, gathered, send_a, recv_a, sends, own)

    def mm(a, b):
        return jnp.dot(a, b, precision=EXACT_MODE, preferred_element_type=jnp.float32)

    x = gathered[...]
    half = x.shape[0]
    tc, ts = tc_ref[...], ts_ref[...]
    stacked = mm(kc_ref[...], x)
    re, im = stacked[:half], -stacked[half:]
    shifted_re = re * tc + im * ts
    shifted_im = im * tc - re * ts
    stacked = jnp.concatenate([shifted_re, shifted_im], axis=0)
    with_cos = mm(stacked, c_ref[...])
    with_sin = mm(stacked, s_ref[...])
    modes_re = with_cos[:half] + with_sin[half:]
    modes_im = with_cos[half:] - with_sin[:half]
    factor = jnp.where(
        zero_ref[...] > 0.0, 1.0, jnp.minimum(1.0, scaled_ref[...] / divisor_ref[...])
    )
    stacked = jnp.concatenate([modes_re * factor, modes_im * factor], axis=0)
    with_cos = mm(stacked, widen_ref[...])
    with_sin = mm(stacked, prev_ref[...])
    back_re = with_cos[:half] - with_sin[half:]
    back_im = with_cos[half:] + with_sin[:half]
    tcw, tsw = next_ref[0], next_ref[1]
    out_re = back_re * tcw - back_im * tsw
    out_im = back_im * tcw + back_re * tsw
    result = mm(ks_ref[...], jnp.concatenate([out_re, out_im], axis=0)) / (n * x.shape[1])
    columns = x.shape[1]
    lane = lax.broadcasted_iota(jnp.int32, result.shape, 1)
    before = jnp.sum(
        jnp.where(lane == columns - 1, jnp.roll(result, rows, axis=0), 0.0), axis=1, keepdims=True
    )
    after = jnp.sum(jnp.where(lane == 0, jnp.roll(result, -rows, axis=0), 0.0), axis=1, keepdims=True)
    restored[...] = jnp.where(lane == columns, before, jnp.where(lane == columns + 1, after, result))
    sends, own = swap(restored, out_ref, send_b, recv_b, 1)
    settle(restored, out_ref, send_b, recv_b, sends, own)
    wind_halos = [halo_copy(i) for i in range(4, 8)]
    for copy in wind_halos:
        copy.start()
    smooth_ref[...] = out_ref[:, : smooth_ref.shape[1]]
    for copy in tracer_halos + wind_halos:
        copy.wait_recv()
    for copy in tracer_halos + wind_halos:
        copy.wait_send()

    @pl.when(band == 0)
    def _():
        south_ref[...] = jnp.zeros(south_ref.shape, jnp.float32)
        vsouth_ref[...] = jnp.zeros(vsouth_ref.shape, jnp.float32)

    @pl.when(band == bands - 1)
    def _():
        north_ref[...] = jnp.zeros(north_ref.shape, jnp.float32)
        vnorth_ref[...] = jnp.zeros(vnorth_ref.shape, jnp.float32)


def spectral_tables(n, rows, columns):
    lon_total = n * columns
    blocks = np.arange(n)
    phase = 2.0 * np.pi * (np.outer(blocks, blocks) % n) / n
    eye = np.eye(rows)
    column_ids = np.arange(columns)
    twist = 2.0 * np.pi * (np.outer(blocks, column_ids) % lon_total) / lon_total
    turn = 2.0 * np.pi * (np.outer(column_ids, column_ids) % columns) / columns
    wavenumber = blocks[:, None] + n * column_ids[None, :]
    sine = np.sin(wavenumber.astype(np.float32) * np.float32(math.pi / lon_total))
    divisor = np.where(wavenumber == 0, np.float32(1.0), sine * sine).astype(np.float32)
    zero_mode = (wavenumber == 0).astype(np.float32)
    widen = np.eye(columns, columns + 2)
    kron_cos, kron_sin = np.kron(np.cos(phase), eye), np.kron(np.sin(phase), eye)
    twist_wide = np.stack(
        [np.repeat(np.cos(twist), rows, axis=0) @ widen, np.repeat(np.sin(twist), rows, axis=0) @ widen]
    )
    tables = (
        np.concatenate([kron_cos, kron_sin], axis=0),
        np.concatenate([kron_cos, -kron_sin], axis=1),
        np.repeat(np.cos(twist), rows, axis=0),
        np.repeat(np.sin(twist), rows, axis=0),
        np.cos(turn),
        np.sin(turn),
        np.repeat(divisor, rows, axis=0),
        np.repeat(zero_mode, rows, axis=0),
        np.cos(turn) @ widen,
        np.sin(turn) @ widen,
        twist_wide,
    )
    return [jnp.asarray(t.astype(np.float32)) for t in tables]


def exchange_all(flat_winds, row_cosine, tracers):
    flat_rows, columns = flat_winds.shape
    levels, lon_cols, merged = tracers.shape
    n = lax.axis_size("lon")
    lon_index = lax.axis_index("lon")
    rows = flat_rows // n
    tracer_count = merged // row_cosine.shape[0]
    own_cosine = lax.dynamic_slice_in_dim(jnp.tile(row_cosine, flat_rows // row_cosine.shape[0]), lon_index * rows, rows, 0)
    scaled = (own_cosine / COS_FLOOR) ** 2
    scaled = jnp.tile(scaled, n).reshape(n * rows, 1)
    vmem = pl.BlockSpec(memory_space=pltpu.VMEM)
    west_cols = lon_cols - (lon_cols - 3) // 8 * 8
    lanes = -(-3 * tracer_count // 128) * 128
    shapes = [
        (flat_rows, columns + 2),
        (flat_rows, columns),
        (levels, west_cols, merged),
        (levels, 8, merged),
        (levels, lon_cols, lanes),
        (levels, lon_cols, lanes),
        (levels, columns + 2),
        (levels, columns + 2),
    ]
    return pl.pallas_call(
        functools.partial(filter_kernel, n, rows),
        out_shape=[jax.ShapeDtypeStruct(shape, jnp.float32) for shape in shapes],
        in_specs=[vmem] * 13 + [pl.BlockSpec(memory_space=pl.ANY)],
        out_specs=[vmem] * len(shapes),
        scratch_shapes=[
            pltpu.VMEM((flat_rows, columns), jnp.float32),
            pltpu.VMEM((flat_rows, columns + 2), jnp.float32),
            pltpu.SemaphoreType.DMA((n,)),
            pltpu.SemaphoreType.DMA((n,)),
            pltpu.SemaphoreType.DMA((n,)),
            pltpu.SemaphoreType.DMA((n,)),
            pltpu.SemaphoreType.DMA((8,)),
            pltpu.SemaphoreType.DMA((8,)),
            pltpu.SemaphoreType.DMA((2,)),
        ],
        compiler_params=pltpu.CompilerParams(collective_id=0, has_side_effects=True),
    )(flat_winds, scaled, *spectral_tables(n, rows, columns), tracers)


def stencil(padded, dim, faces, stride):

    def offset_cells(offset):
        return lax.slice_in_dim(padded, offset * stride, (offset + faces) * stride, axis=dim)

    left = (
        2.0 * offset_cells(0)
        - 13.0 * offset_cells(1)
        + 47.0 * offset_cells(2)
        + 27.0 * offset_cells(3)
        - 3.0 * offset_cells(4)
    ) / 60.0
    right = (
        2.0 * offset_cells(5)
        - 13.0 * offset_cells(4)
        + 47.0 * offset_cells(3)
        + 27.0 * offset_cells(2)
        - 3.0 * offset_cells(1)
    ) / 60.0
    return left, right


def spread(values, rows, tracer_count):
    lanes = jnp.arange(rows * tracer_count, dtype=jnp.int32) // tracer_count
    pick = (jnp.arange(rows, dtype=jnp.int32)[:, None] == lanes[None, :]).astype(jnp.float32)
    return jnp.einsum("ljc,jm->lcm", values, pick, precision=EXACT_MODE)


def local(tracers, wind_field):
    levels, lon_cols, merged = tracers.shape
    lat_rows = wind_field.shape[2]
    tracer_count = merged // lat_rows
    lat_total = lat_rows * lax.axis_size("lat")
    band = lax.axis_index("lat")
    first_row = band * lat_rows
    row_ids = first_row + jnp.arange(lat_rows, dtype=jnp.int32)
    row_cosine = jnp.cos(
        (row_ids.astype(jnp.float32) + 0.5) * (math.pi / lat_total) - 0.5 * math.pi
    )
    flat_winds = wind_field.reshape(2 * levels * lat_rows, lon_cols)
    wide, smoothed, west, east, south, north, v_south, v_north = exchange_all(
        flat_winds, row_cosine, tracers
    )
    west = west[:, west.shape[1] - 3 :]
    east = east[:, :3]
    south = south[..., south.shape[2] - 3 * tracer_count :]
    north = north[..., : 3 * tracer_count]
    v_south = v_south[:, :lon_cols]
    v_north = v_north[:, :lon_cols]
    smoothed = smoothed.reshape(2, levels, lat_rows, lon_cols)
    east_wide = wide.reshape(2, levels, lat_rows, lon_cols + 2)[0]
    north_wind = smoothed[1]
    u_pad = jnp.concatenate(
        [east_wide[..., lon_cols : lon_cols + 1], smoothed[0], east_wide[..., lon_cols + 1 :]],
        axis=2,
    )
    zonal_speed = 0.5 * (u_pad[:, :, : lon_cols + 1] + u_pad[:, :, 1:])
    v_pad = jnp.concatenate([v_south[:, None], north_wind, v_north[:, None]], axis=1)
    face_ids = first_row + jnp.arange(lat_rows + 1, dtype=jnp.int32)
    face_cosine = jnp.cos(face_ids.astype(jnp.float32) * (math.pi / lat_total) - 0.5 * math.pi)
    face_cosine = jnp.where((face_ids == 0) | (face_ids == lat_total), 0.0, face_cosine)
    merid_speed = 0.5 * (v_pad[:, : lat_rows + 1] + v_pad[:, 1:]) * face_cosine[None, :, None]
    zonal_rep = spread(zonal_speed, lat_rows, tracer_count)
    merid_rep = spread(merid_speed, lat_rows + 1, tracer_count)
    zonal_pad = jnp.concatenate([west, tracers, east], axis=1)
    left_x, right_x = stencil(zonal_pad, 1, lon_cols + 1, 1)
    zonal_flux = upwind(zonal_rep, left_x, right_x)
    merid_pad = jnp.concatenate([south, tracers, north], axis=2)
    left_y, right_y = stencil(merid_pad, 2, lat_rows + 1, tracer_count)
    merid_flux = upwind(merid_rep, left_y, right_y)
    metric = jnp.repeat(1.0 / jnp.maximum(row_cosine, COS_FLOOR), tracer_count)
    change = COURANT * (zonal_flux[:, 1:] - zonal_flux[:, :-1]) + COURANT * (
        merid_flux[:, :, tracer_count:] - merid_flux[:, :, :-tracer_count]
    )
    advected = tracers - metric[None, None, :] * change
    return (advected, smoothed)


def solution(mesh):
    placed = (P(None, "lon", "lat"), P(None, None, "lat", "lon"))
    return jax.shard_map(
        local,
        mesh=mesh,
        in_specs=placed,
        out_specs=(P(None, "lon", "lat"), P(None, None, "lat", "lon")),
        check_vma=False,
    )
```

```python
import functools
import math

import jax
import numpy as np
import jax.numpy as jnp
from jax import lax
from jax.experimental import pallas as pl
from jax.experimental.pallas import tpu as pltpu
from jax.sharding import PartitionSpec as P

MESH = pl.DeviceIdType.MESH

COURANT = 0.3
COS_FLOOR = 0.5
EXACT_MODE = lax.Precision.HIGHEST


def extended(array, sides, width, wrap):
    for axis, dim in sides:
        devices, length = (lax.axis_size(axis), array.shape[dim])
        up = [(i, (i + 1) % devices) for i in range(devices if wrap else devices - 1)]
        down = [(j, i) for i, j in up]
        last = lax.slice_in_dim(array, length - width, length, axis=dim)
        first = lax.slice_in_dim(array, 0, width, axis=dim)
        before = lax.ppermute(last, axis, up)
        after = lax.ppermute(first, axis, down)
        array = jnp.concatenate([before, array, after], axis=dim)
    return array


def damping(row_cosine, wavenumber, lon_total):
    sine = jnp.sin(wavenumber.astype(jnp.float32) * (math.pi / lon_total))
    divisor = jnp.where(wavenumber == 0, 1.0, sine * sine)
    scaled = (row_cosine / COS_FLOOR) ** 2
    scaled = scaled.reshape(scaled.shape + (1,) * wavenumber.ndim)
    return jnp.where(wavenumber == 0, 1.0, jnp.minimum(1.0, scaled / divisor))


def face_values(padded, axis, cells, stride):

    def offset_cells(offset):
        return lax.slice_in_dim(padded, offset * stride, (offset + cells + 1) * stride, axis=axis)

    left = (
        2.0 * offset_cells(0)
        - 13.0 * offset_cells(1)
        + 47.0 * offset_cells(2)
        + 27.0 * offset_cells(3)
        - 3.0 * offset_cells(4)
    ) / 60.0
    right = (
        2.0 * offset_cells(5)
        - 13.0 * offset_cells(4)
        + 47.0 * offset_cells(3)
        + 27.0 * offset_cells(2)
        - 3.0 * offset_cells(1)
    ) / 60.0
    return (left, right)


def upwind(speed, left, right):
    return jnp.maximum(speed, 0.0) * left + jnp.minimum(speed, 0.0) * right


def filter_kernel(n, rows, winds_ref, scaled_ref, kc_ref, ks_ref, tc_ref, ts_ref, c_ref, s_ref,
                  divisor_ref, zero_ref, widen_ref, prev_ref, next_ref, tracers_ref,
                  out_ref, smooth_ref, west_ref, east_ref, south_ref, north_ref, vsouth_ref, vnorth_ref,
                  gathered, restored, send_a, recv_a, send_b, recv_b, halo_send, halo_recv, local_sem):
    me = lax.axis_index("lon")
    band = lax.axis_index("lat")
    bands = lax.axis_size("lat")
    up, down = lax.rem(band + 1, bands), lax.rem(band + bands - 1, bands)
    east_peer, west_peer = lax.rem(me + 1, n), lax.rem(me + n - 1, n)
    barrier = pltpu.get_barrier_semaphore()
    for k in range(1, n):
        peer = lax.rem(me + k, n)
        pl.semaphore_signal(barrier, inc=1, device_id=(band, peer), device_id_type=MESH)
    for other in (up, down):
        pl.semaphore_signal(barrier, inc=1, device_id=(other, me), device_id_type=MESH)
    pl.semaphore_wait(barrier, n + 1)

    cols, merged = tracers_ref.shape[1], tracers_ref.shape[2]
    lane_depth = south_ref.shape[2]
    flat_rows = out_ref.shape[0]
    level_rows = flat_rows // 4
    halo_plan = [
        (tracers_ref.at[:, pl.ds(cols - west_ref.shape[1], west_ref.shape[1]), :], west_ref, (band, east_peer)),
        (tracers_ref.at[:, pl.ds(0, east_ref.shape[1]), :], east_ref, (band, west_peer)),
        (tracers_ref.at[:, :, pl.ds(merged - lane_depth, lane_depth)], south_ref, (up, me)),
        (tracers_ref.at[:, :, pl.ds(0, lane_depth)], north_ref, (down, me)),
    ]
    for level in range(2):
        first = 2 * level_rows + level * level_rows
        halo_plan.append(
            (out_ref.at[pl.ds(first + level_rows - 1, 1)], vsouth_ref.at[pl.ds(level, 1)], (up, me))
        )
    for level in range(2):
        first = 2 * level_rows + level * level_rows
        halo_plan.append((out_ref.at[pl.ds(first, 1)], vnorth_ref.at[pl.ds(level, 1)], (down, me)))
    edge_rows = [2 * level_rows + k for k in (0, level_rows - 1, level_rows, 2 * level_rows - 1)]

    def halo_copy(index):
        source, target, device = halo_plan[index]
        return pltpu.make_async_remote_copy(
            src_ref=source,
            dst_ref=target,
            send_sem=halo_send.at[index],
            recv_sem=halo_recv.at[index],
            device_id=device,
            device_id_type=MESH,
        )

    def block(ref, index):
        return ref.at[pl.ds(pl.multiple_of(index * rows, rows), rows)]

    def swap(source, target, send_sem, recv_sem, slot):
        sends = []
        for k in range(1, n):
            peer = lax.rem(me + k, n)
            copy = pltpu.make_async_remote_copy(
                src_ref=block(source, peer),
                dst_ref=block(target, me),
                send_sem=send_sem.at[peer],
                recv_sem=recv_sem.at[me],
                device_id=(band, peer),
                device_id_type=MESH,
            )
            copy.start()
            sends.append(copy)
        own = pltpu.make_async_copy(block(source, me), block(target, me), local_sem.at[slot])
        own.start()
        return sends, own

    def settle(source, target, send_sem, recv_sem, sends, own):
        own.wait()
        for k in range(1, n):
            origin = lax.rem(me + n - k, n)
            pltpu.make_async_remote_copy(
                src_ref=block(source, origin),
                dst_ref=block(target, origin),
                send_sem=send_sem.at[origin],
                recv_sem=recv_sem.at[origin],
                device_id=(band, origin),
                device_id_type=MESH,
            ).wait_recv()
        for copy in sends:
            copy.wait_send()

    sends, own = swap(winds_ref, gathered, send_a, recv_a, 0)
    tracer_halos = [halo_copy(i) for i in range(4)]
    for copy in tracer_halos:
        copy.start()
    settle(winds_ref, gathered, send_a, recv_a, sends, own)

    def mm(a, b):
        return jnp.dot(a, b, precision=EXACT_MODE, preferred_element_type=jnp.float32)

    x = gathered[...]
    half = x.shape[0]
    tc, ts = tc_ref[...], ts_ref[...]
    stacked = mm(kc_ref[...], x)
    re, im = stacked[:half], -stacked[half:]
    shifted_re = re * tc + im * ts
    shifted_im = im * tc - re * ts
    stacked = jnp.concatenate([shifted_re, shifted_im], axis=0)
    with_cos = mm(stacked, c_ref[...])
    with_sin = mm(stacked, s_ref[...])
    modes_re = with_cos[:half] + with_sin[half:]
    modes_im = with_cos[half:] - with_sin[:half]
    factor = jnp.where(
        zero_ref[...] > 0.0, 1.0, jnp.minimum(1.0, scaled_ref[...] / divisor_ref[...])
    )
    stacked = jnp.concatenate([modes_re * factor, modes_im * factor], axis=0)
    with_cos = mm(stacked, widen_ref[...])
    with_sin = mm(stacked, prev_ref[...])
    back_re = with_cos[:half] - with_sin[half:]
    back_im = with_cos[half:] + with_sin[:half]
    tcw, tsw = next_ref[0], next_ref[1]
    out_re = back_re * tcw - back_im * tsw
    out_im = back_im * tcw + back_re * tsw
    result = mm(ks_ref[...], jnp.concatenate([out_re, out_im], axis=0)) / (n * x.shape[1])
    columns = x.shape[1]
    lane = lax.broadcasted_iota(jnp.int32, result.shape, 1)
    before = jnp.sum(
        jnp.where(lane == columns - 1, jnp.roll(result, rows, axis=0), 0.0), axis=1, keepdims=True
    )
    after = jnp.sum(jnp.where(lane == 0, jnp.roll(result, -rows, axis=0), 0.0), axis=1, keepdims=True)
    restored[...] = jnp.where(lane == columns, before, jnp.where(lane == columns + 1, after, result))
    sends, own = swap(restored, out_ref, send_b, recv_b, 1)
    own.wait()
    holders = sorted({row // rows for row in edge_rows})

    def arrival(origin):
        return pltpu.make_async_remote_copy(
            src_ref=block(restored, origin),
            dst_ref=block(out_ref, origin),
            send_sem=send_b.at[origin],
            recv_sem=recv_b.at[origin],
            device_id=(band, origin),
            device_id_type=MESH,
        )

    for holder in holders:

        @pl.when(me != holder)
        def _():
            arrival(holder).wait_recv()

    wind_halos = [halo_copy(i) for i in range(4, 8)]
    for copy in wind_halos:
        copy.start()
    for k in range(1, n):
        origin = lax.rem(me + n - k, n)
        pending = origin >= 0
        for holder in holders:
            pending = jnp.logical_and(pending, origin != holder)

        @pl.when(pending)
        def _():
            arrival(origin).wait_recv()

    for copy in sends:
        copy.wait_send()
    smooth_ref[...] = out_ref[:, : smooth_ref.shape[1]]
    for copy in tracer_halos + wind_halos:
        copy.wait_recv()
    for copy in tracer_halos + wind_halos:
        copy.wait_send()

    @pl.when(band == 0)
    def _():
        south_ref[...] = jnp.zeros(south_ref.shape, jnp.float32)
        vsouth_ref[...] = jnp.zeros(vsouth_ref.shape, jnp.float32)

    @pl.when(band == bands - 1)
    def _():
        north_ref[...] = jnp.zeros(north_ref.shape, jnp.float32)
        vnorth_ref[...] = jnp.zeros(vnorth_ref.shape, jnp.float32)


def spectral_tables(n, rows, columns):
    lon_total = n * columns
    blocks = np.arange(n)
    phase = 2.0 * np.pi * (np.outer(blocks, blocks) % n) / n
    eye = np.eye(rows)
    column_ids = np.arange(columns)
    twist = 2.0 * np.pi * (np.outer(blocks, column_ids) % lon_total) / lon_total
    turn = 2.0 * np.pi * (np.outer(column_ids, column_ids) % columns) / columns
    wavenumber = blocks[:, None] + n * column_ids[None, :]
    sine = np.sin(wavenumber.astype(np.float32) * np.float32(math.pi / lon_total))
    divisor = np.where(wavenumber == 0, np.float32(1.0), sine * sine).astype(np.float32)
    zero_mode = (wavenumber == 0).astype(np.float32)
    widen = np.eye(columns, columns + 2)
    kron_cos, kron_sin = np.kron(np.cos(phase), eye), np.kron(np.sin(phase), eye)
    twist_wide = np.stack(
        [np.repeat(np.cos(twist), rows, axis=0) @ widen, np.repeat(np.sin(twist), rows, axis=0) @ widen]
    )
    tables = (
        np.concatenate([kron_cos, kron_sin], axis=0),
        np.concatenate([kron_cos, -kron_sin], axis=1),
        np.repeat(np.cos(twist), rows, axis=0),
        np.repeat(np.sin(twist), rows, axis=0),
        np.cos(turn),
        np.sin(turn),
        np.repeat(divisor, rows, axis=0),
        np.repeat(zero_mode, rows, axis=0),
        np.cos(turn) @ widen,
        np.sin(turn) @ widen,
        twist_wide,
    )
    return [jnp.asarray(t.astype(np.float32)) for t in tables]


def exchange_all(flat_winds, row_cosine, tracers):
    flat_rows, columns = flat_winds.shape
    levels, lon_cols, merged = tracers.shape
    n = lax.axis_size("lon")
    lon_index = lax.axis_index("lon")
    rows = flat_rows // n
    tracer_count = merged // row_cosine.shape[0]
    own_cosine = lax.dynamic_slice_in_dim(jnp.tile(row_cosine, flat_rows // row_cosine.shape[0]), lon_index * rows, rows, 0)
    scaled = (own_cosine / COS_FLOOR) ** 2
    scaled = jnp.tile(scaled, n).reshape(n * rows, 1)
    vmem = pl.BlockSpec(memory_space=pltpu.VMEM)
    west_cols = lon_cols - (lon_cols - 3) // 8 * 8
    lanes = -(-3 * tracer_count // 128) * 128
    shapes = [
        (flat_rows, columns + 2),
        (flat_rows, columns),
        (levels, west_cols, merged),
        (levels, 8, merged),
        (levels, lon_cols, lanes),
        (levels, lon_cols, lanes),
        (levels, columns + 2),
        (levels, columns + 2),
    ]
    return pl.pallas_call(
        functools.partial(filter_kernel, n, rows),
        out_shape=[jax.ShapeDtypeStruct(shape, jnp.float32) for shape in shapes],
        in_specs=[vmem] * 13 + [pl.BlockSpec(memory_space=pl.ANY)],
        out_specs=[vmem] * len(shapes),
        scratch_shapes=[
            pltpu.VMEM((flat_rows, columns), jnp.float32),
            pltpu.VMEM((flat_rows, columns + 2), jnp.float32),
            pltpu.SemaphoreType.DMA((n,)),
            pltpu.SemaphoreType.DMA((n,)),
            pltpu.SemaphoreType.DMA((n,)),
            pltpu.SemaphoreType.DMA((n,)),
            pltpu.SemaphoreType.DMA((8,)),
            pltpu.SemaphoreType.DMA((8,)),
            pltpu.SemaphoreType.DMA((2,)),
        ],
        compiler_params=pltpu.CompilerParams(collective_id=0, has_side_effects=True),
    )(flat_winds, scaled, *spectral_tables(n, rows, columns), tracers)


def stencil(padded, dim, faces, stride):

    def offset_cells(offset):
        return lax.slice_in_dim(padded, offset * stride, (offset + faces) * stride, axis=dim)

    left = (
        2.0 * offset_cells(0)
        - 13.0 * offset_cells(1)
        + 47.0 * offset_cells(2)
        + 27.0 * offset_cells(3)
        - 3.0 * offset_cells(4)
    ) / 60.0
    right = (
        2.0 * offset_cells(5)
        - 13.0 * offset_cells(4)
        + 47.0 * offset_cells(3)
        + 27.0 * offset_cells(2)
        - 3.0 * offset_cells(1)
    ) / 60.0
    return left, right


def spread(values, rows, tracer_count):
    lanes = jnp.arange(rows * tracer_count, dtype=jnp.int32) // tracer_count
    pick = (jnp.arange(rows, dtype=jnp.int32)[:, None] == lanes[None, :]).astype(jnp.float32)
    return jnp.einsum("ljc,jm->lcm", values, pick, precision=EXACT_MODE)


def local(tracers, wind_field):
    levels, lon_cols, merged = tracers.shape
    lat_rows = wind_field.shape[2]
    tracer_count = merged // lat_rows
    lat_total = lat_rows * lax.axis_size("lat")
    band = lax.axis_index("lat")
    first_row = band * lat_rows
    row_ids = first_row + jnp.arange(lat_rows, dtype=jnp.int32)
    row_cosine = jnp.cos(
        (row_ids.astype(jnp.float32) + 0.5) * (math.pi / lat_total) - 0.5 * math.pi
    )
    flat_winds = wind_field.reshape(2 * levels * lat_rows, lon_cols)
    wide, smoothed, west, east, south, north, v_south, v_north = exchange_all(
        flat_winds, row_cosine, tracers
    )
    west = west[:, west.shape[1] - 3 :]
    east = east[:, :3]
    south = south[..., south.shape[2] - 3 * tracer_count :]
    north = north[..., : 3 * tracer_count]
    v_south = v_south[:, :lon_cols]
    v_north = v_north[:, :lon_cols]
    smoothed = smoothed.reshape(2, levels, lat_rows, lon_cols)
    east_wide = wide.reshape(2, levels, lat_rows, lon_cols + 2)[0]
    north_wind = smoothed[1]
    u_pad = jnp.concatenate(
        [east_wide[..., lon_cols : lon_cols + 1], smoothed[0], east_wide[..., lon_cols + 1 :]],
        axis=2,
    )
    zonal_speed = 0.5 * (u_pad[:, :, : lon_cols + 1] + u_pad[:, :, 1:])
    v_pad = jnp.concatenate([v_south[:, None], north_wind, v_north[:, None]], axis=1)
    face_ids = first_row + jnp.arange(lat_rows + 1, dtype=jnp.int32)
    face_cosine = jnp.cos(face_ids.astype(jnp.float32) * (math.pi / lat_total) - 0.5 * math.pi)
    face_cosine = jnp.where((face_ids == 0) | (face_ids == lat_total), 0.0, face_cosine)
    merid_speed = 0.5 * (v_pad[:, : lat_rows + 1] + v_pad[:, 1:]) * face_cosine[None, :, None]
    zonal_rep = spread(zonal_speed, lat_rows, tracer_count)
    merid_rep = spread(merid_speed, lat_rows + 1, tracer_count)
    zonal_pad = jnp.concatenate([west, tracers, east], axis=1)
    left_x, right_x = stencil(zonal_pad, 1, lon_cols + 1, 1)
    zonal_flux = upwind(zonal_rep, left_x, right_x)
    merid_pad = jnp.concatenate([south, tracers, north], axis=2)
    left_y, right_y = stencil(merid_pad, 2, lat_rows + 1, tracer_count)
    merid_flux = upwind(merid_rep, left_y, right_y)
    metric = jnp.repeat(1.0 / jnp.maximum(row_cosine, COS_FLOOR), tracer_count)
    change = COURANT * (zonal_flux[:, 1:] - zonal_flux[:, :-1]) + COURANT * (
        merid_flux[:, :, tracer_count:] - merid_flux[:, :, :-tracer_count]
    )
    advected = tracers - metric[None, None, :] * change
    return (advected, smoothed)


def solution(mesh):
    placed = (P(None, "lon", "lat"), P(None, None, "lat", "lon"))
    return jax.shard_map(
        local,
        mesh=mesh,
        in_specs=placed,
        out_specs=(P(None, "lon", "lat"), P(None, None, "lat", "lon")),
        check_vma=False,
    )
```

```python
import functools
import math

import jax
import numpy as np
import jax.numpy as jnp
from jax import lax
from jax.experimental import pallas as pl
from jax.experimental.pallas import tpu as pltpu
from jax.sharding import PartitionSpec as P

MESH = pl.DeviceIdType.MESH

COURANT = 0.3
COS_FLOOR = 0.5
EXACT_MODE = lax.Precision.HIGHEST


def extended(array, sides, width, wrap):
    for axis, dim in sides:
        devices, length = (lax.axis_size(axis), array.shape[dim])
        up = [(i, (i + 1) % devices) for i in range(devices if wrap else devices - 1)]
        down = [(j, i) for i, j in up]
        last = lax.slice_in_dim(array, length - width, length, axis=dim)
        first = lax.slice_in_dim(array, 0, width, axis=dim)
        before = lax.ppermute(last, axis, up)
        after = lax.ppermute(first, axis, down)
        array = jnp.concatenate([before, array, after], axis=dim)
    return array


def damping(row_cosine, wavenumber, lon_total):
    sine = jnp.sin(wavenumber.astype(jnp.float32) * (math.pi / lon_total))
    divisor = jnp.where(wavenumber == 0, 1.0, sine * sine)
    scaled = (row_cosine / COS_FLOOR) ** 2
    scaled = scaled.reshape(scaled.shape + (1,) * wavenumber.ndim)
    return jnp.where(wavenumber == 0, 1.0, jnp.minimum(1.0, scaled / divisor))


def face_values(padded, axis, cells, stride):

    def offset_cells(offset):
        return lax.slice_in_dim(padded, offset * stride, (offset + cells + 1) * stride, axis=axis)

    left = (
        2.0 * offset_cells(0)
        - 13.0 * offset_cells(1)
        + 47.0 * offset_cells(2)
        + 27.0 * offset_cells(3)
        - 3.0 * offset_cells(4)
    ) / 60.0
    right = (
        2.0 * offset_cells(5)
        - 13.0 * offset_cells(4)
        + 47.0 * offset_cells(3)
        + 27.0 * offset_cells(2)
        - 3.0 * offset_cells(1)
    ) / 60.0
    return (left, right)


def upwind(speed, left, right):
    return jnp.maximum(speed, 0.0) * left + jnp.minimum(speed, 0.0) * right


def filter_kernel(n, rows, winds_ref, scaled_ref, kc_ref, ks_ref, tc_ref, ts_ref, c_ref, s_ref,
                  divisor_ref, zero_ref, widen_ref, prev_ref, next_ref, pairs_ref, fm_ref, fs_ref, fn_ref,
                  tracers_ref,
                  smooth_ref, zonal_ref, merid_ref, west_ref, east_ref, south_out, north_out,
                  out_ref, south_ref, north_ref, vsouth_ref, vnorth_ref,
                  gathered, restored, send_a, recv_a, send_b, recv_b, halo_send, halo_recv, local_sem):
    me = lax.axis_index("lon")
    band = lax.axis_index("lat")
    bands = lax.axis_size("lat")
    up, down = lax.rem(band + 1, bands), lax.rem(band + bands - 1, bands)
    east_peer, west_peer = lax.rem(me + 1, n), lax.rem(me + n - 1, n)
    barrier = pltpu.get_barrier_semaphore()
    for k in range(1, n):
        peer = lax.rem(me + k, n)
        pl.semaphore_signal(barrier, inc=1, device_id=(band, peer), device_id_type=MESH)
    for other in (up, down):
        pl.semaphore_signal(barrier, inc=1, device_id=(other, me), device_id_type=MESH)
    pl.semaphore_wait(barrier, n + 1)

    cols, merged = tracers_ref.shape[1], tracers_ref.shape[2]
    lane_depth = south_ref.shape[2]
    flat_rows = out_ref.shape[0]
    level_rows = flat_rows // 4
    halo_plan = [
        (tracers_ref.at[:, pl.ds(cols - west_ref.shape[1], west_ref.shape[1]), :], west_ref, (band, east_peer)),
        (tracers_ref.at[:, pl.ds(0, east_ref.shape[1]), :], east_ref, (band, west_peer)),
        (tracers_ref.at[:, :, pl.ds(merged - lane_depth, lane_depth)], south_ref, (up, me)),
        (tracers_ref.at[:, :, pl.ds(0, lane_depth)], north_ref, (down, me)),
    ]
    for level in range(2):
        first = 2 * level_rows + level * level_rows
        halo_plan.append(
            (out_ref.at[pl.ds(first + level_rows - 1, 1)], vsouth_ref.at[pl.ds(level, 1)], (up, me))
        )
    for level in range(2):
        first = 2 * level_rows + level * level_rows
        halo_plan.append((out_ref.at[pl.ds(first, 1)], vnorth_ref.at[pl.ds(level, 1)], (down, me)))
    edge_rows = [2 * level_rows + k for k in (0, level_rows - 1, level_rows, 2 * level_rows - 1)]

    def halo_copy(index):
        source, target, device = halo_plan[index]
        return pltpu.make_async_remote_copy(
            src_ref=source,
            dst_ref=target,
            send_sem=halo_send.at[index],
            recv_sem=halo_recv.at[index],
            device_id=device,
            device_id_type=MESH,
        )

    def block(ref, index):
        return ref.at[pl.ds(pl.multiple_of(index * rows, rows), rows)]

    def swap(source, target, send_sem, recv_sem, slot):
        sends = []
        for k in range(1, n):
            peer = lax.rem(me + k, n)
            copy = pltpu.make_async_remote_copy(
                src_ref=block(source, peer),
                dst_ref=block(target, me),
                send_sem=send_sem.at[peer],
                recv_sem=recv_sem.at[me],
                device_id=(band, peer),
                device_id_type=MESH,
            )
            copy.start()
            sends.append(copy)
        own = pltpu.make_async_copy(block(source, me), block(target, me), local_sem.at[slot])
        own.start()
        return sends, own

    def settle(source, target, send_sem, recv_sem, sends, own):
        own.wait()
        for k in range(1, n):
            origin = lax.rem(me + n - k, n)
            pltpu.make_async_remote_copy(
                src_ref=block(source, origin),
                dst_ref=block(target, origin),
                send_sem=send_sem.at[origin],
                recv_sem=recv_sem.at[origin],
                device_id=(band, origin),
                device_id_type=MESH,
            ).wait_recv()
        for copy in sends:
            copy.wait_send()

    sends, own = swap(winds_ref, gathered, send_a, recv_a, 0)
    tracer_halos = [halo_copy(i) for i in range(4)]
    for copy in tracer_halos:
        copy.start()
    settle(winds_ref, gathered, send_a, recv_a, sends, own)

    def mm(a, b):
        return jnp.dot(a, b, precision=EXACT_MODE, preferred_element_type=jnp.float32)

    x = gathered[...]
    half = x.shape[0]
    tc, ts = tc_ref[...], ts_ref[...]
    stacked = mm(kc_ref[...], x)
    re, im = stacked[:half], -stacked[half:]
    shifted_re = re * tc + im * ts
    shifted_im = im * tc - re * ts
    stacked = jnp.concatenate([shifted_re, shifted_im], axis=0)
    with_cos = mm(stacked, c_ref[...])
    with_sin = mm(stacked, s_ref[...])
    modes_re = with_cos[:half] + with_sin[half:]
    modes_im = with_cos[half:] - with_sin[:half]
    factor = jnp.where(
        zero_ref[...] > 0.0, 1.0, jnp.minimum(1.0, scaled_ref[...] / divisor_ref[...])
    )
    stacked = jnp.concatenate([modes_re * factor, modes_im * factor], axis=0)
    with_cos = mm(stacked, widen_ref[...])
    with_sin = mm(stacked, prev_ref[...])
    back_re = with_cos[:half] - with_sin[half:]
    back_im = with_cos[half:] + with_sin[:half]
    tcw, tsw = next_ref[0], next_ref[1]
    out_re = back_re * tcw - back_im * tsw
    out_im = back_im * tcw + back_re * tsw
    result = mm(ks_ref[...], jnp.concatenate([out_re, out_im], axis=0)) / (n * x.shape[1])
    columns = x.shape[1]
    lane = lax.broadcasted_iota(jnp.int32, result.shape, 1)
    before = jnp.sum(
        jnp.where(lane == columns - 1, jnp.roll(result, rows, axis=0), 0.0), axis=1, keepdims=True
    )
    after = jnp.sum(jnp.where(lane == 0, jnp.roll(result, -rows, axis=0), 0.0), axis=1, keepdims=True)
    restored[...] = jnp.where(lane == columns, before, jnp.where(lane == columns + 1, after, result))
    sends, own = swap(restored, out_ref, send_b, recv_b, 1)
    own.wait()
    holders = sorted({row // rows for row in edge_rows})

    def arrival(origin):
        return pltpu.make_async_remote_copy(
            src_ref=block(restored, origin),
            dst_ref=block(out_ref, origin),
            send_sem=send_b.at[origin],
            recv_sem=recv_b.at[origin],
            device_id=(band, origin),
            device_id_type=MESH,
        )

    for holder in holders:

        @pl.when(me != holder)
        def _():
            arrival(holder).wait_recv()

    wind_halos = [halo_copy(i) for i in range(4, 8)]
    for copy in wind_halos:
        copy.start()
    for k in range(1, n):
        origin = lax.rem(me + n - k, n)
        pending = origin >= 0
        for holder in holders:
            pending = jnp.logical_and(pending, origin != holder)

        @pl.when(pending)
        def _():
            arrival(origin).wait_recv()

    for copy in sends:
        copy.wait_send()
    smooth_ref[...] = out_ref[:, : smooth_ref.shape[1]]
    for copy in tracer_halos + wind_halos:
        copy.wait_recv()
    for copy in tracer_halos + wind_halos:
        copy.wait_send()

    keep_south = jnp.where(band > 0, 1.0, 0.0)
    keep_north = jnp.where(band < bands - 1, 1.0, 0.0)
    width = south_out.shape[2]
    south = pltpu.roll(south_ref[...], width, 2)
    south_out[...] = south[..., :width] * keep_south
    north_out[...] = north_ref[..., :width] * keep_north
    band_rows = level_rows
    for level in range(2):
        east_rows = out_ref[pl.ds(level * band_rows, band_rows), :]
        zonal_ref[level] = mm(east_rows, pairs_ref[...])
        first = 2 * level_rows + level * level_rows
        north_rows = out_ref[pl.ds(first, band_rows), :]
        merid = (
            mm(fm_ref[...], north_rows)
            + fs_ref[...] * (vsouth_ref[pl.ds(level, 1), :] * keep_south)
            + fn_ref[...] * (vnorth_ref[pl.ds(level, 1), :] * keep_north)
        )
        merid_ref[level] = merid[:, : merid_ref.shape[2]]


def spectral_tables(n, rows, columns):
    lon_total = n * columns
    blocks = np.arange(n)
    phase = 2.0 * np.pi * (np.outer(blocks, blocks) % n) / n
    eye = np.eye(rows)
    column_ids = np.arange(columns)
    twist = 2.0 * np.pi * (np.outer(blocks, column_ids) % lon_total) / lon_total
    turn = 2.0 * np.pi * (np.outer(column_ids, column_ids) % columns) / columns
    wavenumber = blocks[:, None] + n * column_ids[None, :]
    sine = np.sin(wavenumber.astype(np.float32) * np.float32(math.pi / lon_total))
    divisor = np.where(wavenumber == 0, np.float32(1.0), sine * sine).astype(np.float32)
    zero_mode = (wavenumber == 0).astype(np.float32)
    widen = np.eye(columns, columns + 2)
    kron_cos, kron_sin = np.kron(np.cos(phase), eye), np.kron(np.sin(phase), eye)
    twist_wide = np.stack(
        [np.repeat(np.cos(twist), rows, axis=0) @ widen, np.repeat(np.sin(twist), rows, axis=0) @ widen]
    )
    tables = (
        np.concatenate([kron_cos, kron_sin], axis=0),
        np.concatenate([kron_cos, -kron_sin], axis=1),
        np.repeat(np.cos(twist), rows, axis=0),
        np.repeat(np.sin(twist), rows, axis=0),
        np.cos(turn),
        np.sin(turn),
        np.repeat(divisor, rows, axis=0),
        np.repeat(zero_mode, rows, axis=0),
        np.cos(turn) @ widen,
        np.sin(turn) @ widen,
        twist_wide,
    )
    return [jnp.asarray(t.astype(np.float32)) for t in tables]


def exchange_all(flat_winds, row_cosine, face_cosine, tracers):
    flat_rows, columns = flat_winds.shape
    levels, lon_cols, merged = tracers.shape
    n = lax.axis_size("lon")
    lon_index = lax.axis_index("lon")
    rows = flat_rows // n
    lat_rows = row_cosine.shape[0]
    tracer_count = merged // lat_rows
    own_cosine = lax.dynamic_slice_in_dim(
        jnp.tile(row_cosine, flat_rows // lat_rows), lon_index * rows, rows, 0
    )
    scaled = (own_cosine / COS_FLOOR) ** 2
    scaled = jnp.tile(scaled, n).reshape(n * rows, 1)
    half_cosine = 0.5 * face_cosine
    pair_rows = np.zeros((columns + 2, columns + 1), np.float32)
    for face in range(columns + 1):
        pair_rows[columns if face == 0 else face - 1, face] = 0.5
        pair_rows[columns + 1 if face == columns else face, face] = 0.5
    faces = jnp.arange(lat_rows + 1)[:, None]
    cells = jnp.arange(lat_rows)[None, :]
    face_weights = jnp.where((cells == faces - 1) | (cells == faces), half_cosine[:, None], 0.0)
    south_weight = jnp.where(faces == 0, half_cosine[:, None], 0.0)
    north_weight = jnp.where(faces == lat_rows, half_cosine[:, None], 0.0)
    vmem = pl.BlockSpec(memory_space=pltpu.VMEM)
    wide_lanes = -(-3 * tracer_count // 128) * 128
    west_cols = lon_cols - (lon_cols - 3) // 8 * 8
    shapes = [
        (flat_rows, columns),
        (levels, lat_rows, columns + 1),
        (levels, lat_rows + 1, columns),
        (levels, west_cols, merged),
        (levels, 8, merged),
        (levels, lon_cols, 3 * tracer_count),
        (levels, lon_cols, 3 * tracer_count),
    ]
    return pl.pallas_call(
        functools.partial(filter_kernel, n, rows),
        out_shape=[jax.ShapeDtypeStruct(shape, jnp.float32) for shape in shapes],
        in_specs=[vmem] * 17 + [pl.BlockSpec(memory_space=pl.ANY)],
        out_specs=[vmem] * len(shapes),
        scratch_shapes=[
            pltpu.VMEM((flat_rows, columns + 2), jnp.float32),
            pltpu.VMEM((levels, lon_cols, wide_lanes), jnp.float32),
            pltpu.VMEM((levels, lon_cols, wide_lanes), jnp.float32),
            pltpu.VMEM((levels, columns + 2), jnp.float32),
            pltpu.VMEM((levels, columns + 2), jnp.float32),
            pltpu.VMEM((flat_rows, columns), jnp.float32),
            pltpu.VMEM((flat_rows, columns + 2), jnp.float32),
            pltpu.SemaphoreType.DMA((n,)),
            pltpu.SemaphoreType.DMA((n,)),
            pltpu.SemaphoreType.DMA((n,)),
            pltpu.SemaphoreType.DMA((n,)),
            pltpu.SemaphoreType.DMA((8,)),
            pltpu.SemaphoreType.DMA((8,)),
            pltpu.SemaphoreType.DMA((2,)),
        ],
        compiler_params=pltpu.CompilerParams(collective_id=0, has_side_effects=True),
    )(
        flat_winds,
        scaled,
        *spectral_tables(n, rows, columns),
        jnp.asarray(pair_rows),
        face_weights,
        south_weight,
        north_weight,
        tracers,
    )


def stencil(padded, dim, faces, stride):

    def offset_cells(offset):
        return lax.slice_in_dim(padded, offset * stride, (offset + faces) * stride, axis=dim)

    left = (
        2.0 * offset_cells(0)
        - 13.0 * offset_cells(1)
        + 47.0 * offset_cells(2)
        + 27.0 * offset_cells(3)
        - 3.0 * offset_cells(4)
    ) / 60.0
    right = (
        2.0 * offset_cells(5)
        - 13.0 * offset_cells(4)
        + 47.0 * offset_cells(3)
        + 27.0 * offset_cells(2)
        - 3.0 * offset_cells(1)
    ) / 60.0
    return left, right


def spread(values, rows, tracer_count):
    lanes = jnp.arange(rows * tracer_count, dtype=jnp.int32) // tracer_count
    pick = (jnp.arange(rows, dtype=jnp.int32)[:, None] == lanes[None, :]).astype(jnp.float32)
    return jnp.einsum("ljc,jm->lcm", values, pick, precision=EXACT_MODE)


def local(tracers, wind_field):
    levels, lon_cols, merged = tracers.shape
    lat_rows = wind_field.shape[2]
    tracer_count = merged // lat_rows
    lat_total = lat_rows * lax.axis_size("lat")
    band = lax.axis_index("lat")
    first_row = band * lat_rows
    row_ids = first_row + jnp.arange(lat_rows, dtype=jnp.int32)
    row_cosine = jnp.cos(
        (row_ids.astype(jnp.float32) + 0.5) * (math.pi / lat_total) - 0.5 * math.pi
    )
    flat_winds = wind_field.reshape(2 * levels * lat_rows, lon_cols)
    face_ids = first_row + jnp.arange(lat_rows + 1, dtype=jnp.int32)
    face_cosine = jnp.cos(face_ids.astype(jnp.float32) * (math.pi / lat_total) - 0.5 * math.pi)
    face_cosine = jnp.where((face_ids == 0) | (face_ids == lat_total), 0.0, face_cosine)
    smoothed, zonal_speed, merid_speed, west, east, south, north = exchange_all(
        flat_winds, row_cosine, face_cosine, tracers
    )
    west = west[:, west.shape[1] - 3 :]
    east = east[:, :3]
    smoothed = smoothed.reshape(2, levels, lat_rows, lon_cols)
    zonal_rep = spread(zonal_speed, lat_rows, tracer_count)
    merid_rep = spread(merid_speed, lat_rows + 1, tracer_count)
    zonal_pad = jnp.concatenate([west, tracers, east], axis=1)
    left_x, right_x = stencil(zonal_pad, 1, lon_cols + 1, 1)
    zonal_flux = upwind(zonal_rep, left_x, right_x)
    merid_pad = jnp.concatenate([south, tracers, north], axis=2)
    left_y, right_y = stencil(merid_pad, 2, lat_rows + 1, tracer_count)
    merid_flux = upwind(merid_rep, left_y, right_y)
    metric = jnp.repeat(1.0 / jnp.maximum(row_cosine, COS_FLOOR), tracer_count)
    change = COURANT * (zonal_flux[:, 1:] - zonal_flux[:, :-1]) + COURANT * (
        merid_flux[:, :, tracer_count:] - merid_flux[:, :, :-tracer_count]
    )
    advected = tracers - metric[None, None, :] * change
    return (advected, smoothed)


def solution(mesh):
    placed = (P(None, "lon", "lat"), P(None, None, "lat", "lon"))
    return jax.shard_map(
        local,
        mesh=mesh,
        in_specs=placed,
        out_specs=(P(None, "lon", "lat"), P(None, None, "lat", "lon")),
        check_vma=False,
    )
```

```python
import functools
import math

import jax
import numpy as np
import jax.numpy as jnp
from jax import lax
from jax.experimental import pallas as pl
from jax.experimental.pallas import tpu as pltpu
from jax.sharding import PartitionSpec as P

MESH = pl.DeviceIdType.MESH

COURANT = 0.3
COS_FLOOR = 0.5
EXACT_MODE = lax.Precision.HIGHEST


def extended(array, sides, width, wrap):
    for axis, dim in sides:
        devices, length = (lax.axis_size(axis), array.shape[dim])
        up = [(i, (i + 1) % devices) for i in range(devices if wrap else devices - 1)]
        down = [(j, i) for i, j in up]
        last = lax.slice_in_dim(array, length - width, length, axis=dim)
        first = lax.slice_in_dim(array, 0, width, axis=dim)
        before = lax.ppermute(last, axis, up)
        after = lax.ppermute(first, axis, down)
        array = jnp.concatenate([before, array, after], axis=dim)
    return array


def damping(row_cosine, wavenumber, lon_total):
    sine = jnp.sin(wavenumber.astype(jnp.float32) * (math.pi / lon_total))
    divisor = jnp.where(wavenumber == 0, 1.0, sine * sine)
    scaled = (row_cosine / COS_FLOOR) ** 2
    scaled = scaled.reshape(scaled.shape + (1,) * wavenumber.ndim)
    return jnp.where(wavenumber == 0, 1.0, jnp.minimum(1.0, scaled / divisor))


def face_values(padded, axis, cells, stride):

    def offset_cells(offset):
        return lax.slice_in_dim(padded, offset * stride, (offset + cells + 1) * stride, axis=axis)

    left = (
        2.0 * offset_cells(0)
        - 13.0 * offset_cells(1)
        + 47.0 * offset_cells(2)
        + 27.0 * offset_cells(3)
        - 3.0 * offset_cells(4)
    ) / 60.0
    right = (
        2.0 * offset_cells(5)
        - 13.0 * offset_cells(4)
        + 47.0 * offset_cells(3)
        + 27.0 * offset_cells(2)
        - 3.0 * offset_cells(1)
    ) / 60.0
    return (left, right)


def upwind(speed, left, right):
    return jnp.maximum(speed, 0.0) * left + jnp.minimum(speed, 0.0) * right


def filter_kernel(n, rows, winds_ref, scales_ref, kc_ref, ks_ref, tc_ref, ts_ref, c_ref, s_ref,
                  divisor_ref, zero_ref, widen_ref, prev_ref, next_ref, pairs_ref, halves_ref,
                  tracers_ref,
                  smooth_ref, zonal_ref, merid_ref, west_ref, east_ref, south_out, north_out,
                  out_ref, south_ref, north_ref, vsouth_ref, vnorth_ref,
                  gathered, restored, send_a, recv_a, send_b, recv_b, halo_send, halo_recv, local_sem):
    me = lax.axis_index("lon")
    band = lax.axis_index("lat")
    bands = lax.axis_size("lat")
    up, down = lax.rem(band + 1, bands), lax.rem(band + bands - 1, bands)
    east_peer, west_peer = lax.rem(me + 1, n), lax.rem(me + n - 1, n)
    barrier = pltpu.get_barrier_semaphore()
    for k in range(1, n):
        peer = lax.rem(me + k, n)
        pl.semaphore_signal(barrier, inc=1, device_id=(band, peer), device_id_type=MESH)
    for other in (up, down):
        pl.semaphore_signal(barrier, inc=1, device_id=(other, me), device_id_type=MESH)
    pl.semaphore_wait(barrier, n + 1)

    cols, merged = tracers_ref.shape[1], tracers_ref.shape[2]
    lane_depth = south_ref.shape[2]
    flat_rows = out_ref.shape[0]
    level_rows = flat_rows // 4
    halo_plan = [
        (tracers_ref.at[:, pl.ds(cols - west_ref.shape[1], west_ref.shape[1]), :], west_ref, (band, east_peer)),
        (tracers_ref.at[:, pl.ds(0, east_ref.shape[1]), :], east_ref, (band, west_peer)),
        (tracers_ref.at[:, :, pl.ds(merged - lane_depth, lane_depth)], south_ref, (up, me)),
        (tracers_ref.at[:, :, pl.ds(0, lane_depth)], north_ref, (down, me)),
    ]
    for level in range(2):
        first = 2 * level_rows + level * level_rows
        halo_plan.append(
            (out_ref.at[pl.ds(first + level_rows - 1, 1)], vsouth_ref.at[pl.ds(level, 1)], (up, me))
        )
    for level in range(2):
        first = 2 * level_rows + level * level_rows
        halo_plan.append((out_ref.at[pl.ds(first, 1)], vnorth_ref.at[pl.ds(level, 1)], (down, me)))
    edge_rows = [2 * level_rows + k for k in (0, level_rows - 1, level_rows, 2 * level_rows - 1)]

    def halo_copy(index):
        source, target, device = halo_plan[index]
        return pltpu.make_async_remote_copy(
            src_ref=source,
            dst_ref=target,
            send_sem=halo_send.at[index],
            recv_sem=halo_recv.at[index],
            device_id=device,
            device_id_type=MESH,
        )

    def block(ref, index):
        return ref.at[pl.ds(pl.multiple_of(index * rows, rows), rows)]

    def swap(source, target, send_sem, recv_sem, slot):
        sends = []
        for k in range(1, n):
            peer = lax.rem(me + k, n)
            copy = pltpu.make_async_remote_copy(
                src_ref=block(source, peer),
                dst_ref=block(target, me),
                send_sem=send_sem.at[peer],
                recv_sem=recv_sem.at[me],
                device_id=(band, peer),
                device_id_type=MESH,
            )
            copy.start()
            sends.append(copy)
        own = pltpu.make_async_copy(block(source, me), block(target, me), local_sem.at[slot])
        own.start()
        return sends, own

    def settle(source, target, send_sem, recv_sem, sends, own):
        own.wait()
        for k in range(1, n):
            origin = lax.rem(me + n - k, n)
            pltpu.make_async_remote_copy(
                src_ref=block(source, origin),
                dst_ref=block(target, origin),
                send_sem=send_sem.at[origin],
                recv_sem=recv_sem.at[origin],
                device_id=(band, origin),
                device_id_type=MESH,
            ).wait_recv()
        for copy in sends:
            copy.wait_send()

    sends, own = swap(winds_ref, gathered, send_a, recv_a, 0)
    tracer_halos = [halo_copy(i) for i in range(4)]
    for copy in tracer_halos:
        copy.start()
    settle(winds_ref, gathered, send_a, recv_a, sends, own)

    def mm(a, b):
        return jnp.dot(a, b, precision=EXACT_MODE, preferred_element_type=jnp.float32)

    x = gathered[...]
    half = x.shape[0]
    tc, ts = tc_ref[...], ts_ref[...]
    stacked = mm(kc_ref[...], x)
    re, im = stacked[:half], -stacked[half:]
    shifted_re = re * tc + im * ts
    shifted_im = im * tc - re * ts
    stacked = jnp.concatenate([shifted_re, shifted_im], axis=0)
    with_cos = mm(stacked, c_ref[...])
    with_sin = mm(stacked, s_ref[...])
    modes_re = with_cos[:half] + with_sin[half:]
    modes_im = with_cos[half:] - with_sin[:half]
    lane_rows = lax.broadcasted_iota(jnp.int32, (n * rows, 1), 0) % rows
    base = (band * n + me) * rows
    scaled = jnp.zeros((n * rows, 1), jnp.float32)
    for r in range(rows):
        scaled = jnp.where(lane_rows == r, scales_ref[base + r], scaled)
    factor = jnp.where(zero_ref[...] > 0.0, 1.0, jnp.minimum(1.0, scaled / divisor_ref[...]))
    stacked = jnp.concatenate([modes_re * factor, modes_im * factor], axis=0)
    with_cos = mm(stacked, widen_ref[...])
    with_sin = mm(stacked, prev_ref[...])
    back_re = with_cos[:half] - with_sin[half:]
    back_im = with_cos[half:] + with_sin[:half]
    tcw, tsw = next_ref[0], next_ref[1]
    out_re = back_re * tcw - back_im * tsw
    out_im = back_im * tcw + back_re * tsw
    result = mm(ks_ref[...], jnp.concatenate([out_re, out_im], axis=0)) / (n * x.shape[1])
    columns = x.shape[1]
    lane = lax.broadcasted_iota(jnp.int32, result.shape, 1)
    before = jnp.sum(
        jnp.where(lane == columns - 1, jnp.roll(result, rows, axis=0), 0.0), axis=1, keepdims=True
    )
    after = jnp.sum(jnp.where(lane == 0, jnp.roll(result, -rows, axis=0), 0.0), axis=1, keepdims=True)
    restored[...] = jnp.where(lane == columns, before, jnp.where(lane == columns + 1, after, result))
    sends, own = swap(restored, out_ref, send_b, recv_b, 1)
    own.wait()
    holders = sorted({row // rows for row in edge_rows})

    def arrival(origin):
        return pltpu.make_async_remote_copy(
            src_ref=block(restored, origin),
            dst_ref=block(out_ref, origin),
            send_sem=send_b.at[origin],
            recv_sem=recv_b.at[origin],
            device_id=(band, origin),
            device_id_type=MESH,
        )

    for holder in holders:

        @pl.when(me != holder)
        def _():
            arrival(holder).wait_recv()

    wind_halos = [halo_copy(i) for i in range(4, 8)]
    for copy in wind_halos:
        copy.start()
    for k in range(1, n):
        origin = lax.rem(me + n - k, n)
        pending = origin >= 0
        for holder in holders:
            pending = jnp.logical_and(pending, origin != holder)

        @pl.when(pending)
        def _():
            arrival(origin).wait_recv()

    for copy in sends:
        copy.wait_send()
    smooth_ref[...] = out_ref[:, : smooth_ref.shape[1]]
    for copy in tracer_halos + wind_halos:
        copy.wait_recv()
    for copy in tracer_halos + wind_halos:
        copy.wait_send()

    keep_south = jnp.where(band > 0, 1.0, 0.0)
    keep_north = jnp.where(band < bands - 1, 1.0, 0.0)
    width = south_out.shape[2]
    south = pltpu.roll(south_ref[...], width, 2)
    south_out[...] = south[..., :width] * keep_south
    north_out[...] = north_ref[..., :width] * keep_north
    band_rows = level_rows
    face_ids = lax.broadcasted_iota(jnp.int32, (band_rows + 1, 1), 0)
    half = jnp.zeros((band_rows + 1, 1), jnp.float32)
    for face in range(band_rows + 1):
        half = jnp.where(face_ids == face, halves_ref[band * (band_rows + 1) + face], half)
    faces = lax.broadcasted_iota(jnp.int32, (band_rows + 1, band_rows), 0)
    cells = lax.broadcasted_iota(jnp.int32, (band_rows + 1, band_rows), 1)
    face_weights = jnp.where((cells == faces - 1) | (cells == faces), half, 0.0)
    south_weight = jnp.where(face_ids == 0, half, 0.0)
    north_weight = jnp.where(face_ids == band_rows, half, 0.0)
    for level in range(2):
        east_rows = out_ref[pl.ds(level * band_rows, band_rows), :]
        zonal_ref[level] = mm(east_rows, pairs_ref[...])
        first = 2 * level_rows + level * level_rows
        north_rows = out_ref[pl.ds(first, band_rows), :]
        merid = (
            mm(face_weights, north_rows)
            + south_weight * (vsouth_ref[pl.ds(level, 1), :] * keep_south)
            + north_weight * (vnorth_ref[pl.ds(level, 1), :] * keep_north)
        )
        merid_ref[level] = merid[:, : merid_ref.shape[2]]


def spectral_tables(n, rows, columns):
    lon_total = n * columns
    blocks = np.arange(n)
    phase = 2.0 * np.pi * (np.outer(blocks, blocks) % n) / n
    eye = np.eye(rows)
    column_ids = np.arange(columns)
    twist = 2.0 * np.pi * (np.outer(blocks, column_ids) % lon_total) / lon_total
    turn = 2.0 * np.pi * (np.outer(column_ids, column_ids) % columns) / columns
    wavenumber = blocks[:, None] + n * column_ids[None, :]
    sine = np.sin(wavenumber.astype(np.float32) * np.float32(math.pi / lon_total))
    divisor = np.where(wavenumber == 0, np.float32(1.0), sine * sine).astype(np.float32)
    zero_mode = (wavenumber == 0).astype(np.float32)
    widen = np.eye(columns, columns + 2)
    kron_cos, kron_sin = np.kron(np.cos(phase), eye), np.kron(np.sin(phase), eye)
    twist_wide = np.stack(
        [np.repeat(np.cos(twist), rows, axis=0) @ widen, np.repeat(np.sin(twist), rows, axis=0) @ widen]
    )
    tables = (
        np.concatenate([kron_cos, kron_sin], axis=0),
        np.concatenate([kron_cos, -kron_sin], axis=1),
        np.repeat(np.cos(twist), rows, axis=0),
        np.repeat(np.sin(twist), rows, axis=0),
        np.cos(turn),
        np.sin(turn),
        np.repeat(divisor, rows, axis=0),
        np.repeat(zero_mode, rows, axis=0),
        np.cos(turn) @ widen,
        np.sin(turn) @ widen,
        twist_wide,
    )
    return [jnp.asarray(t.astype(np.float32)) for t in tables]


def position_tables(n, rows, bands, lat_rows, flat_rows):
    lat_total = bands * lat_rows
    cells = np.arange(lat_total, dtype=np.float32)
    row_cosine = np.cos(
        (cells + np.float32(0.5)) * np.float32(math.pi / lat_total) - np.float32(0.5 * math.pi)
    ).astype(np.float32)
    scaled = ((row_cosine / np.float32(COS_FLOOR)) ** 2).astype(np.float32)
    own_rows = (np.arange(n)[:, None] * rows + np.arange(rows)[None, :]) % lat_rows
    scales = scaled[np.arange(bands)[:, None, None] * lat_rows + own_rows[None]]
    face_ids = np.arange(bands)[:, None] * lat_rows + np.arange(lat_rows + 1)[None, :]
    face_cosine = np.cos(
        face_ids.astype(np.float32) * np.float32(math.pi / lat_total) - np.float32(0.5 * math.pi)
    ).astype(np.float32)
    face_cosine = np.where((face_ids == 0) | (face_ids == lat_total), 0.0, face_cosine)
    halves = (np.float32(0.5) * face_cosine).astype(np.float32)
    return jnp.asarray(scales.reshape(-1)), jnp.asarray(halves.reshape(-1))


def exchange_all(flat_winds, lat_rows, tracers):
    flat_rows, columns = flat_winds.shape
    levels, lon_cols, merged = tracers.shape
    n = lax.axis_size("lon")
    rows = flat_rows // n
    tracer_count = merged // lat_rows
    scales, halves = position_tables(n, rows, lax.axis_size("lat"), lat_rows, flat_rows)
    pair_rows = np.zeros((columns + 2, columns + 1), np.float32)
    for face in range(columns + 1):
        pair_rows[columns if face == 0 else face - 1, face] = 0.5
        pair_rows[columns + 1 if face == columns else face, face] = 0.5
    vmem = pl.BlockSpec(memory_space=pltpu.VMEM)
    smem = pl.BlockSpec(memory_space=pltpu.SMEM)
    wide_lanes = -(-3 * tracer_count // 128) * 128
    west_cols = lon_cols - (lon_cols - 3) // 8 * 8
    shapes = [
        (flat_rows, columns),
        (levels, lat_rows, columns + 1),
        (levels, lat_rows + 1, columns),
        (levels, west_cols, merged),
        (levels, 8, merged),
        (levels, lon_cols, 3 * tracer_count),
        (levels, lon_cols, 3 * tracer_count),
    ]
    return pl.pallas_call(
        functools.partial(filter_kernel, n, rows),
        out_shape=[jax.ShapeDtypeStruct(shape, jnp.float32) for shape in shapes],
        in_specs=[vmem, smem]
        + [vmem] * 12
        + [smem, pl.BlockSpec(memory_space=pl.ANY)],
        out_specs=[vmem] * len(shapes),
        scratch_shapes=[
            pltpu.VMEM((flat_rows, columns + 2), jnp.float32),
            pltpu.VMEM((levels, lon_cols, wide_lanes), jnp.float32),
            pltpu.VMEM((levels, lon_cols, wide_lanes), jnp.float32),
            pltpu.VMEM((levels, columns + 2), jnp.float32),
            pltpu.VMEM((levels, columns + 2), jnp.float32),
            pltpu.VMEM((flat_rows, columns), jnp.float32),
            pltpu.VMEM((flat_rows, columns + 2), jnp.float32),
            pltpu.SemaphoreType.DMA((n,)),
            pltpu.SemaphoreType.DMA((n,)),
            pltpu.SemaphoreType.DMA((n,)),
            pltpu.SemaphoreType.DMA((n,)),
            pltpu.SemaphoreType.DMA((8,)),
            pltpu.SemaphoreType.DMA((8,)),
            pltpu.SemaphoreType.DMA((2,)),
        ],
        compiler_params=pltpu.CompilerParams(collective_id=0, has_side_effects=True),
    )(
        flat_winds,
        scales,
        *spectral_tables(n, rows, columns),
        jnp.asarray(pair_rows),
        halves,
        tracers,
    )


def stencil(padded, dim, faces, stride):

    def offset_cells(offset):
        return lax.slice_in_dim(padded, offset * stride, (offset + faces) * stride, axis=dim)

    left = (
        2.0 * offset_cells(0)
        - 13.0 * offset_cells(1)
        + 47.0 * offset_cells(2)
        + 27.0 * offset_cells(3)
        - 3.0 * offset_cells(4)
    ) / 60.0
    right = (
        2.0 * offset_cells(5)
        - 13.0 * offset_cells(4)
        + 47.0 * offset_cells(3)
        + 27.0 * offset_cells(2)
        - 3.0 * offset_cells(1)
    ) / 60.0
    return left, right


def spread(values, rows, tracer_count):
    lanes = jnp.arange(rows * tracer_count, dtype=jnp.int32) // tracer_count
    pick = (jnp.arange(rows, dtype=jnp.int32)[:, None] == lanes[None, :]).astype(jnp.float32)
    return jnp.einsum("ljc,jm->lcm", values, pick, precision=EXACT_MODE)


def local(tracers, wind_field):
    levels, lon_cols, merged = tracers.shape
    lat_rows = wind_field.shape[2]
    tracer_count = merged // lat_rows
    lat_total = lat_rows * lax.axis_size("lat")
    band = lax.axis_index("lat")
    first_row = band * lat_rows
    row_ids = first_row + jnp.arange(lat_rows, dtype=jnp.int32)
    row_cosine = jnp.cos(
        (row_ids.astype(jnp.float32) + 0.5) * (math.pi / lat_total) - 0.5 * math.pi
    )
    flat_winds = wind_field.reshape(2 * levels * lat_rows, lon_cols)
    smoothed, zonal_speed, merid_speed, west, east, south, north = exchange_all(
        flat_winds, lat_rows, tracers
    )
    west = west[:, west.shape[1] - 3 :]
    east = east[:, :3]
    smoothed = smoothed.reshape(2, levels, lat_rows, lon_cols)
    zonal_rep = spread(zonal_speed, lat_rows, tracer_count)
    merid_rep = spread(merid_speed, lat_rows + 1, tracer_count)
    zonal_pad = jnp.concatenate([west, tracers, east], axis=1)
    left_x, right_x = stencil(zonal_pad, 1, lon_cols + 1, 1)
    zonal_flux = upwind(zonal_rep, left_x, right_x)
    merid_pad = jnp.concatenate([south, tracers, north], axis=2)
    left_y, right_y = stencil(merid_pad, 2, lat_rows + 1, tracer_count)
    merid_flux = upwind(merid_rep, left_y, right_y)
    metric = jnp.repeat(1.0 / jnp.maximum(row_cosine, COS_FLOOR), tracer_count)
    change = COURANT * (zonal_flux[:, 1:] - zonal_flux[:, :-1]) + COURANT * (
        merid_flux[:, :, tracer_count:] - merid_flux[:, :, :-tracer_count]
    )
    advected = tracers - metric[None, None, :] * change
    return (advected, smoothed)


def solution(mesh):
    placed = (P(None, "lon", "lat"), P(None, None, "lat", "lon"))
    return jax.shard_map(
        local,
        mesh=mesh,
        in_specs=placed,
        out_specs=(P(None, "lon", "lat"), P(None, None, "lat", "lon")),
        check_vma=False,
    )
```

```python
import functools
import math

import jax
import numpy as np
import jax.numpy as jnp
from jax import lax
from jax.experimental import pallas as pl
from jax.experimental.pallas import tpu as pltpu
from jax.sharding import PartitionSpec as P

MESH = pl.DeviceIdType.MESH

COURANT = 0.3
COS_FLOOR = 0.5
EXACT_MODE = lax.Precision.HIGHEST


def extended(array, sides, width, wrap):
    for axis, dim in sides:
        devices, length = (lax.axis_size(axis), array.shape[dim])
        up = [(i, (i + 1) % devices) for i in range(devices if wrap else devices - 1)]
        down = [(j, i) for i, j in up]
        last = lax.slice_in_dim(array, length - width, length, axis=dim)
        first = lax.slice_in_dim(array, 0, width, axis=dim)
        before = lax.ppermute(last, axis, up)
        after = lax.ppermute(first, axis, down)
        array = jnp.concatenate([before, array, after], axis=dim)
    return array


def damping(row_cosine, wavenumber, lon_total):
    sine = jnp.sin(wavenumber.astype(jnp.float32) * (math.pi / lon_total))
    divisor = jnp.where(wavenumber == 0, 1.0, sine * sine)
    scaled = (row_cosine / COS_FLOOR) ** 2
    scaled = scaled.reshape(scaled.shape + (1,) * wavenumber.ndim)
    return jnp.where(wavenumber == 0, 1.0, jnp.minimum(1.0, scaled / divisor))


def face_values(padded, axis, cells, stride):

    def offset_cells(offset):
        return lax.slice_in_dim(padded, offset * stride, (offset + cells + 1) * stride, axis=axis)

    left = (
        2.0 * offset_cells(0)
        - 13.0 * offset_cells(1)
        + 47.0 * offset_cells(2)
        + 27.0 * offset_cells(3)
        - 3.0 * offset_cells(4)
    ) / 60.0
    right = (
        2.0 * offset_cells(5)
        - 13.0 * offset_cells(4)
        + 47.0 * offset_cells(3)
        + 27.0 * offset_cells(2)
        - 3.0 * offset_cells(1)
    ) / 60.0
    return (left, right)


def upwind(speed, left, right):
    return jnp.maximum(speed, 0.0) * left + jnp.minimum(speed, 0.0) * right


def filter_kernel(n, rows, winds_ref, scales_ref, kc_ref, ks_ref, tc_ref, ts_ref, c_ref, s_ref,
                  divisor_ref, zero_ref, widen_ref, prev_ref, next_ref, pairs_ref, tracers_ref,
                  smooth_ref, zonal_ref, west_ref, east_ref, south_out, north_out, out_ref,
                  south_ref, north_ref,
                  gathered, restored, send_a, recv_a, send_b, recv_b, halo_send, halo_recv, local_sem):
    me = lax.axis_index("lon")
    band = lax.axis_index("lat")
    bands = lax.axis_size("lat")
    up, down = lax.rem(band + 1, bands), lax.rem(band + bands - 1, bands)
    east_peer, west_peer = lax.rem(me + 1, n), lax.rem(me + n - 1, n)
    barrier = pltpu.get_barrier_semaphore()
    for k in range(1, n):
        peer = lax.rem(me + k, n)
        pl.semaphore_signal(barrier, inc=1, device_id=(band, peer), device_id_type=MESH)
    for other in (up, down):
        pl.semaphore_signal(barrier, inc=1, device_id=(other, me), device_id_type=MESH)
    pl.semaphore_wait(barrier, n + 1)

    cols, merged = tracers_ref.shape[1], tracers_ref.shape[2]
    lane_depth = south_ref.shape[2]
    flat_rows = out_ref.shape[0]
    level_rows = flat_rows // 4
    halo_plan = [
        (tracers_ref.at[:, pl.ds(cols - west_ref.shape[1], west_ref.shape[1]), :], west_ref, (band, east_peer)),
        (tracers_ref.at[:, pl.ds(0, east_ref.shape[1]), :], east_ref, (band, west_peer)),
        (tracers_ref.at[:, :, pl.ds(merged - lane_depth, lane_depth)], south_ref, (up, me)),
        (tracers_ref.at[:, :, pl.ds(0, lane_depth)], north_ref, (down, me)),
    ]

    def halo_copy(index):
        source, target, device = halo_plan[index]
        return pltpu.make_async_remote_copy(
            src_ref=source,
            dst_ref=target,
            send_sem=halo_send.at[index],
            recv_sem=halo_recv.at[index],
            device_id=device,
            device_id_type=MESH,
        )

    def block(ref, index):
        return ref.at[pl.ds(pl.multiple_of(index * rows, rows), rows)]

    def swap(source, target, send_sem, recv_sem, slot):
        sends = []
        for k in range(1, n):
            peer = lax.rem(me + k, n)
            copy = pltpu.make_async_remote_copy(
                src_ref=block(source, peer),
                dst_ref=block(target, me),
                send_sem=send_sem.at[peer],
                recv_sem=recv_sem.at[me],
                device_id=(band, peer),
                device_id_type=MESH,
            )
            copy.start()
            sends.append(copy)
        own = pltpu.make_async_copy(block(source, me), block(target, me), local_sem.at[slot])
        own.start()
        return sends, own

    def settle(source, target, send_sem, recv_sem, sends, own):
        own.wait()
        for k in range(1, n):
            origin = lax.rem(me + n - k, n)
            pltpu.make_async_remote_copy(
                src_ref=block(source, origin),
                dst_ref=block(target, origin),
                send_sem=send_sem.at[origin],
                recv_sem=recv_sem.at[origin],
                device_id=(band, origin),
                device_id_type=MESH,
            ).wait_recv()
        for copy in sends:
            copy.wait_send()

    sends, own = swap(winds_ref, gathered, send_a, recv_a, 0)
    tracer_halos = [halo_copy(i) for i in range(4)]
    for copy in tracer_halos:
        copy.start()
    settle(winds_ref, gathered, send_a, recv_a, sends, own)

    def mm(a, b):
        return jnp.dot(a, b, precision=EXACT_MODE, preferred_element_type=jnp.float32)

    x = gathered[...]
    half = x.shape[0]
    tc, ts = tc_ref[...], ts_ref[...]
    stacked = mm(kc_ref[...], x)
    re, im = stacked[:half], -stacked[half:]
    shifted_re = re * tc + im * ts
    shifted_im = im * tc - re * ts
    stacked = jnp.concatenate([shifted_re, shifted_im], axis=0)
    with_cos = mm(stacked, c_ref[...])
    with_sin = mm(stacked, s_ref[...])
    modes_re = with_cos[:half] + with_sin[half:]
    modes_im = with_cos[half:] - with_sin[:half]
    lane_rows = lax.broadcasted_iota(jnp.int32, (n * rows, 1), 0) % rows
    base = (band * n + me) * rows
    scaled = jnp.zeros((n * rows, 1), jnp.float32)
    for r in range(rows):
        scaled = jnp.where(lane_rows == r, scales_ref[base + r], scaled)
    factor = jnp.where(zero_ref[...] > 0.0, 1.0, jnp.minimum(1.0, scaled / divisor_ref[...]))
    stacked = jnp.concatenate([modes_re * factor, modes_im * factor], axis=0)
    with_cos = mm(stacked, widen_ref[...])
    with_sin = mm(stacked, prev_ref[...])
    back_re = with_cos[:half] - with_sin[half:]
    back_im = with_cos[half:] + with_sin[:half]
    tcw, tsw = next_ref[0], next_ref[1]
    out_re = back_re * tcw - back_im * tsw
    out_im = back_im * tcw + back_re * tsw
    result = mm(ks_ref[...], jnp.concatenate([out_re, out_im], axis=0)) / (n * x.shape[1])
    columns = x.shape[1]
    lane = lax.broadcasted_iota(jnp.int32, result.shape, 1)
    before = jnp.sum(
        jnp.where(lane == columns - 1, jnp.roll(result, rows, axis=0), 0.0), axis=1, keepdims=True
    )
    after = jnp.sum(jnp.where(lane == 0, jnp.roll(result, -rows, axis=0), 0.0), axis=1, keepdims=True)
    restored[...] = jnp.where(lane == columns, before, jnp.where(lane == columns + 1, after, result))
    sends, own = swap(restored, out_ref, send_b, recv_b, 1)
    settle(restored, out_ref, send_b, recv_b, sends, own)
    smooth_ref[...] = out_ref[:, : smooth_ref.shape[1]]
    for copy in tracer_halos:
        copy.wait_recv()
    for copy in tracer_halos:
        copy.wait_send()
    keep_south = jnp.where(band > 0, 1.0, 0.0)
    keep_north = jnp.where(band < bands - 1, 1.0, 0.0)
    width = south_out.shape[2]
    south = pltpu.roll(south_ref[...], width, 2)
    south_out[...] = south[..., :width] * keep_south
    north_out[...] = north_ref[..., :width] * keep_north
    band_rows = level_rows
    for level in range(2):
        east_rows = out_ref[pl.ds(level * band_rows, band_rows), :]
        zonal_ref[level] = mm(east_rows, pairs_ref[...])


def merid_kernel(wide_ref, halves_ref, after_ref, merid_ref, vsouth_ref, vnorth_ref, send_sem, recv_sem):
    band = lax.axis_index("lat")
    me = lax.axis_index("lon")
    bands = lax.axis_size("lat")
    up, down = lax.rem(band + 1, bands), lax.rem(band + bands - 1, bands)
    barrier = pltpu.get_barrier_semaphore()
    for other in (up, down):
        pl.semaphore_signal(barrier, inc=1, device_id=(other, me), device_id_type=MESH)
    pl.semaphore_wait(barrier, 2)
    band_rows = merid_ref.shape[1] - 1
    plan = []
    for level in range(2):
        first = (2 + level) * band_rows
        plan.append((wide_ref.at[pl.ds(first + band_rows - 1, 1)], vsouth_ref.at[pl.ds(level, 1)], up))
        plan.append((wide_ref.at[pl.ds(first, 1)], vnorth_ref.at[pl.ds(level, 1)], down))
    copies = []
    for index, (source, target, other) in enumerate(plan):
        copy = pltpu.make_async_remote_copy(
            src_ref=source,
            dst_ref=target,
            send_sem=send_sem.at[index],
            recv_sem=recv_sem.at[index],
            device_id=(other, me),
            device_id_type=MESH,
        )
        copy.start()
        copies.append(copy)
    face_ids = lax.broadcasted_iota(jnp.int32, (band_rows + 1, 1), 0)
    half = jnp.zeros((band_rows + 1, 1), jnp.float32)
    for face in range(band_rows + 1):
        half = jnp.where(face_ids == face, halves_ref[band * (band_rows + 1) + face], half)
    faces = lax.broadcasted_iota(jnp.int32, (band_rows + 1, band_rows), 0)
    cells = lax.broadcasted_iota(jnp.int32, (band_rows + 1, band_rows), 1)
    face_weights = jnp.where((cells == faces - 1) | (cells == faces), half, 0.0)
    south_weight = jnp.where(face_ids == 0, half, 0.0)
    north_weight = jnp.where(face_ids == band_rows, half, 0.0)
    inner = [
        jnp.dot(
            face_weights,
            wide_ref[pl.ds((2 + level) * band_rows, band_rows), :],
            precision=EXACT_MODE,
            preferred_element_type=jnp.float32,
        )
        for level in range(2)
    ]
    for copy in copies:
        copy.wait_recv()
    for copy in copies:
        copy.wait_send()
    keep_south = jnp.where(band > 0, 1.0, 0.0)
    keep_north = jnp.where(band < bands - 1, 1.0, 0.0)
    for level in range(2):
        merid = (
            inner[level]
            + south_weight * (vsouth_ref[pl.ds(level, 1), :] * keep_south)
            + north_weight * (vnorth_ref[pl.ds(level, 1), :] * keep_north)
        )
        merid_ref[level] = merid[:, : merid_ref.shape[2]]


def merid_speeds(wide, halves, after, levels, lat_rows, columns):
    return pl.pallas_call(
        merid_kernel,
        out_shape=jax.ShapeDtypeStruct((levels, lat_rows + 1, columns), jnp.float32),
        in_specs=[
            pl.BlockSpec(memory_space=pltpu.VMEM),
            pl.BlockSpec(memory_space=pltpu.SMEM),
            pl.BlockSpec(memory_space=pltpu.VMEM),
        ],
        out_specs=pl.BlockSpec(memory_space=pltpu.VMEM),
        scratch_shapes=[
            pltpu.VMEM((levels, columns + 2), jnp.float32),
            pltpu.VMEM((levels, columns + 2), jnp.float32),
            pltpu.SemaphoreType.DMA((2 * levels,)),
            pltpu.SemaphoreType.DMA((2 * levels,)),
        ],
        compiler_params=pltpu.CompilerParams(collective_id=1, has_side_effects=True),
    )(wide, halves, after)


def spectral_tables(n, rows, columns):
    lon_total = n * columns
    blocks = np.arange(n)
    phase = 2.0 * np.pi * (np.outer(blocks, blocks) % n) / n
    eye = np.eye(rows)
    column_ids = np.arange(columns)
    twist = 2.0 * np.pi * (np.outer(blocks, column_ids) % lon_total) / lon_total
    turn = 2.0 * np.pi * (np.outer(column_ids, column_ids) % columns) / columns
    wavenumber = blocks[:, None] + n * column_ids[None, :]
    sine = np.sin(wavenumber.astype(np.float32) * np.float32(math.pi / lon_total))
    divisor = np.where(wavenumber == 0, np.float32(1.0), sine * sine).astype(np.float32)
    zero_mode = (wavenumber == 0).astype(np.float32)
    widen = np.eye(columns, columns + 2)
    kron_cos, kron_sin = np.kron(np.cos(phase), eye), np.kron(np.sin(phase), eye)
    twist_wide = np.stack(
        [np.repeat(np.cos(twist), rows, axis=0) @ widen, np.repeat(np.sin(twist), rows, axis=0) @ widen]
    )
    tables = (
        np.concatenate([kron_cos, kron_sin], axis=0),
        np.concatenate([kron_cos, -kron_sin], axis=1),
        np.repeat(np.cos(twist), rows, axis=0),
        np.repeat(np.sin(twist), rows, axis=0),
        np.cos(turn),
        np.sin(turn),
        np.repeat(divisor, rows, axis=0),
        np.repeat(zero_mode, rows, axis=0),
        np.cos(turn) @ widen,
        np.sin(turn) @ widen,
        twist_wide,
    )
    return [jnp.asarray(t.astype(np.float32)) for t in tables]


def position_tables(n, rows, bands, lat_rows, flat_rows):
    lat_total = bands * lat_rows
    cells = np.arange(lat_total, dtype=np.float32)
    row_cosine = np.cos(
        (cells + np.float32(0.5)) * np.float32(math.pi / lat_total) - np.float32(0.5 * math.pi)
    ).astype(np.float32)
    scaled = ((row_cosine / np.float32(COS_FLOOR)) ** 2).astype(np.float32)
    own_rows = (np.arange(n)[:, None] * rows + np.arange(rows)[None, :]) % lat_rows
    scales = scaled[np.arange(bands)[:, None, None] * lat_rows + own_rows[None]]
    face_ids = np.arange(bands)[:, None] * lat_rows + np.arange(lat_rows + 1)[None, :]
    face_cosine = np.cos(
        face_ids.astype(np.float32) * np.float32(math.pi / lat_total) - np.float32(0.5 * math.pi)
    ).astype(np.float32)
    face_cosine = np.where((face_ids == 0) | (face_ids == lat_total), 0.0, face_cosine)
    halves = (np.float32(0.5) * face_cosine).astype(np.float32)
    return jnp.asarray(scales.reshape(-1)), jnp.asarray(halves.reshape(-1))


def exchange_all(flat_winds, lat_rows, tracers):
    flat_rows, columns = flat_winds.shape
    levels, lon_cols, merged = tracers.shape
    n = lax.axis_size("lon")
    rows = flat_rows // n
    tracer_count = merged // lat_rows
    scales, halves = position_tables(n, rows, lax.axis_size("lat"), lat_rows, flat_rows)
    pair_rows = np.zeros((columns + 2, columns + 1), np.float32)
    for face in range(columns + 1):
        pair_rows[columns if face == 0 else face - 1, face] = 0.5
        pair_rows[columns + 1 if face == columns else face, face] = 0.5
    vmem = pl.BlockSpec(memory_space=pltpu.VMEM)
    smem = pl.BlockSpec(memory_space=pltpu.SMEM)
    wide_lanes = -(-3 * tracer_count // 128) * 128
    west_cols = lon_cols - (lon_cols - 3) // 8 * 8
    shapes = [
        (flat_rows, columns),
        (levels, lat_rows, columns + 1),
        (levels, west_cols, merged),
        (levels, 8, merged),
        (levels, lon_cols, 3 * tracer_count),
        (levels, lon_cols, 3 * tracer_count),
        (flat_rows, columns + 2),
    ]
    return pl.pallas_call(
        functools.partial(filter_kernel, n, rows),
        out_shape=[jax.ShapeDtypeStruct(shape, jnp.float32) for shape in shapes],
        in_specs=[vmem, smem] + [vmem] * 12 + [pl.BlockSpec(memory_space=pl.ANY)],
        out_specs=[vmem] * len(shapes),
        scratch_shapes=[
            pltpu.VMEM((levels, lon_cols, wide_lanes), jnp.float32),
            pltpu.VMEM((levels, lon_cols, wide_lanes), jnp.float32),
            pltpu.VMEM((flat_rows, columns), jnp.float32),
            pltpu.VMEM((flat_rows, columns + 2), jnp.float32),
            pltpu.SemaphoreType.DMA((n,)),
            pltpu.SemaphoreType.DMA((n,)),
            pltpu.SemaphoreType.DMA((n,)),
            pltpu.SemaphoreType.DMA((n,)),
            pltpu.SemaphoreType.DMA((8,)),
            pltpu.SemaphoreType.DMA((8,)),
            pltpu.SemaphoreType.DMA((2,)),
        ],
        compiler_params=pltpu.CompilerParams(collective_id=0, has_side_effects=True),
    )(
        flat_winds,
        scales,
        *spectral_tables(n, rows, columns),
        jnp.asarray(pair_rows),
        tracers,
    ), halves


def stencil(padded, dim, faces, stride):

    def offset_cells(offset):
        return lax.slice_in_dim(padded, offset * stride, (offset + faces) * stride, axis=dim)

    left = (
        2.0 * offset_cells(0)
        - 13.0 * offset_cells(1)
        + 47.0 * offset_cells(2)
        + 27.0 * offset_cells(3)
        - 3.0 * offset_cells(4)
    ) / 60.0
    right = (
        2.0 * offset_cells(5)
        - 13.0 * offset_cells(4)
        + 47.0 * offset_cells(3)
        + 27.0 * offset_cells(2)
        - 3.0 * offset_cells(1)
    ) / 60.0
    return left, right


def spread(values, rows, tracer_count):
    lanes = jnp.arange(rows * tracer_count, dtype=jnp.int32) // tracer_count
    pick = (jnp.arange(rows, dtype=jnp.int32)[:, None] == lanes[None, :]).astype(jnp.float32)
    return jnp.einsum("ljc,jm->lcm", values, pick, precision=EXACT_MODE)


def local(tracers, wind_field):
    levels, lon_cols, merged = tracers.shape
    lat_rows = wind_field.shape[2]
    tracer_count = merged // lat_rows
    lat_total = lat_rows * lax.axis_size("lat")
    band = lax.axis_index("lat")
    first_row = band * lat_rows
    row_ids = first_row + jnp.arange(lat_rows, dtype=jnp.int32)
    row_cosine = jnp.cos(
        (row_ids.astype(jnp.float32) + 0.5) * (math.pi / lat_total) - 0.5 * math.pi
    )
    flat_winds = wind_field.reshape(2 * levels * lat_rows, lon_cols)
    outputs, halves = exchange_all(flat_winds, lat_rows, tracers)
    smoothed, zonal_speed, west, east, south, north, wide = outputs
    west = west[:, west.shape[1] - 3 :]
    east = east[:, :3]
    smoothed = smoothed.reshape(2, levels, lat_rows, lon_cols)
    zonal_rep = spread(zonal_speed, lat_rows, tracer_count)
    zonal_pad = jnp.concatenate([west, tracers, east], axis=1)
    left_x, right_x = stencil(zonal_pad, 1, lon_cols + 1, 1)
    zonal_flux = upwind(zonal_rep, left_x, right_x)
    merid_speed = merid_speeds(wide, halves, zonal_flux[:, :8, :128], levels, lat_rows, lon_cols)
    merid_rep = spread(merid_speed, lat_rows + 1, tracer_count)
    merid_pad = jnp.concatenate([south, tracers, north], axis=2)
    left_y, right_y = stencil(merid_pad, 2, lat_rows + 1, tracer_count)
    merid_flux = upwind(merid_rep, left_y, right_y)
    metric = jnp.repeat(1.0 / jnp.maximum(row_cosine, COS_FLOOR), tracer_count)
    change = COURANT * (zonal_flux[:, 1:] - zonal_flux[:, :-1]) + COURANT * (
        merid_flux[:, :, tracer_count:] - merid_flux[:, :, :-tracer_count]
    )
    advected = tracers - metric[None, None, :] * change
    return (advected, smoothed)


def solution(mesh):
    placed = (P(None, "lon", "lat"), P(None, None, "lat", "lon"))
    return jax.shard_map(
        local,
        mesh=mesh,
        in_specs=placed,
        out_specs=(P(None, "lon", "lat"), P(None, None, "lat", "lon")),
        check_vma=False,
    )
```

```python
import functools
import math

import jax
import numpy as np
import jax.numpy as jnp
from jax import lax
from jax.experimental import pallas as pl
from jax.experimental.pallas import tpu as pltpu
from jax.sharding import PartitionSpec as P

MESH = pl.DeviceIdType.MESH

COURANT = 0.3
COS_FLOOR = 0.5
EXACT_MODE = lax.Precision.HIGHEST


def extended(array, sides, width, wrap):
    for axis, dim in sides:
        devices, length = (lax.axis_size(axis), array.shape[dim])
        up = [(i, (i + 1) % devices) for i in range(devices if wrap else devices - 1)]
        down = [(j, i) for i, j in up]
        last = lax.slice_in_dim(array, length - width, length, axis=dim)
        first = lax.slice_in_dim(array, 0, width, axis=dim)
        before = lax.ppermute(last, axis, up)
        after = lax.ppermute(first, axis, down)
        array = jnp.concatenate([before, array, after], axis=dim)
    return array


def damping(row_cosine, wavenumber, lon_total):
    sine = jnp.sin(wavenumber.astype(jnp.float32) * (math.pi / lon_total))
    divisor = jnp.where(wavenumber == 0, 1.0, sine * sine)
    scaled = (row_cosine / COS_FLOOR) ** 2
    scaled = scaled.reshape(scaled.shape + (1,) * wavenumber.ndim)
    return jnp.where(wavenumber == 0, 1.0, jnp.minimum(1.0, scaled / divisor))


def face_values(padded, axis, cells, stride):

    def offset_cells(offset):
        return lax.slice_in_dim(padded, offset * stride, (offset + cells + 1) * stride, axis=axis)

    left = (
        2.0 * offset_cells(0)
        - 13.0 * offset_cells(1)
        + 47.0 * offset_cells(2)
        + 27.0 * offset_cells(3)
        - 3.0 * offset_cells(4)
    ) / 60.0
    right = (
        2.0 * offset_cells(5)
        - 13.0 * offset_cells(4)
        + 47.0 * offset_cells(3)
        + 27.0 * offset_cells(2)
        - 3.0 * offset_cells(1)
    ) / 60.0
    return (left, right)


def upwind(speed, left, right):
    return jnp.maximum(speed, 0.0) * left + jnp.minimum(speed, 0.0) * right


def filter_kernel(n, rows, winds_ref, scales_ref, kc_ref, ks_ref, tc_ref, ts_ref, c_ref, s_ref,
                  divisor_ref, zero_ref, widen_ref, prev_ref, next_ref, pairs_ref, halves_ref,
                  tracers_ref,
                  smooth_ref, zonal_ref, merid_ref, west_ref, east_ref, south_out, north_out,
                  out_ref, south_ref, north_ref, vsouth_ref, vnorth_ref,
                  gathered, restored, send_a, recv_a, send_b, recv_b, halo_send, halo_recv, local_sem,
                  stage_up, stage_down, stage_sem):
    me = lax.axis_index("lon")
    band = lax.axis_index("lat")
    bands = lax.axis_size("lat")
    up, down = lax.rem(band + 1, bands), lax.rem(band + bands - 1, bands)
    east_peer, west_peer = lax.rem(me + 1, n), lax.rem(me + n - 1, n)
    barrier = pltpu.get_barrier_semaphore()
    for k in range(1, n):
        peer = lax.rem(me + k, n)
        pl.semaphore_signal(barrier, inc=1, device_id=(band, peer), device_id_type=MESH)
    for other in (up, down):
        pl.semaphore_signal(barrier, inc=1, device_id=(other, me), device_id_type=MESH)
    pl.semaphore_wait(barrier, n + 1)

    cols, merged = tracers_ref.shape[1], tracers_ref.shape[2]
    lane_depth = south_ref.shape[2]
    flat_rows = out_ref.shape[0]
    level_rows = flat_rows // 4
    halo_plan = [
        (tracers_ref.at[:, pl.ds(cols - west_ref.shape[1], west_ref.shape[1]), :], west_ref, (band, east_peer)),
        (tracers_ref.at[:, pl.ds(0, east_ref.shape[1]), :], east_ref, (band, west_peer)),
        (tracers_ref.at[:, :, pl.ds(merged - lane_depth, lane_depth)], south_ref, (up, me)),
        (tracers_ref.at[:, :, pl.ds(0, lane_depth)], north_ref, (down, me)),
    ]
    halo_plan.append((stage_up, vsouth_ref, (up, me)))
    halo_plan.append((stage_down, vnorth_ref, (down, me)))
    edge_rows = [2 * level_rows + k for k in (0, level_rows - 1, level_rows, 2 * level_rows - 1)]

    def halo_copy(index):
        source, target, device = halo_plan[index]
        return pltpu.make_async_remote_copy(
            src_ref=source,
            dst_ref=target,
            send_sem=halo_send.at[index],
            recv_sem=halo_recv.at[index],
            device_id=device,
            device_id_type=MESH,
        )

    def block(ref, index):
        return ref.at[pl.ds(pl.multiple_of(index * rows, rows), rows)]

    def swap(source, target, send_sem, recv_sem, slot):
        sends = []
        for k in range(1, n):
            peer = lax.rem(me + k, n)
            copy = pltpu.make_async_remote_copy(
                src_ref=block(source, peer),
                dst_ref=block(target, me),
                send_sem=send_sem.at[peer],
                recv_sem=recv_sem.at[me],
                device_id=(band, peer),
                device_id_type=MESH,
            )
            copy.start()
            sends.append(copy)
        own = pltpu.make_async_copy(block(source, me), block(target, me), local_sem.at[slot])
        own.start()
        return sends, own

    def settle(source, target, send_sem, recv_sem, sends, own):
        own.wait()
        for k in range(1, n):
            origin = lax.rem(me + n - k, n)
            pltpu.make_async_remote_copy(
                src_ref=block(source, origin),
                dst_ref=block(target, origin),
                send_sem=send_sem.at[origin],
                recv_sem=recv_sem.at[origin],
                device_id=(band, origin),
                device_id_type=MESH,
            ).wait_recv()
        for copy in sends:
            copy.wait_send()

    sends, own = swap(winds_ref, gathered, send_a, recv_a, 0)
    tracer_halos = [halo_copy(i) for i in range(4)]
    for copy in tracer_halos:
        copy.start()
    settle(winds_ref, gathered, send_a, recv_a, sends, own)

    def mm(a, b):
        return jnp.dot(a, b, precision=EXACT_MODE, preferred_element_type=jnp.float32)

    x = gathered[...]
    half = x.shape[0]
    tc, ts = tc_ref[...], ts_ref[...]
    stacked = mm(kc_ref[...], x)
    re, im = stacked[:half], -stacked[half:]
    shifted_re = re * tc + im * ts
    shifted_im = im * tc - re * ts
    stacked = jnp.concatenate([shifted_re, shifted_im], axis=0)
    with_cos = mm(stacked, c_ref[...])
    with_sin = mm(stacked, s_ref[...])
    modes_re = with_cos[:half] + with_sin[half:]
    modes_im = with_cos[half:] - with_sin[:half]
    lane_rows = lax.broadcasted_iota(jnp.int32, (n * rows, 1), 0) % rows
    base = (band * n + me) * rows
    scaled = jnp.zeros((n * rows, 1), jnp.float32)
    for r in range(rows):
        scaled = jnp.where(lane_rows == r, scales_ref[base + r], scaled)
    factor = jnp.where(zero_ref[...] > 0.0, 1.0, jnp.minimum(1.0, scaled / divisor_ref[...]))
    stacked = jnp.concatenate([modes_re * factor, modes_im * factor], axis=0)
    with_cos = mm(stacked, widen_ref[...])
    with_sin = mm(stacked, prev_ref[...])
    back_re = with_cos[:half] - with_sin[half:]
    back_im = with_cos[half:] + with_sin[:half]
    tcw, tsw = next_ref[0], next_ref[1]
    out_re = back_re * tcw - back_im * tsw
    out_im = back_im * tcw + back_re * tsw
    result = mm(ks_ref[...], jnp.concatenate([out_re, out_im], axis=0)) / (n * x.shape[1])
    columns = x.shape[1]
    lane = lax.broadcasted_iota(jnp.int32, result.shape, 1)
    before = jnp.sum(
        jnp.where(lane == columns - 1, jnp.roll(result, rows, axis=0), 0.0), axis=1, keepdims=True
    )
    after = jnp.sum(jnp.where(lane == 0, jnp.roll(result, -rows, axis=0), 0.0), axis=1, keepdims=True)
    restored[...] = jnp.where(lane == columns, before, jnp.where(lane == columns + 1, after, result))
    sends, own = swap(restored, out_ref, send_b, recv_b, 1)
    own.wait()
    holders = sorted({row // rows for row in edge_rows})

    def arrival(origin):
        return pltpu.make_async_remote_copy(
            src_ref=block(restored, origin),
            dst_ref=block(out_ref, origin),
            send_sem=send_b.at[origin],
            recv_sem=recv_b.at[origin],
            device_id=(band, origin),
            device_id_type=MESH,
        )

    for holder in holders:

        @pl.when(me != holder)
        def _():
            arrival(holder).wait_recv()

    staged = []
    for level in range(2):
        first = 2 * level_rows + level * level_rows
        for slot, (row, stage) in enumerate(((first + level_rows - 1, stage_up), (first, stage_down))):
            copy = pltpu.make_async_copy(
                out_ref.at[pl.ds(row, 1)], stage.at[pl.ds(level, 1)], stage_sem.at[2 * level + slot]
            )
            copy.start()
            staged.append(copy)
    for copy in staged:
        copy.wait()
    wind_halos = [halo_copy(i) for i in range(4, 6)]
    for copy in wind_halos:
        copy.start()
    for k in range(1, n):
        origin = lax.rem(me + n - k, n)
        pending = origin >= 0
        for holder in holders:
            pending = jnp.logical_and(pending, origin != holder)

        @pl.when(pending)
        def _():
            arrival(origin).wait_recv()

    for copy in sends:
        copy.wait_send()
    smooth_ref[...] = out_ref[:, : smooth_ref.shape[1]]
    for copy in tracer_halos + wind_halos:
        copy.wait_recv()
    for copy in tracer_halos + wind_halos:
        copy.wait_send()

    keep_south = jnp.where(band > 0, 1.0, 0.0)
    keep_north = jnp.where(band < bands - 1, 1.0, 0.0)
    width = south_out.shape[2]
    south = pltpu.roll(south_ref[...], width, 2)
    south_out[...] = south[..., :width] * keep_south
    north_out[...] = north_ref[..., :width] * keep_north
    band_rows = level_rows
    face_ids = lax.broadcasted_iota(jnp.int32, (band_rows + 1, 1), 0)
    half = jnp.zeros((band_rows + 1, 1), jnp.float32)
    for face in range(band_rows + 1):
        half = jnp.where(face_ids == face, halves_ref[band * (band_rows + 1) + face], half)
    faces = lax.broadcasted_iota(jnp.int32, (band_rows + 1, band_rows), 0)
    cells = lax.broadcasted_iota(jnp.int32, (band_rows + 1, band_rows), 1)
    face_weights = jnp.where((cells == faces - 1) | (cells == faces), half, 0.0)
    south_weight = jnp.where(face_ids == 0, half, 0.0)
    north_weight = jnp.where(face_ids == band_rows, half, 0.0)
    for level in range(2):
        east_rows = out_ref[pl.ds(level * band_rows, band_rows), :]
        zonal_ref[level] = mm(east_rows, pairs_ref[...])
        first = 2 * level_rows + level * level_rows
        north_rows = out_ref[pl.ds(first, band_rows), :]
        merid = (
            mm(face_weights, north_rows)
            + south_weight * (vsouth_ref[pl.ds(level, 1), :] * keep_south)
            + north_weight * (vnorth_ref[pl.ds(level, 1), :] * keep_north)
        )
        merid_ref[level] = merid[:, : merid_ref.shape[2]]


def spectral_tables(n, rows, columns):
    lon_total = n * columns
    blocks = np.arange(n)
    phase = 2.0 * np.pi * (np.outer(blocks, blocks) % n) / n
    eye = np.eye(rows)
    column_ids = np.arange(columns)
    twist = 2.0 * np.pi * (np.outer(blocks, column_ids) % lon_total) / lon_total
    turn = 2.0 * np.pi * (np.outer(column_ids, column_ids) % columns) / columns
    wavenumber = blocks[:, None] + n * column_ids[None, :]
    sine = np.sin(wavenumber.astype(np.float32) * np.float32(math.pi / lon_total))
    divisor = np.where(wavenumber == 0, np.float32(1.0), sine * sine).astype(np.float32)
    zero_mode = (wavenumber == 0).astype(np.float32)
    widen = np.eye(columns, columns + 2)
    kron_cos, kron_sin = np.kron(np.cos(phase), eye), np.kron(np.sin(phase), eye)
    twist_wide = np.stack(
        [np.repeat(np.cos(twist), rows, axis=0) @ widen, np.repeat(np.sin(twist), rows, axis=0) @ widen]
    )
    tables = (
        np.concatenate([kron_cos, kron_sin], axis=0),
        np.concatenate([kron_cos, -kron_sin], axis=1),
        np.repeat(np.cos(twist), rows, axis=0),
        np.repeat(np.sin(twist), rows, axis=0),
        np.cos(turn),
        np.sin(turn),
        np.repeat(divisor, rows, axis=0),
        np.repeat(zero_mode, rows, axis=0),
        np.cos(turn) @ widen,
        np.sin(turn) @ widen,
        twist_wide,
    )
    return [jnp.asarray(t.astype(np.float32)) for t in tables]


def position_tables(n, rows, bands, lat_rows, flat_rows):
    lat_total = bands * lat_rows
    cells = np.arange(lat_total, dtype=np.float32)
    row_cosine = np.cos(
        (cells + np.float32(0.5)) * np.float32(math.pi / lat_total) - np.float32(0.5 * math.pi)
    ).astype(np.float32)
    scaled = ((row_cosine / np.float32(COS_FLOOR)) ** 2).astype(np.float32)
    own_rows = (np.arange(n)[:, None] * rows + np.arange(rows)[None, :]) % lat_rows
    scales = scaled[np.arange(bands)[:, None, None] * lat_rows + own_rows[None]]
    face_ids = np.arange(bands)[:, None] * lat_rows + np.arange(lat_rows + 1)[None, :]
    face_cosine = np.cos(
        face_ids.astype(np.float32) * np.float32(math.pi / lat_total) - np.float32(0.5 * math.pi)
    ).astype(np.float32)
    face_cosine = np.where((face_ids == 0) | (face_ids == lat_total), 0.0, face_cosine)
    halves = (np.float32(0.5) * face_cosine).astype(np.float32)
    return jnp.asarray(scales.reshape(-1)), jnp.asarray(halves.reshape(-1))


def exchange_all(flat_winds, lat_rows, tracers):
    flat_rows, columns = flat_winds.shape
    levels, lon_cols, merged = tracers.shape
    n = lax.axis_size("lon")
    rows = flat_rows // n
    tracer_count = merged // lat_rows
    scales, halves = position_tables(n, rows, lax.axis_size("lat"), lat_rows, flat_rows)
    pair_rows = np.zeros((columns + 2, columns + 1), np.float32)
    for face in range(columns + 1):
        pair_rows[columns if face == 0 else face - 1, face] = 0.5
        pair_rows[columns + 1 if face == columns else face, face] = 0.5
    vmem = pl.BlockSpec(memory_space=pltpu.VMEM)
    smem = pl.BlockSpec(memory_space=pltpu.SMEM)
    wide_lanes = -(-3 * tracer_count // 128) * 128
    west_cols = lon_cols - (lon_cols - 3) // 8 * 8
    shapes = [
        (flat_rows, columns),
        (levels, lat_rows, columns + 1),
        (levels, lat_rows + 1, columns),
        (levels, west_cols, merged),
        (levels, 8, merged),
        (levels, lon_cols, 3 * tracer_count),
        (levels, lon_cols, 3 * tracer_count),
    ]
    return pl.pallas_call(
        functools.partial(filter_kernel, n, rows),
        out_shape=[jax.ShapeDtypeStruct(shape, jnp.float32) for shape in shapes],
        in_specs=[vmem, smem]
        + [vmem] * 12
        + [smem, pl.BlockSpec(memory_space=pl.ANY)],
        out_specs=[vmem] * len(shapes),
        scratch_shapes=[
            pltpu.VMEM((flat_rows, columns + 2), jnp.float32),
            pltpu.VMEM((levels, lon_cols, wide_lanes), jnp.float32),
            pltpu.VMEM((levels, lon_cols, wide_lanes), jnp.float32),
            pltpu.VMEM((levels, columns + 2), jnp.float32),
            pltpu.VMEM((levels, columns + 2), jnp.float32),
            pltpu.VMEM((flat_rows, columns), jnp.float32),
            pltpu.VMEM((flat_rows, columns + 2), jnp.float32),
            pltpu.SemaphoreType.DMA((n,)),
            pltpu.SemaphoreType.DMA((n,)),
            pltpu.SemaphoreType.DMA((n,)),
            pltpu.SemaphoreType.DMA((n,)),
            pltpu.SemaphoreType.DMA((8,)),
            pltpu.SemaphoreType.DMA((8,)),
            pltpu.SemaphoreType.DMA((2,)),
            pltpu.VMEM((levels, columns + 2), jnp.float32),
            pltpu.VMEM((levels, columns + 2), jnp.float32),
            pltpu.SemaphoreType.DMA((4,)),
        ],
        compiler_params=pltpu.CompilerParams(collective_id=0, has_side_effects=True),
    )(
        flat_winds,
        scales,
        *spectral_tables(n, rows, columns),
        jnp.asarray(pair_rows),
        halves,
        tracers,
    )


def stencil(padded, dim, faces, stride):

    def offset_cells(offset):
        return lax.slice_in_dim(padded, offset * stride, (offset + faces) * stride, axis=dim)

    left = (
        2.0 * offset_cells(0)
        - 13.0 * offset_cells(1)
        + 47.0 * offset_cells(2)
        + 27.0 * offset_cells(3)
        - 3.0 * offset_cells(4)
    ) / 60.0
    right = (
        2.0 * offset_cells(5)
        - 13.0 * offset_cells(4)
        + 47.0 * offset_cells(3)
        + 27.0 * offset_cells(2)
        - 3.0 * offset_cells(1)
    ) / 60.0
    return left, right


def spread(values, rows, tracer_count):
    lanes = jnp.arange(rows * tracer_count, dtype=jnp.int32) // tracer_count
    pick = (jnp.arange(rows, dtype=jnp.int32)[:, None] == lanes[None, :]).astype(jnp.float32)
    return jnp.einsum("ljc,jm->lcm", values, pick, precision=EXACT_MODE)


def local(tracers, wind_field):
    levels, lon_cols, merged = tracers.shape
    lat_rows = wind_field.shape[2]
    tracer_count = merged // lat_rows
    lat_total = lat_rows * lax.axis_size("lat")
    band = lax.axis_index("lat")
    first_row = band * lat_rows
    row_ids = first_row + jnp.arange(lat_rows, dtype=jnp.int32)
    row_cosine = jnp.cos(
        (row_ids.astype(jnp.float32) + 0.5) * (math.pi / lat_total) - 0.5 * math.pi
    )
    flat_winds = wind_field.reshape(2 * levels * lat_rows, lon_cols)
    smoothed, zonal_speed, merid_speed, west, east, south, north = exchange_all(
        flat_winds, lat_rows, tracers
    )
    west = west[:, west.shape[1] - 3 :]
    east = east[:, :3]
    smoothed = smoothed.reshape(2, levels, lat_rows, lon_cols)
    zonal_rep = spread(zonal_speed, lat_rows, tracer_count)
    merid_rep = spread(merid_speed, lat_rows + 1, tracer_count)
    zonal_pad = jnp.concatenate([west, tracers, east], axis=1)
    left_x, right_x = stencil(zonal_pad, 1, lon_cols + 1, 1)
    zonal_flux = upwind(zonal_rep, left_x, right_x)
    merid_pad = jnp.concatenate([south, tracers, north], axis=2)
    left_y, right_y = stencil(merid_pad, 2, lat_rows + 1, tracer_count)
    merid_flux = upwind(merid_rep, left_y, right_y)
    metric = jnp.repeat(1.0 / jnp.maximum(row_cosine, COS_FLOOR), tracer_count)
    change = COURANT * (zonal_flux[:, 1:] - zonal_flux[:, :-1]) + COURANT * (
        merid_flux[:, :, tracer_count:] - merid_flux[:, :, :-tracer_count]
    )
    advected = tracers - metric[None, None, :] * change
    return (advected, smoothed)


def solution(mesh):
    placed = (P(None, "lon", "lat"), P(None, None, "lat", "lon"))
    return jax.shard_map(
        local,
        mesh=mesh,
        in_specs=placed,
        out_specs=(P(None, "lon", "lat"), P(None, None, "lat", "lon")),
        check_vma=False,
    )
```

```python
import functools
import math

import jax
import numpy as np
import jax.numpy as jnp
from jax import lax
from jax.experimental import pallas as pl
from jax.experimental.pallas import tpu as pltpu
from jax.sharding import PartitionSpec as P

MESH = pl.DeviceIdType.MESH

COURANT = 0.3
COS_FLOOR = 0.5
EXACT_MODE = lax.Precision.HIGHEST


def extended(array, sides, width, wrap):
    for axis, dim in sides:
        devices, length = (lax.axis_size(axis), array.shape[dim])
        up = [(i, (i + 1) % devices) for i in range(devices if wrap else devices - 1)]
        down = [(j, i) for i, j in up]
        last = lax.slice_in_dim(array, length - width, length, axis=dim)
        first = lax.slice_in_dim(array, 0, width, axis=dim)
        before = lax.ppermute(last, axis, up)
        after = lax.ppermute(first, axis, down)
        array = jnp.concatenate([before, array, after], axis=dim)
    return array


def damping(row_cosine, wavenumber, lon_total):
    sine = jnp.sin(wavenumber.astype(jnp.float32) * (math.pi / lon_total))
    divisor = jnp.where(wavenumber == 0, 1.0, sine * sine)
    scaled = (row_cosine / COS_FLOOR) ** 2
    scaled = scaled.reshape(scaled.shape + (1,) * wavenumber.ndim)
    return jnp.where(wavenumber == 0, 1.0, jnp.minimum(1.0, scaled / divisor))


def face_values(padded, axis, cells, stride):

    def offset_cells(offset):
        return lax.slice_in_dim(padded, offset * stride, (offset + cells + 1) * stride, axis=axis)

    left = (
        2.0 * offset_cells(0)
        - 13.0 * offset_cells(1)
        + 47.0 * offset_cells(2)
        + 27.0 * offset_cells(3)
        - 3.0 * offset_cells(4)
    ) / 60.0
    right = (
        2.0 * offset_cells(5)
        - 13.0 * offset_cells(4)
        + 47.0 * offset_cells(3)
        + 27.0 * offset_cells(2)
        - 3.0 * offset_cells(1)
    ) / 60.0
    return (left, right)


def upwind(speed, left, right):
    return jnp.maximum(speed, 0.0) * left + jnp.minimum(speed, 0.0) * right


def filter_kernel(n, rows, winds_ref, scales_ref, kc_ref, ks_ref, tc_ref, ts_ref, c_ref, s_ref,
                  divisor_ref, zero_ref, widen_ref, prev_ref, next_ref, pairs_ref, halves_ref,
                  tracers_ref,
                  smooth_ref, zonal_ref, merid_ref, west_ref, east_ref, south_out, north_out,
                  out_ref, south_ref, north_ref, vsouth_ref, vnorth_ref,
                  gathered, restored, send_a, recv_a, send_b, recv_b, halo_send, halo_recv, local_sem):
    me = lax.axis_index("lon")
    band = lax.axis_index("lat")
    bands = lax.axis_size("lat")
    up, down = lax.rem(band + 1, bands), lax.rem(band + bands - 1, bands)
    east_peer, west_peer = lax.rem(me + 1, n), lax.rem(me + n - 1, n)
    barrier = pltpu.get_barrier_semaphore()
    for k in range(1, n):
        peer = lax.rem(me + k, n)
        pl.semaphore_signal(barrier, inc=1, device_id=(band, peer), device_id_type=MESH)
    for other in (up, down):
        pl.semaphore_signal(barrier, inc=1, device_id=(other, me), device_id_type=MESH)
    pl.semaphore_wait(barrier, n + 1)

    cols, merged = tracers_ref.shape[1], tracers_ref.shape[2]
    lane_depth = south_ref.shape[2]
    flat_rows = out_ref.shape[0]
    level_rows = flat_rows // 4
    halo_plan = [
        (tracers_ref.at[:, pl.ds(cols - west_ref.shape[1], west_ref.shape[1]), :], west_ref, (band, east_peer)),
        (tracers_ref.at[:, pl.ds(0, east_ref.shape[1]), :], east_ref, (band, west_peer)),
        (tracers_ref.at[:, :, pl.ds(merged - lane_depth, lane_depth)], south_ref, (up, me)),
        (tracers_ref.at[:, :, pl.ds(0, lane_depth)], north_ref, (down, me)),
    ]
    for level in range(2):
        first = 2 * level_rows + level * level_rows
        halo_plan.append(
            (out_ref.at[pl.ds(first + level_rows - 1, 1)], vsouth_ref.at[pl.ds(level, 1)], (up, me))
        )
    for level in range(2):
        first = 2 * level_rows + level * level_rows
        halo_plan.append((out_ref.at[pl.ds(first, 1)], vnorth_ref.at[pl.ds(level, 1)], (down, me)))
    edge_rows = [2 * level_rows + k for k in (0, level_rows - 1, level_rows, 2 * level_rows - 1)]

    def halo_copy(index):
        source, target, device = halo_plan[index]
        return pltpu.make_async_remote_copy(
            src_ref=source,
            dst_ref=target,
            send_sem=halo_send.at[index],
            recv_sem=halo_recv.at[index],
            device_id=device,
            device_id_type=MESH,
        )

    def block(ref, index):
        return ref.at[pl.ds(pl.multiple_of(index * rows, rows), rows)]

    def swap(source, target, send_sem, recv_sem, slot):
        sends = []
        for k in range(1, n):
            peer = lax.rem(me + k, n)
            copy = pltpu.make_async_remote_copy(
                src_ref=block(source, peer),
                dst_ref=block(target, me),
                send_sem=send_sem.at[peer],
                recv_sem=recv_sem.at[me],
                device_id=(band, peer),
                device_id_type=MESH,
            )
            copy.start()
            sends.append(copy)
        own = pltpu.make_async_copy(block(source, me), block(target, me), local_sem.at[slot])
        own.start()
        return sends, own

    def settle(source, target, send_sem, recv_sem, sends, own):
        own.wait()
        for k in range(1, n):
            origin = lax.rem(me + n - k, n)
            pltpu.make_async_remote_copy(
                src_ref=block(source, origin),
                dst_ref=block(target, origin),
                send_sem=send_sem.at[origin],
                recv_sem=recv_sem.at[origin],
                device_id=(band, origin),
                device_id_type=MESH,
            ).wait_recv()
        for copy in sends:
            copy.wait_send()

    sends, own = swap(winds_ref, gathered, send_a, recv_a, 0)
    tracer_halos = [halo_copy(i) for i in range(4)]
    for copy in tracer_halos:
        copy.start()
    settle(winds_ref, gathered, send_a, recv_a, sends, own)

    def mm(a, b):
        return jnp.dot(a, b, precision=EXACT_MODE, preferred_element_type=jnp.float32)

    x = gathered[...]
    half = x.shape[0]
    tc, ts = tc_ref[...], ts_ref[...]
    stacked = mm(kc_ref[...], x)
    re, im = stacked[:half], -stacked[half:]
    shifted_re = re * tc + im * ts
    shifted_im = im * tc - re * ts
    stacked = jnp.concatenate([shifted_re, shifted_im], axis=0)
    with_cos = mm(stacked, c_ref[...])
    with_sin = mm(stacked, s_ref[...])
    modes_re = with_cos[:half] + with_sin[half:]
    modes_im = with_cos[half:] - with_sin[:half]
    lane_rows = lax.broadcasted_iota(jnp.int32, (n * rows, 1), 0) % rows
    base = (band * n + me) * rows
    scaled = jnp.zeros((n * rows, 1), jnp.float32)
    for r in range(rows):
        scaled = jnp.where(lane_rows == r, scales_ref[base + r], scaled)
    factor = jnp.where(zero_ref[...] > 0.0, 1.0, jnp.minimum(1.0, scaled / divisor_ref[...]))
    stacked = jnp.concatenate([modes_re * factor, modes_im * factor], axis=0)
    with_cos = mm(stacked, widen_ref[...])
    with_sin = mm(stacked, prev_ref[...])
    back_re = with_cos[:half] - with_sin[half:]
    back_im = with_cos[half:] + with_sin[:half]
    tcw, tsw = next_ref[0], next_ref[1]
    out_re = back_re * tcw - back_im * tsw
    out_im = back_im * tcw + back_re * tsw
    result = mm(ks_ref[...], jnp.concatenate([out_re, out_im], axis=0)) / (n * x.shape[1])
    columns = x.shape[1]
    lane = lax.broadcasted_iota(jnp.int32, result.shape, 1)
    before = jnp.sum(
        jnp.where(lane == columns - 1, jnp.roll(result, rows, axis=0), 0.0), axis=1, keepdims=True
    )
    after = jnp.sum(jnp.where(lane == 0, jnp.roll(result, -rows, axis=0), 0.0), axis=1, keepdims=True)
    restored[...] = jnp.where(lane == columns, before, jnp.where(lane == columns + 1, after, result))
    sends, own = swap(restored, out_ref, send_b, recv_b, 1)
    own.wait()
    holders = sorted({row // rows for row in edge_rows})

    def arrival(origin):
        return pltpu.make_async_remote_copy(
            src_ref=block(restored, origin),
            dst_ref=block(out_ref, origin),
            send_sem=send_b.at[origin],
            recv_sem=recv_b.at[origin],
            device_id=(band, origin),
            device_id_type=MESH,
        )

    for holder in holders:

        @pl.when(me != holder)
        def _():
            arrival(holder).wait_recv()

    wind_halos = [halo_copy(i) for i in range(4, 8)]
    for copy in wind_halos:
        copy.start()
    for k in range(1, n):
        origin = lax.rem(me + n - k, n)
        pending = origin >= 0
        for holder in holders:
            pending = jnp.logical_and(pending, origin != holder)

        @pl.when(pending)
        def _():
            arrival(origin).wait_recv()

    for copy in sends:
        copy.wait_send()
    smooth_ref[...] = out_ref[:, : smooth_ref.shape[1]]
    keep_south = jnp.where(band > 0, 1.0, 0.0)
    keep_north = jnp.where(band < bands - 1, 1.0, 0.0)
    band_rows = level_rows
    face_ids = lax.broadcasted_iota(jnp.int32, (band_rows + 1, 1), 0)
    half = jnp.zeros((band_rows + 1, 1), jnp.float32)
    for face in range(band_rows + 1):
        half = jnp.where(face_ids == face, halves_ref[band * (band_rows + 1) + face], half)
    faces = lax.broadcasted_iota(jnp.int32, (band_rows + 1, band_rows), 0)
    cells = lax.broadcasted_iota(jnp.int32, (band_rows + 1, band_rows), 1)
    face_weights = jnp.where((cells == faces - 1) | (cells == faces), half, 0.0)
    south_weight = jnp.where(face_ids == 0, half, 0.0)
    north_weight = jnp.where(face_ids == band_rows, half, 0.0)
    inner = []
    for level in range(2):
        east_rows = out_ref[pl.ds(level * band_rows, band_rows), :]
        zonal_ref[level] = mm(east_rows, pairs_ref[...])
        first = 2 * level_rows + level * level_rows
        inner.append(mm(face_weights, out_ref[pl.ds(first, band_rows), :]))
    for copy in tracer_halos:
        copy.wait_recv()
    width = south_out.shape[2]
    south = pltpu.roll(south_ref[...], width, 2)
    south_out[...] = south[..., :width] * keep_south
    north_out[...] = north_ref[..., :width] * keep_north
    for copy in wind_halos:
        copy.wait_recv()
    for copy in tracer_halos + wind_halos:
        copy.wait_send()
    for level in range(2):
        merid = (
            inner[level]
            + south_weight * (vsouth_ref[pl.ds(level, 1), :] * keep_south)
            + north_weight * (vnorth_ref[pl.ds(level, 1), :] * keep_north)
        )
        merid_ref[level] = merid[:, : merid_ref.shape[2]]


def spectral_tables(n, rows, columns):
    lon_total = n * columns
    blocks = np.arange(n)
    phase = 2.0 * np.pi * (np.outer(blocks, blocks) % n) / n
    eye = np.eye(rows)
    column_ids = np.arange(columns)
    twist = 2.0 * np.pi * (np.outer(blocks, column_ids) % lon_total) / lon_total
    turn = 2.0 * np.pi * (np.outer(column_ids, column_ids) % columns) / columns
    wavenumber = blocks[:, None] + n * column_ids[None, :]
    sine = np.sin(wavenumber.astype(np.float32) * np.float32(math.pi / lon_total))
    divisor = np.where(wavenumber == 0, np.float32(1.0), sine * sine).astype(np.float32)
    zero_mode = (wavenumber == 0).astype(np.float32)
    widen = np.eye(columns, columns + 2)
    kron_cos, kron_sin = np.kron(np.cos(phase), eye), np.kron(np.sin(phase), eye)
    twist_wide = np.stack(
        [np.repeat(np.cos(twist), rows, axis=0) @ widen, np.repeat(np.sin(twist), rows, axis=0) @ widen]
    )
    tables = (
        np.concatenate([kron_cos, kron_sin], axis=0),
        np.concatenate([kron_cos, -kron_sin], axis=1),
        np.repeat(np.cos(twist), rows, axis=0),
        np.repeat(np.sin(twist), rows, axis=0),
        np.cos(turn),
        np.sin(turn),
        np.repeat(divisor, rows, axis=0),
        np.repeat(zero_mode, rows, axis=0),
        np.cos(turn) @ widen,
        np.sin(turn) @ widen,
        twist_wide,
    )
    return [jnp.asarray(t.astype(np.float32)) for t in tables]


def position_tables(n, rows, bands, lat_rows, flat_rows):
    lat_total = bands * lat_rows
    cells = np.arange(lat_total, dtype=np.float32)
    row_cosine = np.cos(
        (cells + np.float32(0.5)) * np.float32(math.pi / lat_total) - np.float32(0.5 * math.pi)
    ).astype(np.float32)
    scaled = ((row_cosine / np.float32(COS_FLOOR)) ** 2).astype(np.float32)
    own_rows = (np.arange(n)[:, None] * rows + np.arange(rows)[None, :]) % lat_rows
    scales = scaled[np.arange(bands)[:, None, None] * lat_rows + own_rows[None]]
    face_ids = np.arange(bands)[:, None] * lat_rows + np.arange(lat_rows + 1)[None, :]
    face_cosine = np.cos(
        face_ids.astype(np.float32) * np.float32(math.pi / lat_total) - np.float32(0.5 * math.pi)
    ).astype(np.float32)
    face_cosine = np.where((face_ids == 0) | (face_ids == lat_total), 0.0, face_cosine)
    halves = (np.float32(0.5) * face_cosine).astype(np.float32)
    return jnp.asarray(scales.reshape(-1)), jnp.asarray(halves.reshape(-1))


def exchange_all(flat_winds, lat_rows, tracers):
    flat_rows, columns = flat_winds.shape
    levels, lon_cols, merged = tracers.shape
    n = lax.axis_size("lon")
    rows = flat_rows // n
    tracer_count = merged // lat_rows
    scales, halves = position_tables(n, rows, lax.axis_size("lat"), lat_rows, flat_rows)
    pair_rows = np.zeros((columns + 2, columns + 1), np.float32)
    for face in range(columns + 1):
        pair_rows[columns if face == 0 else face - 1, face] = 0.5
        pair_rows[columns + 1 if face == columns else face, face] = 0.5
    vmem = pl.BlockSpec(memory_space=pltpu.VMEM)
    smem = pl.BlockSpec(memory_space=pltpu.SMEM)
    wide_lanes = -(-3 * tracer_count // 128) * 128
    west_cols = lon_cols - (lon_cols - 3) // 8 * 8
    shapes = [
        (flat_rows, columns),
        (levels, lat_rows, columns + 1),
        (levels, lat_rows + 1, columns),
        (levels, west_cols, merged),
        (levels, 8, merged),
        (levels, lon_cols, 3 * tracer_count),
        (levels, lon_cols, 3 * tracer_count),
    ]
    return pl.pallas_call(
        functools.partial(filter_kernel, n, rows),
        out_shape=[jax.ShapeDtypeStruct(shape, jnp.float32) for shape in shapes],
        in_specs=[vmem, smem]
        + [vmem] * 12
        + [smem, pl.BlockSpec(memory_space=pl.ANY)],
        out_specs=[vmem] * len(shapes),
        scratch_shapes=[
            pltpu.VMEM((flat_rows, columns + 2), jnp.float32),
            pltpu.VMEM((levels, lon_cols, wide_lanes), jnp.float32),
            pltpu.VMEM((levels, lon_cols, wide_lanes), jnp.float32),
            pltpu.VMEM((levels, columns + 2), jnp.float32),
            pltpu.VMEM((levels, columns + 2), jnp.float32),
            pltpu.VMEM((flat_rows, columns), jnp.float32),
            pltpu.VMEM((flat_rows, columns + 2), jnp.float32),
            pltpu.SemaphoreType.DMA((n,)),
            pltpu.SemaphoreType.DMA((n,)),
            pltpu.SemaphoreType.DMA((n,)),
            pltpu.SemaphoreType.DMA((n,)),
            pltpu.SemaphoreType.DMA((8,)),
            pltpu.SemaphoreType.DMA((8,)),
            pltpu.SemaphoreType.DMA((2,)),
        ],
        compiler_params=pltpu.CompilerParams(collective_id=0, has_side_effects=True),
    )(
        flat_winds,
        scales,
        *spectral_tables(n, rows, columns),
        jnp.asarray(pair_rows),
        halves,
        tracers,
    )


def stencil(padded, dim, faces, stride):

    def offset_cells(offset):
        return lax.slice_in_dim(padded, offset * stride, (offset + faces) * stride, axis=dim)

    left = (
        2.0 * offset_cells(0)
        - 13.0 * offset_cells(1)
        + 47.0 * offset_cells(2)
        + 27.0 * offset_cells(3)
        - 3.0 * offset_cells(4)
    ) / 60.0
    right = (
        2.0 * offset_cells(5)
        - 13.0 * offset_cells(4)
        + 47.0 * offset_cells(3)
        + 27.0 * offset_cells(2)
        - 3.0 * offset_cells(1)
    ) / 60.0
    return left, right


def spread(values, rows, tracer_count):
    lanes = jnp.arange(rows * tracer_count, dtype=jnp.int32) // tracer_count
    pick = (jnp.arange(rows, dtype=jnp.int32)[:, None] == lanes[None, :]).astype(jnp.float32)
    return jnp.einsum("ljc,jm->lcm", values, pick, precision=EXACT_MODE)


def local(tracers, wind_field):
    levels, lon_cols, merged = tracers.shape
    lat_rows = wind_field.shape[2]
    tracer_count = merged // lat_rows
    lat_total = lat_rows * lax.axis_size("lat")
    band = lax.axis_index("lat")
    first_row = band * lat_rows
    row_ids = first_row + jnp.arange(lat_rows, dtype=jnp.int32)
    row_cosine = jnp.cos(
        (row_ids.astype(jnp.float32) + 0.5) * (math.pi / lat_total) - 0.5 * math.pi
    )
    flat_winds = wind_field.reshape(2 * levels * lat_rows, lon_cols)
    smoothed, zonal_speed, merid_speed, west, east, south, north = exchange_all(
        flat_winds, lat_rows, tracers
    )
    west = west[:, west.shape[1] - 3 :]
    east = east[:, :3]
    smoothed = smoothed.reshape(2, levels, lat_rows, lon_cols)
    zonal_rep = spread(zonal_speed, lat_rows, tracer_count)
    merid_rep = spread(merid_speed, lat_rows + 1, tracer_count)
    zonal_pad = jnp.concatenate([west, tracers, east], axis=1)
    left_x, right_x = stencil(zonal_pad, 1, lon_cols + 1, 1)
    zonal_flux = upwind(zonal_rep, left_x, right_x)
    merid_pad = jnp.concatenate([south, tracers, north], axis=2)
    left_y, right_y = stencil(merid_pad, 2, lat_rows + 1, tracer_count)
    merid_flux = upwind(merid_rep, left_y, right_y)
    metric = jnp.repeat(1.0 / jnp.maximum(row_cosine, COS_FLOOR), tracer_count)
    change = COURANT * (zonal_flux[:, 1:] - zonal_flux[:, :-1]) + COURANT * (
        merid_flux[:, :, tracer_count:] - merid_flux[:, :, :-tracer_count]
    )
    advected = tracers - metric[None, None, :] * change
    return (advected, smoothed)


def solution(mesh):
    placed = (P(None, "lon", "lat"), P(None, None, "lat", "lon"))
    return jax.shard_map(
        local,
        mesh=mesh,
        in_specs=placed,
        out_specs=(P(None, "lon", "lat"), P(None, None, "lat", "lon")),
        check_vma=False,
    )
```

```python
import functools
import math

import jax
import numpy as np
import jax.numpy as jnp
from jax import lax
from jax.experimental import pallas as pl
from jax.experimental.pallas import tpu as pltpu
from jax.sharding import PartitionSpec as P

MESH = pl.DeviceIdType.MESH

COURANT = 0.3
COS_FLOOR = 0.5
EXACT_MODE = lax.Precision.HIGHEST


def extended(array, sides, width, wrap):
    for axis, dim in sides:
        devices, length = (lax.axis_size(axis), array.shape[dim])
        up = [(i, (i + 1) % devices) for i in range(devices if wrap else devices - 1)]
        down = [(j, i) for i, j in up]
        last = lax.slice_in_dim(array, length - width, length, axis=dim)
        first = lax.slice_in_dim(array, 0, width, axis=dim)
        before = lax.ppermute(last, axis, up)
        after = lax.ppermute(first, axis, down)
        array = jnp.concatenate([before, array, after], axis=dim)
    return array


def damping(row_cosine, wavenumber, lon_total):
    sine = jnp.sin(wavenumber.astype(jnp.float32) * (math.pi / lon_total))
    divisor = jnp.where(wavenumber == 0, 1.0, sine * sine)
    scaled = (row_cosine / COS_FLOOR) ** 2
    scaled = scaled.reshape(scaled.shape + (1,) * wavenumber.ndim)
    return jnp.where(wavenumber == 0, 1.0, jnp.minimum(1.0, scaled / divisor))


def face_values(padded, axis, cells, stride):

    def offset_cells(offset):
        return lax.slice_in_dim(padded, offset * stride, (offset + cells + 1) * stride, axis=axis)

    left = (
        2.0 * offset_cells(0)
        - 13.0 * offset_cells(1)
        + 47.0 * offset_cells(2)
        + 27.0 * offset_cells(3)
        - 3.0 * offset_cells(4)
    ) / 60.0
    right = (
        2.0 * offset_cells(5)
        - 13.0 * offset_cells(4)
        + 47.0 * offset_cells(3)
        + 27.0 * offset_cells(2)
        - 3.0 * offset_cells(1)
    ) / 60.0
    return (left, right)


def upwind(speed, left, right):
    return jnp.maximum(speed, 0.0) * left + jnp.minimum(speed, 0.0) * right


def filter_kernel(n, rows, winds_ref, scales_ref, kc_ref, ks_ref, tc_ref, ts_ref, c_ref, s_ref,
                  divisor_ref, zero_ref, widen_ref, prev_ref, next_ref, pairs_ref, halves_ref,
                  tracers_ref,
                  smooth_ref, zonal_ref, merid_ref, west_ref, east_ref, south_out, north_out,
                  out_ref, south_ref, north_ref, vsouth_ref, vnorth_ref,
                  gathered, restored, send_a, recv_a, send_b, recv_b, halo_send, halo_recv, local_sem):
    me = lax.axis_index("lon")
    band = lax.axis_index("lat")
    bands = lax.axis_size("lat")
    up, down = lax.rem(band + 1, bands), lax.rem(band + bands - 1, bands)
    east_peer, west_peer = lax.rem(me + 1, n), lax.rem(me + n - 1, n)
    barrier = pltpu.get_barrier_semaphore()
    for k in range(1, n):
        peer = lax.rem(me + k, n)
        pl.semaphore_signal(barrier, inc=1, device_id=(band, peer), device_id_type=MESH)
    for other in (up, down):
        pl.semaphore_signal(barrier, inc=1, device_id=(other, me), device_id_type=MESH)
    pl.semaphore_wait(barrier, n + 1)

    cols, merged = tracers_ref.shape[1], tracers_ref.shape[2]
    lane_depth = south_ref.shape[2]
    flat_rows = out_ref.shape[0]
    level_rows = flat_rows // 4
    halo_plan = [
        (tracers_ref.at[:, pl.ds(cols - west_ref.shape[1], west_ref.shape[1]), :], west_ref, (band, east_peer)),
        (tracers_ref.at[:, pl.ds(0, east_ref.shape[1]), :], east_ref, (band, west_peer)),
        (tracers_ref.at[:, :, pl.ds(merged - lane_depth, lane_depth)], south_ref, (up, me)),
        (tracers_ref.at[:, :, pl.ds(0, lane_depth)], north_ref, (down, me)),
    ]
    for level in range(2):
        first = 2 * level_rows + level * level_rows
        halo_plan.append(
            (out_ref.at[pl.ds(first + level_rows - 1, 1)], vsouth_ref.at[pl.ds(level, 1)], (up, me))
        )
    for level in range(2):
        first = 2 * level_rows + level * level_rows
        halo_plan.append((out_ref.at[pl.ds(first, 1)], vnorth_ref.at[pl.ds(level, 1)], (down, me)))
    edge_rows = [2 * level_rows + k for k in (0, level_rows - 1, level_rows, 2 * level_rows - 1)]

    def halo_copy(index):
        source, target, device = halo_plan[index]
        return pltpu.make_async_remote_copy(
            src_ref=source,
            dst_ref=target,
            send_sem=halo_send.at[index],
            recv_sem=halo_recv.at[index],
            device_id=device,
            device_id_type=MESH,
        )

    def block(ref, index):
        return ref.at[pl.ds(pl.multiple_of(index * rows, rows), rows)]

    def swap(source, target, send_sem, recv_sem, slot):
        sends = []
        for k in range(1, n):
            peer = lax.rem(me + k, n)
            copy = pltpu.make_async_remote_copy(
                src_ref=block(source, peer),
                dst_ref=block(target, me),
                send_sem=send_sem.at[peer],
                recv_sem=recv_sem.at[me],
                device_id=(band, peer),
                device_id_type=MESH,
            )
            copy.start()
            sends.append(copy)
        own = pltpu.make_async_copy(block(source, me), block(target, me), local_sem.at[slot])
        own.start()
        return sends, own

    def settle(source, target, send_sem, recv_sem, sends, own):
        own.wait()
        for k in range(1, n):
            origin = lax.rem(me + n - k, n)
            pltpu.make_async_remote_copy(
                src_ref=block(source, origin),
                dst_ref=block(target, origin),
                send_sem=send_sem.at[origin],
                recv_sem=recv_sem.at[origin],
                device_id=(band, origin),
                device_id_type=MESH,
            ).wait_recv()
        for copy in sends:
            copy.wait_send()

    sends, own = swap(winds_ref, gathered, send_a, recv_a, 0)
    tracer_halos = [halo_copy(i) for i in range(4)]
    for copy in tracer_halos:
        copy.start()
    settle(winds_ref, gathered, send_a, recv_a, sends, own)

    def mm(a, b):
        return jnp.dot(a, b, precision=EXACT_MODE, preferred_element_type=jnp.float32)

    x = gathered[...]
    half = x.shape[0]
    tc, ts = tc_ref[...], ts_ref[...]
    stacked = mm(kc_ref[...], x)
    re, im = stacked[:half], -stacked[half:]
    shifted_re = re * tc + im * ts
    shifted_im = im * tc - re * ts
    stacked = jnp.concatenate([shifted_re, shifted_im], axis=0)
    with_cos = mm(stacked, c_ref[...])
    with_sin = mm(stacked, s_ref[...])
    modes_re = with_cos[:half] + with_sin[half:]
    modes_im = with_cos[half:] - with_sin[:half]
    lane_rows = lax.broadcasted_iota(jnp.int32, (n * rows, 1), 0) % rows
    base = (band * n + me) * rows
    scaled = jnp.zeros((n * rows, 1), jnp.float32)
    for r in range(rows):
        scaled = jnp.where(lane_rows == r, scales_ref[base + r], scaled)
    factor = jnp.where(zero_ref[...] > 0.0, 1.0, jnp.minimum(1.0, scaled / divisor_ref[...]))
    stacked = jnp.concatenate([modes_re * factor, modes_im * factor], axis=0)
    with_cos = mm(stacked, widen_ref[...])
    with_sin = mm(stacked, prev_ref[...])
    back_re = with_cos[:half] - with_sin[half:]
    back_im = with_cos[half:] + with_sin[:half]
    tcw, tsw = next_ref[0], next_ref[1]
    out_re = back_re * tcw - back_im * tsw
    out_im = back_im * tcw + back_re * tsw
    result = mm(ks_ref[...], jnp.concatenate([out_re, out_im], axis=0)) / (n * x.shape[1])
    columns = x.shape[1]
    lane = lax.broadcasted_iota(jnp.int32, result.shape, 1)
    before = jnp.sum(
        jnp.where(lane == columns - 1, jnp.roll(result, rows, axis=0), 0.0), axis=1, keepdims=True
    )
    after = jnp.sum(jnp.where(lane == 0, jnp.roll(result, -rows, axis=0), 0.0), axis=1, keepdims=True)
    restored[...] = jnp.where(lane == columns, before, jnp.where(lane == columns + 1, after, result))
    sends, own = swap(restored, out_ref, send_b, recv_b, 1)
    own.wait()
    holders = sorted({row // rows for row in edge_rows})

    def arrival(origin):
        return pltpu.make_async_remote_copy(
            src_ref=block(restored, origin),
            dst_ref=block(out_ref, origin),
            send_sem=send_b.at[origin],
            recv_sem=recv_b.at[origin],
            device_id=(band, origin),
            device_id_type=MESH,
        )

    for holder in holders:

        @pl.when(me != holder)
        def _():
            arrival(holder).wait_recv()

    wind_halos = [halo_copy(i) for i in range(4, 8)]
    for copy in wind_halos:
        copy.start()
    for k in range(1, n):
        origin = lax.rem(me + n - k, n)
        pending = origin >= 0
        for holder in holders:
            pending = jnp.logical_and(pending, origin != holder)

        @pl.when(pending)
        def _():
            arrival(origin).wait_recv()

    for copy in sends:
        copy.wait_send()
    smooth_ref[...] = out_ref[:, : smooth_ref.shape[1]]
    keep_south = jnp.where(band > 0, 1.0, 0.0)
    keep_north = jnp.where(band < bands - 1, 1.0, 0.0)
    band_rows = level_rows
    face_ids = lax.broadcasted_iota(jnp.int32, (band_rows + 1, 1), 0)
    half = jnp.zeros((band_rows + 1, 1), jnp.float32)
    for face in range(band_rows + 1):
        half = jnp.where(face_ids == face, halves_ref[band * (band_rows + 1) + face], half)
    faces = lax.broadcasted_iota(jnp.int32, (band_rows + 1, band_rows), 0)
    cells = lax.broadcasted_iota(jnp.int32, (band_rows + 1, band_rows), 1)
    face_weights = jnp.where((cells == faces - 1) | (cells == faces), half, 0.0)
    south_weight = jnp.where(face_ids == 0, half, 0.0)
    north_weight = jnp.where(face_ids == band_rows, half, 0.0)
    inner = []
    for level in range(2):
        east_rows = out_ref[pl.ds(level * band_rows, band_rows), :]
        zonal_ref[level] = mm(east_rows, pairs_ref[...])
        first = 2 * level_rows + level * level_rows
        inner.append(mm(face_weights, out_ref[pl.ds(first, band_rows), :]))
    for copy in tracer_halos:
        copy.wait_recv()
    width = south_out.shape[2]
    south = pltpu.roll(south_ref[...], width, 2)
    south_out[...] = south[..., :width] * keep_south
    north_out[...] = north_ref[..., :width] * keep_north
    for copy in wind_halos:
        copy.wait_recv()
    for copy in tracer_halos + wind_halos:
        copy.wait_send()
    for level in range(2):
        merid = (
            inner[level]
            + south_weight * (vsouth_ref[pl.ds(level, 1), :] * keep_south)
            + north_weight * (vnorth_ref[pl.ds(level, 1), :] * keep_north)
        )
        merid_ref[level] = merid[:, : merid_ref.shape[2]]


def spectral_tables(n, rows, columns):
    lon_total = n * columns
    blocks = np.arange(n)
    phase = 2.0 * np.pi * (np.outer(blocks, blocks) % n) / n
    eye = np.eye(rows)
    column_ids = np.arange(columns)
    twist = 2.0 * np.pi * (np.outer(blocks, column_ids) % lon_total) / lon_total
    turn = 2.0 * np.pi * (np.outer(column_ids, column_ids) % columns) / columns
    wavenumber = blocks[:, None] + n * column_ids[None, :]
    sine = np.sin(wavenumber.astype(np.float32) * np.float32(math.pi / lon_total))
    divisor = np.where(wavenumber == 0, np.float32(1.0), sine * sine).astype(np.float32)
    zero_mode = (wavenumber == 0).astype(np.float32)
    widen = np.eye(columns, columns + 2)
    kron_cos, kron_sin = np.kron(np.cos(phase), eye), np.kron(np.sin(phase), eye)
    twist_wide = np.stack(
        [np.repeat(np.cos(twist), rows, axis=0) @ widen, np.repeat(np.sin(twist), rows, axis=0) @ widen]
    )
    tables = (
        np.concatenate([kron_cos, kron_sin], axis=0),
        np.concatenate([kron_cos, -kron_sin], axis=1),
        np.repeat(np.cos(twist), rows, axis=0),
        np.repeat(np.sin(twist), rows, axis=0),
        np.cos(turn),
        np.sin(turn),
        np.repeat(divisor, rows, axis=0),
        np.repeat(zero_mode, rows, axis=0),
        np.cos(turn) @ widen,
        np.sin(turn) @ widen,
        twist_wide,
    )
    return [jnp.asarray(t.astype(np.float32)) for t in tables]


def position_tables(n, rows, bands, lat_rows, flat_rows):
    lat_total = bands * lat_rows
    cells = np.arange(lat_total, dtype=np.float32)
    row_cosine = np.cos(
        (cells + np.float32(0.5)) * np.float32(math.pi / lat_total) - np.float32(0.5 * math.pi)
    ).astype(np.float32)
    scaled = ((row_cosine / np.float32(COS_FLOOR)) ** 2).astype(np.float32)
    own_rows = (np.arange(n)[:, None] * rows + np.arange(rows)[None, :]) % lat_rows
    scales = scaled[np.arange(bands)[:, None, None] * lat_rows + own_rows[None]]
    face_ids = np.arange(bands)[:, None] * lat_rows + np.arange(lat_rows + 1)[None, :]
    face_cosine = np.cos(
        face_ids.astype(np.float32) * np.float32(math.pi / lat_total) - np.float32(0.5 * math.pi)
    ).astype(np.float32)
    face_cosine = np.where((face_ids == 0) | (face_ids == lat_total), 0.0, face_cosine)
    halves = (np.float32(0.5) * face_cosine).astype(np.float32)
    return jnp.asarray(scales.reshape(-1)), jnp.asarray(halves.reshape(-1))


def exchange_all(flat_winds, lat_rows, tracers):
    flat_rows, columns = flat_winds.shape
    levels, lon_cols, merged = tracers.shape
    n = lax.axis_size("lon")
    rows = flat_rows // n
    tracer_count = merged // lat_rows
    scales, halves = position_tables(n, rows, lax.axis_size("lat"), lat_rows, flat_rows)
    pair_rows = np.zeros((columns + 2, columns + 1), np.float32)
    for face in range(columns + 1):
        pair_rows[columns if face == 0 else face - 1, face] = 0.5
        pair_rows[columns + 1 if face == columns else face, face] = 0.5
    vmem = pl.BlockSpec(memory_space=pltpu.VMEM)
    smem = pl.BlockSpec(memory_space=pltpu.SMEM)
    wide_lanes = -(-3 * tracer_count // 128) * 128
    west_cols = lon_cols - (lon_cols - 3) // 8 * 8
    shapes = [
        (flat_rows, columns),
        (levels, lat_rows, columns + 1),
        (levels, lat_rows + 1, columns),
        (levels, west_cols, merged),
        (levels, 8, merged),
        (levels, lon_cols, 3 * tracer_count),
        (levels, lon_cols, 3 * tracer_count),
    ]
    return pl.pallas_call(
        functools.partial(filter_kernel, n, rows),
        out_shape=[jax.ShapeDtypeStruct(shape, jnp.float32) for shape in shapes],
        in_specs=[vmem, smem]
        + [vmem] * 12
        + [smem, pl.BlockSpec(memory_space=pl.ANY)],
        out_specs=[vmem] * len(shapes),
        scratch_shapes=[
            pltpu.VMEM((flat_rows, columns + 2), jnp.float32),
            pltpu.VMEM((levels, lon_cols, wide_lanes), jnp.float32),
            pltpu.VMEM((levels, lon_cols, wide_lanes), jnp.float32),
            pltpu.VMEM((levels, columns + 2), jnp.float32),
            pltpu.VMEM((levels, columns + 2), jnp.float32),
            pltpu.VMEM((flat_rows, columns), jnp.float32),
            pltpu.VMEM((flat_rows, columns + 2), jnp.float32),
            pltpu.SemaphoreType.DMA((n,)),
            pltpu.SemaphoreType.DMA((n,)),
            pltpu.SemaphoreType.DMA((n,)),
            pltpu.SemaphoreType.DMA((n,)),
            pltpu.SemaphoreType.DMA((8,)),
            pltpu.SemaphoreType.DMA((8,)),
            pltpu.SemaphoreType.DMA((2,)),
        ],
        compiler_params=pltpu.CompilerParams(collective_id=0, has_side_effects=True),
    )(
        flat_winds,
        scales,
        *spectral_tables(n, rows, columns),
        jnp.asarray(pair_rows),
        halves,
        tracers,
    )


def stencil(padded, dim, faces, stride):

    def offset_cells(offset):
        return lax.slice_in_dim(padded, offset * stride, (offset + faces) * stride, axis=dim)

    left = (
        2.0 * offset_cells(0)
        - 13.0 * offset_cells(1)
        + 47.0 * offset_cells(2)
        + 27.0 * offset_cells(3)
        - 3.0 * offset_cells(4)
    ) / 60.0
    right = (
        2.0 * offset_cells(5)
        - 13.0 * offset_cells(4)
        + 47.0 * offset_cells(3)
        + 27.0 * offset_cells(2)
        - 3.0 * offset_cells(1)
    ) / 60.0
    return left, right


def spread(values, rows, tracer_count):
    lanes = jnp.arange(rows * tracer_count, dtype=jnp.int32) // tracer_count
    pick = (jnp.arange(rows, dtype=jnp.int32)[:, None] == lanes[None, :]).astype(jnp.float32)
    return jnp.einsum("ljc,jm->lcm", values, pick, precision=lax.Precision.HIGH)


def local(tracers, wind_field):
    levels, lon_cols, merged = tracers.shape
    lat_rows = wind_field.shape[2]
    tracer_count = merged // lat_rows
    lat_total = lat_rows * lax.axis_size("lat")
    band = lax.axis_index("lat")
    first_row = band * lat_rows
    row_ids = first_row + jnp.arange(lat_rows, dtype=jnp.int32)
    row_cosine = jnp.cos(
        (row_ids.astype(jnp.float32) + 0.5) * (math.pi / lat_total) - 0.5 * math.pi
    )
    flat_winds = wind_field.reshape(2 * levels * lat_rows, lon_cols)
    smoothed, zonal_speed, merid_speed, west, east, south, north = exchange_all(
        flat_winds, lat_rows, tracers
    )
    west = west[:, west.shape[1] - 3 :]
    east = east[:, :3]
    smoothed = smoothed.reshape(2, levels, lat_rows, lon_cols)
    zonal_rep = spread(zonal_speed, lat_rows, tracer_count)
    merid_rep = spread(merid_speed, lat_rows + 1, tracer_count)
    zonal_pad = jnp.concatenate([west, tracers, east], axis=1)
    left_x, right_x = stencil(zonal_pad, 1, lon_cols + 1, 1)
    zonal_flux = upwind(zonal_rep, left_x, right_x)
    merid_pad = jnp.concatenate([south, tracers, north], axis=2)
    left_y, right_y = stencil(merid_pad, 2, lat_rows + 1, tracer_count)
    merid_flux = upwind(merid_rep, left_y, right_y)
    metric = jnp.repeat(1.0 / jnp.maximum(row_cosine, COS_FLOOR), tracer_count)
    change = COURANT * (zonal_flux[:, 1:] - zonal_flux[:, :-1]) + COURANT * (
        merid_flux[:, :, tracer_count:] - merid_flux[:, :, :-tracer_count]
    )
    advected = tracers - metric[None, None, :] * change
    return (advected, smoothed)


def solution(mesh):
    placed = (P(None, "lon", "lat"), P(None, None, "lat", "lon"))
    return jax.shard_map(
        local,
        mesh=mesh,
        in_specs=placed,
        out_specs=(P(None, "lon", "lat"), P(None, None, "lat", "lon")),
        check_vma=False,
    )
```

```python
import functools
import math

import jax
import numpy as np
import jax.numpy as jnp
from jax import lax
from jax.experimental import pallas as pl
from jax.experimental.pallas import tpu as pltpu
from jax.sharding import PartitionSpec as P

MESH = pl.DeviceIdType.MESH

COURANT = 0.3
COS_FLOOR = 0.5
EXACT_MODE = lax.Precision.HIGHEST


def extended(array, sides, width, wrap):
    for axis, dim in sides:
        devices, length = (lax.axis_size(axis), array.shape[dim])
        up = [(i, (i + 1) % devices) for i in range(devices if wrap else devices - 1)]
        down = [(j, i) for i, j in up]
        last = lax.slice_in_dim(array, length - width, length, axis=dim)
        first = lax.slice_in_dim(array, 0, width, axis=dim)
        before = lax.ppermute(last, axis, up)
        after = lax.ppermute(first, axis, down)
        array = jnp.concatenate([before, array, after], axis=dim)
    return array


def damping(row_cosine, wavenumber, lon_total):
    sine = jnp.sin(wavenumber.astype(jnp.float32) * (math.pi / lon_total))
    divisor = jnp.where(wavenumber == 0, 1.0, sine * sine)
    scaled = (row_cosine / COS_FLOOR) ** 2
    scaled = scaled.reshape(scaled.shape + (1,) * wavenumber.ndim)
    return jnp.where(wavenumber == 0, 1.0, jnp.minimum(1.0, scaled / divisor))


def face_values(padded, axis, cells, stride):

    def offset_cells(offset):
        return lax.slice_in_dim(padded, offset * stride, (offset + cells + 1) * stride, axis=axis)

    left = (
        2.0 * offset_cells(0)
        - 13.0 * offset_cells(1)
        + 47.0 * offset_cells(2)
        + 27.0 * offset_cells(3)
        - 3.0 * offset_cells(4)
    ) / 60.0
    right = (
        2.0 * offset_cells(5)
        - 13.0 * offset_cells(4)
        + 47.0 * offset_cells(3)
        + 27.0 * offset_cells(2)
        - 3.0 * offset_cells(1)
    ) / 60.0
    return (left, right)


def upwind(speed, left, right):
    return jnp.maximum(speed, 0.0) * left + jnp.minimum(speed, 0.0) * right


def filter_kernel(n, rows, winds_ref, scales_ref, kc_ref, ks_ref, tc_ref, ts_ref, c_ref, s_ref,
                  divisor_ref, zero_ref, widen_ref, prev_ref, next_ref, pairs_ref, halves_ref,
                  tracers_ref,
                  smooth_ref, zonal_ref, merid_ref, west_ref, east_ref, south_out, north_out,
                  out_ref, south_ref, north_ref, vsouth_ref, vnorth_ref,
                  gathered, restored, send_a, recv_a, send_b, recv_b, halo_send, halo_recv, local_sem):
    me = lax.axis_index("lon")
    band = lax.axis_index("lat")
    bands = lax.axis_size("lat")
    up, down = lax.rem(band + 1, bands), lax.rem(band + bands - 1, bands)
    east_peer, west_peer = lax.rem(me + 1, n), lax.rem(me + n - 1, n)
    barrier = pltpu.get_barrier_semaphore()
    for k in range(1, n):
        peer = lax.rem(me + k, n)
        pl.semaphore_signal(barrier, inc=1, device_id=(band, peer), device_id_type=MESH)
    for other in (up, down):
        pl.semaphore_signal(barrier, inc=1, device_id=(other, me), device_id_type=MESH)
    pl.semaphore_wait(barrier, n + 1)

    cols, merged = tracers_ref.shape[1], tracers_ref.shape[2]
    lane_depth = south_ref.shape[2]
    flat_rows = out_ref.shape[0]
    level_rows = flat_rows // 4
    halo_plan = [
        (tracers_ref.at[:, pl.ds(cols - west_ref.shape[1], west_ref.shape[1]), :], west_ref, (band, east_peer)),
        (tracers_ref.at[:, pl.ds(0, east_ref.shape[1]), :], east_ref, (band, west_peer)),
        (tracers_ref.at[:, :, pl.ds(merged - lane_depth, lane_depth)], south_ref, (up, me)),
        (tracers_ref.at[:, :, pl.ds(0, lane_depth)], north_ref, (down, me)),
    ]
    for level in range(2):
        first = 2 * level_rows + level * level_rows
        halo_plan.append(
            (out_ref.at[pl.ds(first + level_rows - 1, 1)], vsouth_ref.at[pl.ds(level, 1)], (up, me))
        )
    for level in range(2):
        first = 2 * level_rows + level * level_rows
        halo_plan.append((out_ref.at[pl.ds(first, 1)], vnorth_ref.at[pl.ds(level, 1)], (down, me)))
    edge_rows = [2 * level_rows + k for k in (0, level_rows - 1, level_rows, 2 * level_rows - 1)]

    def halo_copy(index):
        source, target, device = halo_plan[index]
        return pltpu.make_async_remote_copy(
            src_ref=source,
            dst_ref=target,
            send_sem=halo_send.at[index],
            recv_sem=halo_recv.at[index],
            device_id=device,
            device_id_type=MESH,
        )

    def block(ref, index):
        return ref.at[pl.ds(pl.multiple_of(index * rows, rows), rows)]

    def swap(source, target, send_sem, recv_sem, slot):
        sends = []
        for k in range(1, n):
            peer = lax.rem(me + k, n)
            copy = pltpu.make_async_remote_copy(
                src_ref=block(source, peer),
                dst_ref=block(target, me),
                send_sem=send_sem.at[peer],
                recv_sem=recv_sem.at[me],
                device_id=(band, peer),
                device_id_type=MESH,
            )
            copy.start()
            sends.append(copy)
        own = pltpu.make_async_copy(block(source, me), block(target, me), local_sem.at[slot])
        own.start()
        return sends, own

    def settle(source, target, send_sem, recv_sem, sends, own):
        own.wait()
        for k in range(1, n):
            origin = lax.rem(me + n - k, n)
            pltpu.make_async_remote_copy(
                src_ref=block(source, origin),
                dst_ref=block(target, origin),
                send_sem=send_sem.at[origin],
                recv_sem=recv_sem.at[origin],
                device_id=(band, origin),
                device_id_type=MESH,
            ).wait_recv()
        for copy in sends:
            copy.wait_send()

    sends, own = swap(winds_ref, gathered, send_a, recv_a, 0)
    tracer_halos = [halo_copy(i) for i in range(4)]
    for copy in tracer_halos:
        copy.start()
    settle(winds_ref, gathered, send_a, recv_a, sends, own)

    def mm(a, b):
        return jnp.dot(a, b, precision=EXACT_MODE, preferred_element_type=jnp.float32)

    x = gathered[...]
    half = x.shape[0]
    tc, ts = tc_ref[...], ts_ref[...]
    stacked = mm(kc_ref[...], x)
    re, im = stacked[:half], -stacked[half:]
    shifted_re = re * tc + im * ts
    shifted_im = im * tc - re * ts
    stacked = jnp.concatenate([shifted_re, shifted_im], axis=0)
    with_cos = mm(stacked, c_ref[...])
    with_sin = mm(stacked, s_ref[...])
    modes_re = with_cos[:half] + with_sin[half:]
    modes_im = with_cos[half:] - with_sin[:half]
    lane_rows = lax.broadcasted_iota(jnp.int32, (n * rows, 1), 0) % rows
    base = (band * n + me) * rows
    scaled = jnp.zeros((n * rows, 1), jnp.float32)
    for r in range(rows):
        scaled = jnp.where(lane_rows == r, scales_ref[base + r], scaled)
    factor = jnp.where(zero_ref[...] > 0.0, 1.0, jnp.minimum(1.0, scaled / divisor_ref[...]))
    stacked = jnp.concatenate([modes_re * factor, modes_im * factor], axis=0)
    with_cos = mm(stacked, widen_ref[...])
    with_sin = mm(stacked, prev_ref[...])
    back_re = with_cos[:half] - with_sin[half:]
    back_im = with_cos[half:] + with_sin[:half]
    tcw, tsw = next_ref[0], next_ref[1]
    out_re = back_re * tcw - back_im * tsw
    out_im = back_im * tcw + back_re * tsw
    result = mm(ks_ref[...], jnp.concatenate([out_re, out_im], axis=0)) / (n * x.shape[1])
    columns = x.shape[1]
    lane = lax.broadcasted_iota(jnp.int32, result.shape, 1)
    before = jnp.sum(
        jnp.where(lane == columns - 1, jnp.roll(result, rows, axis=0), 0.0), axis=1, keepdims=True
    )
    after = jnp.sum(jnp.where(lane == 0, jnp.roll(result, -rows, axis=0), 0.0), axis=1, keepdims=True)
    restored[...] = jnp.where(lane == columns, before, jnp.where(lane == columns + 1, after, result))
    sends, own = swap(restored, out_ref, send_b, recv_b, 1)
    own.wait()
    holders = sorted({row // rows for row in edge_rows})

    def arrival(origin):
        return pltpu.make_async_remote_copy(
            src_ref=block(restored, origin),
            dst_ref=block(out_ref, origin),
            send_sem=send_b.at[origin],
            recv_sem=recv_b.at[origin],
            device_id=(band, origin),
            device_id_type=MESH,
        )

    for holder in holders:

        @pl.when(me != holder)
        def _():
            arrival(holder).wait_recv()

    wind_halos = [halo_copy(i) for i in range(4, 8)]
    for copy in wind_halos:
        copy.start()
    for k in range(1, n):
        origin = lax.rem(me + n - k, n)
        pending = origin >= 0
        for holder in holders:
            pending = jnp.logical_and(pending, origin != holder)

        @pl.when(pending)
        def _():
            arrival(origin).wait_recv()

    for copy in sends:
        copy.wait_send()
    smooth_ref[...] = out_ref[:, : smooth_ref.shape[1]]
    keep_south = jnp.where(band > 0, 1.0, 0.0)
    keep_north = jnp.where(band < bands - 1, 1.0, 0.0)
    band_rows = level_rows
    face_ids = lax.broadcasted_iota(jnp.int32, (band_rows + 1, 1), 0)
    half = jnp.zeros((band_rows + 1, 1), jnp.float32)
    for face in range(band_rows + 1):
        half = jnp.where(face_ids == face, halves_ref[band * (band_rows + 1) + face], half)
    faces = lax.broadcasted_iota(jnp.int32, (band_rows + 1, band_rows), 0)
    cells = lax.broadcasted_iota(jnp.int32, (band_rows + 1, band_rows), 1)
    face_weights = jnp.where((cells == faces - 1) | (cells == faces), half, 0.0)
    south_weight = jnp.where(face_ids == 0, half, 0.0)
    north_weight = jnp.where(face_ids == band_rows, half, 0.0)
    inner = []
    for level in range(2):
        east_rows = out_ref[pl.ds(level * band_rows, band_rows), :]
        zonal_ref[level] = mm(east_rows, pairs_ref[...])
        first = 2 * level_rows + level * level_rows
        inner.append(mm(face_weights, out_ref[pl.ds(first, band_rows), :]))
    for copy in tracer_halos:
        copy.wait_recv()
    width = south_out.shape[2]
    south = pltpu.roll(south_ref[...], width, 2)
    south_out[...] = south[..., :width] * keep_south
    north_out[...] = north_ref[..., :width] * keep_north
    for copy in wind_halos:
        copy.wait_recv()
    for copy in tracer_halos + wind_halos:
        copy.wait_send()
    for level in range(2):
        merid = (
            inner[level]
            + south_weight * (vsouth_ref[pl.ds(level, 1), :] * keep_south)
            + north_weight * (vnorth_ref[pl.ds(level, 1), :] * keep_north)
        )
        merid_ref[level] = merid[:, : merid_ref.shape[2]]


def spectral_tables(n, rows, columns):
    lon_total = n * columns
    blocks = np.arange(n)
    phase = 2.0 * np.pi * (np.outer(blocks, blocks) % n) / n
    eye = np.eye(rows)
    column_ids = np.arange(columns)
    twist = 2.0 * np.pi * (np.outer(blocks, column_ids) % lon_total) / lon_total
    turn = 2.0 * np.pi * (np.outer(column_ids, column_ids) % columns) / columns
    wavenumber = blocks[:, None] + n * column_ids[None, :]
    sine = np.sin(wavenumber.astype(np.float32) * np.float32(math.pi / lon_total))
    divisor = np.where(wavenumber == 0, np.float32(1.0), sine * sine).astype(np.float32)
    zero_mode = (wavenumber == 0).astype(np.float32)
    widen = np.eye(columns, columns + 2)
    kron_cos, kron_sin = np.kron(np.cos(phase), eye), np.kron(np.sin(phase), eye)
    twist_wide = np.stack(
        [np.repeat(np.cos(twist), rows, axis=0) @ widen, np.repeat(np.sin(twist), rows, axis=0) @ widen]
    )
    tables = (
        np.concatenate([kron_cos, kron_sin], axis=0),
        np.concatenate([kron_cos, -kron_sin], axis=1),
        np.repeat(np.cos(twist), rows, axis=0),
        np.repeat(np.sin(twist), rows, axis=0),
        np.cos(turn),
        np.sin(turn),
        np.repeat(divisor, rows, axis=0),
        np.repeat(zero_mode, rows, axis=0),
        np.cos(turn) @ widen,
        np.sin(turn) @ widen,
        twist_wide,
    )
    return [jnp.asarray(t.astype(np.float32)) for t in tables]


def position_tables(n, rows, bands, lat_rows, flat_rows):
    lat_total = bands * lat_rows
    cells = np.arange(lat_total, dtype=np.float32)
    row_cosine = np.cos(
        (cells + np.float32(0.5)) * np.float32(math.pi / lat_total) - np.float32(0.5 * math.pi)
    ).astype(np.float32)
    scaled = ((row_cosine / np.float32(COS_FLOOR)) ** 2).astype(np.float32)
    own_rows = (np.arange(n)[:, None] * rows + np.arange(rows)[None, :]) % lat_rows
    scales = scaled[np.arange(bands)[:, None, None] * lat_rows + own_rows[None]]
    face_ids = np.arange(bands)[:, None] * lat_rows + np.arange(lat_rows + 1)[None, :]
    face_cosine = np.cos(
        face_ids.astype(np.float32) * np.float32(math.pi / lat_total) - np.float32(0.5 * math.pi)
    ).astype(np.float32)
    face_cosine = np.where((face_ids == 0) | (face_ids == lat_total), 0.0, face_cosine)
    halves = (np.float32(0.5) * face_cosine).astype(np.float32)
    return jnp.asarray(scales.reshape(-1)), jnp.asarray(halves.reshape(-1))


def exchange_all(flat_winds, lat_rows, tracers):
    flat_rows, columns = flat_winds.shape
    levels, lon_cols, merged = tracers.shape
    n = lax.axis_size("lon")
    rows = flat_rows // n
    tracer_count = merged // lat_rows
    scales, halves = position_tables(n, rows, lax.axis_size("lat"), lat_rows, flat_rows)
    pair_rows = np.zeros((columns + 2, columns + 1), np.float32)
    for face in range(columns + 1):
        pair_rows[columns if face == 0 else face - 1, face] = 0.5
        pair_rows[columns + 1 if face == columns else face, face] = 0.5
    vmem = pl.BlockSpec(memory_space=pltpu.VMEM)
    smem = pl.BlockSpec(memory_space=pltpu.SMEM)
    wide_lanes = -(-3 * tracer_count // 128) * 128
    west_cols = lon_cols - (lon_cols - 3) // 8 * 8
    shapes = [
        (flat_rows, columns),
        (levels, lat_rows, columns + 1),
        (levels, lat_rows + 1, columns),
        (levels, west_cols, merged),
        (levels, 8, merged),
        (levels, lon_cols, 3 * tracer_count),
        (levels, lon_cols, 3 * tracer_count),
    ]
    return pl.pallas_call(
        functools.partial(filter_kernel, n, rows),
        out_shape=[jax.ShapeDtypeStruct(shape, jnp.float32) for shape in shapes],
        in_specs=[vmem, smem]
        + [vmem] * 12
        + [smem, pl.BlockSpec(memory_space=pl.ANY)],
        out_specs=[vmem] * len(shapes),
        scratch_shapes=[
            pltpu.VMEM((flat_rows, columns + 2), jnp.float32),
            pltpu.VMEM((levels, lon_cols, wide_lanes), jnp.float32),
            pltpu.VMEM((levels, lon_cols, wide_lanes), jnp.float32),
            pltpu.VMEM((levels, columns + 2), jnp.float32),
            pltpu.VMEM((levels, columns + 2), jnp.float32),
            pltpu.VMEM((flat_rows, columns), jnp.float32),
            pltpu.VMEM((flat_rows, columns + 2), jnp.float32),
            pltpu.SemaphoreType.DMA((n,)),
            pltpu.SemaphoreType.DMA((n,)),
            pltpu.SemaphoreType.DMA((n,)),
            pltpu.SemaphoreType.DMA((n,)),
            pltpu.SemaphoreType.DMA((8,)),
            pltpu.SemaphoreType.DMA((8,)),
            pltpu.SemaphoreType.DMA((2,)),
        ],
        compiler_params=pltpu.CompilerParams(collective_id=0, has_side_effects=True),
    )(
        flat_winds,
        scales,
        *spectral_tables(n, rows, columns),
        jnp.asarray(pair_rows),
        halves,
        tracers,
    )


def stencil(padded, dim, faces, stride):

    def offset_cells(offset):
        return lax.slice_in_dim(padded, offset * stride, (offset + faces) * stride, axis=dim)

    left = (
        2.0 * offset_cells(0)
        - 13.0 * offset_cells(1)
        + 47.0 * offset_cells(2)
        + 27.0 * offset_cells(3)
        - 3.0 * offset_cells(4)
    ) / 60.0
    right = (
        2.0 * offset_cells(5)
        - 13.0 * offset_cells(4)
        + 47.0 * offset_cells(3)
        + 27.0 * offset_cells(2)
        - 3.0 * offset_cells(1)
    ) / 60.0
    return left, right


def spread(values, rows, tracer_count):
    lanes = jnp.arange(rows * tracer_count, dtype=jnp.int32) // tracer_count
    pick = (jnp.arange(rows, dtype=jnp.int32)[:, None] == lanes[None, :]).astype(jnp.float32)
    return jnp.einsum("ljc,jm->lcm", values, pick, precision=EXACT_MODE)


def local(tracers, wind_field):
    levels, lon_cols, merged = tracers.shape
    lat_rows = wind_field.shape[2]
    tracer_count = merged // lat_rows
    lat_total = lat_rows * lax.axis_size("lat")
    band = lax.axis_index("lat")
    first_row = band * lat_rows
    row_ids = first_row + jnp.arange(lat_rows, dtype=jnp.int32)
    row_cosine = jnp.cos(
        (row_ids.astype(jnp.float32) + 0.5) * (math.pi / lat_total) - 0.5 * math.pi
    )
    flat_winds = wind_field.reshape(2 * levels * lat_rows, lon_cols)
    smoothed, zonal_speed, merid_speed, west, east, south, north = exchange_all(
        flat_winds, lat_rows, tracers
    )
    west = west[:, west.shape[1] - 3 :]
    east = east[:, :3]
    smoothed = smoothed.reshape(2, levels, lat_rows, lon_cols)
    zonal_rep = spread(zonal_speed, lat_rows, tracer_count)
    merid_rep = lax.optimization_barrier(spread(merid_speed, lat_rows + 1, tracer_count))
    zonal_pad = jnp.concatenate([west, tracers, east], axis=1)
    left_x, right_x = stencil(zonal_pad, 1, lon_cols + 1, 1)
    zonal_flux = upwind(zonal_rep, left_x, right_x)
    merid_pad = jnp.concatenate([south, tracers, north], axis=2)
    left_y, right_y = stencil(merid_pad, 2, lat_rows + 1, tracer_count)
    merid_flux = upwind(merid_rep, left_y, right_y)
    metric = jnp.repeat(1.0 / jnp.maximum(row_cosine, COS_FLOOR), tracer_count)
    change = COURANT * (zonal_flux[:, 1:] - zonal_flux[:, :-1]) + COURANT * (
        merid_flux[:, :, tracer_count:] - merid_flux[:, :, :-tracer_count]
    )
    advected = tracers - metric[None, None, :] * change
    return (advected, smoothed)


def solution(mesh):
    placed = (P(None, "lon", "lat"), P(None, None, "lat", "lon"))
    return jax.shard_map(
        local,
        mesh=mesh,
        in_specs=placed,
        out_specs=(P(None, "lon", "lat"), P(None, None, "lat", "lon")),
        check_vma=False,
    )
```

```python
import functools
import math

import jax
import numpy as np
import jax.numpy as jnp
from jax import lax
from jax.experimental import pallas as pl
from jax.experimental.pallas import tpu as pltpu
from jax.sharding import PartitionSpec as P

MESH = pl.DeviceIdType.MESH

COURANT = 0.3
COS_FLOOR = 0.5
EXACT_MODE = lax.Precision.HIGHEST


def extended(array, sides, width, wrap):
    for axis, dim in sides:
        devices, length = (lax.axis_size(axis), array.shape[dim])
        up = [(i, (i + 1) % devices) for i in range(devices if wrap else devices - 1)]
        down = [(j, i) for i, j in up]
        last = lax.slice_in_dim(array, length - width, length, axis=dim)
        first = lax.slice_in_dim(array, 0, width, axis=dim)
        before = lax.ppermute(last, axis, up)
        after = lax.ppermute(first, axis, down)
        array = jnp.concatenate([before, array, after], axis=dim)
    return array


def damping(row_cosine, wavenumber, lon_total):
    sine = jnp.sin(wavenumber.astype(jnp.float32) * (math.pi / lon_total))
    divisor = jnp.where(wavenumber == 0, 1.0, sine * sine)
    scaled = (row_cosine / COS_FLOOR) ** 2
    scaled = scaled.reshape(scaled.shape + (1,) * wavenumber.ndim)
    return jnp.where(wavenumber == 0, 1.0, jnp.minimum(1.0, scaled / divisor))


def face_values(padded, axis, cells, stride):

    def offset_cells(offset):
        return lax.slice_in_dim(padded, offset * stride, (offset + cells + 1) * stride, axis=axis)

    left = (
        2.0 * offset_cells(0)
        - 13.0 * offset_cells(1)
        + 47.0 * offset_cells(2)
        + 27.0 * offset_cells(3)
        - 3.0 * offset_cells(4)
    ) / 60.0
    right = (
        2.0 * offset_cells(5)
        - 13.0 * offset_cells(4)
        + 47.0 * offset_cells(3)
        + 27.0 * offset_cells(2)
        - 3.0 * offset_cells(1)
    ) / 60.0
    return (left, right)


def upwind(speed, left, right):
    return jnp.maximum(speed, 0.0) * left + jnp.minimum(speed, 0.0) * right


def filter_kernel(n, rows, winds_ref, scales_ref, kc_ref, ks_ref, tc_ref, ts_ref, c_ref, s_ref,
                  divisor_ref, zero_ref, widen_ref, prev_ref, next_ref, pairs_ref, halves_ref,
                  tracers_ref,
                  smooth_ref, zonal_ref, merid_ref, west_ref, east_ref, south_out, north_out,
                  out_ref, south_ref, north_ref, vsouth_ref, vnorth_ref,
                  gathered, restored, send_a, recv_a, send_b, recv_b, halo_send, halo_recv, local_sem):
    me = lax.axis_index("lon")
    band = lax.axis_index("lat")
    bands = lax.axis_size("lat")
    up, down = lax.rem(band + 1, bands), lax.rem(band + bands - 1, bands)
    east_peer, west_peer = lax.rem(me + 1, n), lax.rem(me + n - 1, n)
    barrier = pltpu.get_barrier_semaphore()
    for k in range(1, n):
        peer = lax.rem(me + k, n)
        pl.semaphore_signal(barrier, inc=1, device_id=(band, peer), device_id_type=MESH)
    for other in (up, down):
        pl.semaphore_signal(barrier, inc=1, device_id=(other, me), device_id_type=MESH)
    pl.semaphore_wait(barrier, n + 1)

    cols, merged = tracers_ref.shape[1], tracers_ref.shape[2]
    lane_depth = south_ref.shape[2]
    flat_rows = out_ref.shape[0]
    level_rows = flat_rows // 4
    halo_plan = [
        (tracers_ref.at[:, pl.ds(cols - west_ref.shape[1], west_ref.shape[1]), :], west_ref, (band, east_peer)),
        (tracers_ref.at[:, pl.ds(0, east_ref.shape[1]), :], east_ref, (band, west_peer)),
        (tracers_ref.at[:, :, pl.ds(merged - lane_depth, lane_depth)], south_ref, (up, me)),
        (tracers_ref.at[:, :, pl.ds(0, lane_depth)], north_ref, (down, me)),
    ]
    for level in range(2):
        first = 2 * level_rows + level * level_rows
        halo_plan.append(
            (out_ref.at[pl.ds(first + level_rows - 1, 1)], vsouth_ref.at[pl.ds(level, 1)], (up, me))
        )
    for level in range(2):
        first = 2 * level_rows + level * level_rows
        halo_plan.append((out_ref.at[pl.ds(first, 1)], vnorth_ref.at[pl.ds(level, 1)], (down, me)))
    edge_rows = [2 * level_rows + k for k in (0, level_rows - 1, level_rows, 2 * level_rows - 1)]

    def halo_copy(index):
        source, target, device = halo_plan[index]
        return pltpu.make_async_remote_copy(
            src_ref=source,
            dst_ref=target,
            send_sem=halo_send.at[index],
            recv_sem=halo_recv.at[index],
            device_id=device,
            device_id_type=MESH,
        )

    def block(ref, index):
        return ref.at[pl.ds(pl.multiple_of(index * rows, rows), rows)]

    def swap(source, target, send_sem, recv_sem, slot):
        sends = []
        for k in range(1, n):
            peer = lax.rem(me + k, n)
            copy = pltpu.make_async_remote_copy(
                src_ref=block(source, peer),
                dst_ref=block(target, me),
                send_sem=send_sem.at[peer],
                recv_sem=recv_sem.at[me],
                device_id=(band, peer),
                device_id_type=MESH,
            )
            copy.start()
            sends.append(copy)
        own = pltpu.make_async_copy(block(source, me), block(target, me), local_sem.at[slot])
        own.start()
        return sends, own

    def settle(source, target, send_sem, recv_sem, sends, own):
        own.wait()
        for k in range(1, n):
            origin = lax.rem(me + n - k, n)
            pltpu.make_async_remote_copy(
                src_ref=block(source, origin),
                dst_ref=block(target, origin),
                send_sem=send_sem.at[origin],
                recv_sem=recv_sem.at[origin],
                device_id=(band, origin),
                device_id_type=MESH,
            ).wait_recv()
        for copy in sends:
            copy.wait_send()

    sends, own = swap(winds_ref, gathered, send_a, recv_a, 0)
    tracer_halos = [halo_copy(i) for i in range(4)]
    for copy in tracer_halos:
        copy.start()
    settle(winds_ref, gathered, send_a, recv_a, sends, own)

    def mm(a, b):
        return jnp.dot(a, b, precision=EXACT_MODE, preferred_element_type=jnp.float32)

    x = gathered[...]
    half = x.shape[0]
    tc, ts = tc_ref[...], ts_ref[...]
    stacked = mm(kc_ref[...], x)
    re, im = stacked[:half], -stacked[half:]
    shifted_re = re * tc + im * ts
    shifted_im = im * tc - re * ts
    stacked = jnp.concatenate([shifted_re, shifted_im], axis=0)
    with_cos = mm(stacked, c_ref[...])
    with_sin = mm(stacked, s_ref[...])
    modes_re = with_cos[:half] + with_sin[half:]
    modes_im = with_cos[half:] - with_sin[:half]
    lane_rows = lax.broadcasted_iota(jnp.int32, (n * rows, 1), 0) % rows
    base = (band * n + me) * rows
    scaled = jnp.zeros((n * rows, 1), jnp.float32)
    for r in range(rows):
        scaled = jnp.where(lane_rows == r, scales_ref[base + r], scaled)
    factor = jnp.where(zero_ref[...] > 0.0, 1.0, jnp.minimum(1.0, scaled / divisor_ref[...]))
    stacked = jnp.concatenate([modes_re * factor, modes_im * factor], axis=0)
    with_cos = mm(stacked, widen_ref[...])
    with_sin = mm(stacked, prev_ref[...])
    back_re = with_cos[:half] - with_sin[half:]
    back_im = with_cos[half:] + with_sin[:half]
    tcw, tsw = next_ref[0], next_ref[1]
    out_re = back_re * tcw - back_im * tsw
    out_im = back_im * tcw + back_re * tsw
    result = mm(ks_ref[...], jnp.concatenate([out_re, out_im], axis=0)) / (n * x.shape[1])
    columns = x.shape[1]
    lane = lax.broadcasted_iota(jnp.int32, result.shape, 1)
    before = jnp.sum(
        jnp.where(lane == columns - 1, jnp.roll(result, rows, axis=0), 0.0), axis=1, keepdims=True
    )
    after = jnp.sum(jnp.where(lane == 0, jnp.roll(result, -rows, axis=0), 0.0), axis=1, keepdims=True)
    restored[...] = jnp.where(lane == columns, before, jnp.where(lane == columns + 1, after, result))
    sends, own = swap(restored, out_ref, send_b, recv_b, 1)
    own.wait()
    holders = sorted({row // rows for row in edge_rows})

    def arrival(origin):
        return pltpu.make_async_remote_copy(
            src_ref=block(restored, origin),
            dst_ref=block(out_ref, origin),
            send_sem=send_b.at[origin],
            recv_sem=recv_b.at[origin],
            device_id=(band, origin),
            device_id_type=MESH,
        )

    for holder in holders:

        @pl.when(me != holder)
        def _():
            arrival(holder).wait_recv()

    wind_halos = [halo_copy(i) for i in range(4, 8)]
    for copy in wind_halos:
        copy.start()
    for k in range(1, n):
        origin = lax.rem(me + n - k, n)
        pending = origin >= 0
        for holder in holders:
            pending = jnp.logical_and(pending, origin != holder)

        @pl.when(pending)
        def _():
            arrival(origin).wait_recv()

    for copy in sends:
        copy.wait_send()
    smooth_ref[...] = out_ref[:, : smooth_ref.shape[1]]
    keep_south = jnp.where(band > 0, 1.0, 0.0)
    keep_north = jnp.where(band < bands - 1, 1.0, 0.0)
    band_rows = level_rows
    face_ids = lax.broadcasted_iota(jnp.int32, (band_rows + 1, 1), 0)
    half = jnp.zeros((band_rows + 1, 1), jnp.float32)
    for face in range(band_rows + 1):
        half = jnp.where(face_ids == face, halves_ref[band * (band_rows + 1) + face], half)
    faces = lax.broadcasted_iota(jnp.int32, (band_rows + 1, band_rows), 0)
    cells = lax.broadcasted_iota(jnp.int32, (band_rows + 1, band_rows), 1)
    face_weights = jnp.where((cells == faces - 1) | (cells == faces), half, 0.0)
    south_weight = jnp.where(face_ids == 0, half, 0.0)
    north_weight = jnp.where(face_ids == band_rows, half, 0.0)
    inner = []
    for level in range(2):
        east_rows = out_ref[pl.ds(level * band_rows, band_rows), :]
        zonal_ref[level] = mm(east_rows, pairs_ref[...])
        first = 2 * level_rows + level * level_rows
        inner.append(mm(face_weights, out_ref[pl.ds(first, band_rows), :]))
    for copy in tracer_halos:
        copy.wait_recv()
    width = south_out.shape[2]
    south = pltpu.roll(south_ref[...], width, 2)
    south_out[...] = south[..., :width] * keep_south
    north_out[...] = north_ref[..., :width] * keep_north
    for copy in wind_halos:
        copy.wait_recv()
    for copy in tracer_halos + wind_halos:
        copy.wait_send()
    for level in range(2):
        merid = (
            inner[level]
            + south_weight * (vsouth_ref[pl.ds(level, 1), :] * keep_south)
            + north_weight * (vnorth_ref[pl.ds(level, 1), :] * keep_north)
        )
        merid_ref[level] = merid[:, : merid_ref.shape[2]]


def spectral_tables(n, rows, columns):
    lon_total = n * columns
    blocks = np.arange(n)
    phase = 2.0 * np.pi * (np.outer(blocks, blocks) % n) / n
    eye = np.eye(rows)
    column_ids = np.arange(columns)
    twist = 2.0 * np.pi * (np.outer(blocks, column_ids) % lon_total) / lon_total
    turn = 2.0 * np.pi * (np.outer(column_ids, column_ids) % columns) / columns
    wavenumber = blocks[:, None] + n * column_ids[None, :]
    sine = np.sin(wavenumber.astype(np.float32) * np.float32(math.pi / lon_total))
    divisor = np.where(wavenumber == 0, np.float32(1.0), sine * sine).astype(np.float32)
    zero_mode = (wavenumber == 0).astype(np.float32)
    widen = np.eye(columns, columns + 2)
    kron_cos, kron_sin = np.kron(np.cos(phase), eye), np.kron(np.sin(phase), eye)
    twist_wide = np.stack(
        [np.repeat(np.cos(twist), rows, axis=0) @ widen, np.repeat(np.sin(twist), rows, axis=0) @ widen]
    )
    tables = (
        np.concatenate([kron_cos, kron_sin], axis=0),
        np.concatenate([kron_cos, -kron_sin], axis=1),
        np.repeat(np.cos(twist), rows, axis=0),
        np.repeat(np.sin(twist), rows, axis=0),
        np.cos(turn),
        np.sin(turn),
        np.repeat(divisor, rows, axis=0),
        np.repeat(zero_mode, rows, axis=0),
        np.cos(turn) @ widen,
        np.sin(turn) @ widen,
        twist_wide,
    )
    return [jnp.asarray(t.astype(np.float32)) for t in tables]


def position_tables(n, rows, bands, lat_rows, flat_rows):
    lat_total = bands * lat_rows
    cells = np.arange(lat_total, dtype=np.float32)
    row_cosine = np.cos(
        (cells + np.float32(0.5)) * np.float32(math.pi / lat_total) - np.float32(0.5 * math.pi)
    ).astype(np.float32)
    scaled = ((row_cosine / np.float32(COS_FLOOR)) ** 2).astype(np.float32)
    own_rows = (np.arange(n)[:, None] * rows + np.arange(rows)[None, :]) % lat_rows
    scales = scaled[np.arange(bands)[:, None, None] * lat_rows + own_rows[None]]
    face_ids = np.arange(bands)[:, None] * lat_rows + np.arange(lat_rows + 1)[None, :]
    face_cosine = np.cos(
        face_ids.astype(np.float32) * np.float32(math.pi / lat_total) - np.float32(0.5 * math.pi)
    ).astype(np.float32)
    face_cosine = np.where((face_ids == 0) | (face_ids == lat_total), 0.0, face_cosine)
    halves = (np.float32(0.5) * face_cosine).astype(np.float32)
    return jnp.asarray(scales.reshape(-1)), jnp.asarray(halves.reshape(-1))


def exchange_all(flat_winds, lat_rows, tracers):
    flat_rows, columns = flat_winds.shape
    levels, lon_cols, merged = tracers.shape
    n = lax.axis_size("lon")
    rows = flat_rows // n
    tracer_count = merged // lat_rows
    scales, halves = position_tables(n, rows, lax.axis_size("lat"), lat_rows, flat_rows)
    pair_rows = np.zeros((columns + 2, columns + 1), np.float32)
    for face in range(columns + 1):
        pair_rows[columns if face == 0 else face - 1, face] = 0.5
        pair_rows[columns + 1 if face == columns else face, face] = 0.5
    vmem = pl.BlockSpec(memory_space=pltpu.VMEM)
    smem = pl.BlockSpec(memory_space=pltpu.SMEM)
    wide_lanes = -(-3 * tracer_count // 128) * 128
    west_cols = lon_cols - (lon_cols - 3) // 8 * 8
    shapes = [
        (flat_rows, columns),
        (levels, lat_rows, columns + 1),
        (levels, lat_rows + 1, columns),
        (levels, west_cols, merged),
        (levels, 8, merged),
        (levels, lon_cols, 3 * tracer_count),
        (levels, lon_cols, 3 * tracer_count),
    ]
    return pl.pallas_call(
        functools.partial(filter_kernel, n, rows),
        out_shape=[jax.ShapeDtypeStruct(shape, jnp.float32) for shape in shapes],
        in_specs=[vmem, smem]
        + [vmem] * 12
        + [smem, pl.BlockSpec(memory_space=pl.ANY)],
        out_specs=[vmem] * len(shapes),
        scratch_shapes=[
            pltpu.VMEM((flat_rows, columns + 2), jnp.float32),
            pltpu.VMEM((levels, lon_cols, wide_lanes), jnp.float32),
            pltpu.VMEM((levels, lon_cols, wide_lanes), jnp.float32),
            pltpu.VMEM((levels, columns + 2), jnp.float32),
            pltpu.VMEM((levels, columns + 2), jnp.float32),
            pltpu.VMEM((flat_rows, columns), jnp.float32),
            pltpu.VMEM((flat_rows, columns + 2), jnp.float32),
            pltpu.SemaphoreType.DMA((n,)),
            pltpu.SemaphoreType.DMA((n,)),
            pltpu.SemaphoreType.DMA((n,)),
            pltpu.SemaphoreType.DMA((n,)),
            pltpu.SemaphoreType.DMA((8,)),
            pltpu.SemaphoreType.DMA((8,)),
            pltpu.SemaphoreType.DMA((2,)),
        ],
        compiler_params=pltpu.CompilerParams(collective_id=0, has_side_effects=True),
    )(
        flat_winds,
        scales,
        *spectral_tables(n, rows, columns),
        jnp.asarray(pair_rows),
        halves,
        tracers,
    )


def stencil(padded, dim, faces, stride):

    def offset_cells(offset):
        return lax.slice_in_dim(padded, offset * stride, (offset + faces) * stride, axis=dim)

    left = (
        2.0 * offset_cells(0)
        - 13.0 * offset_cells(1)
        + 47.0 * offset_cells(2)
        + 27.0 * offset_cells(3)
        - 3.0 * offset_cells(4)
    ) / 60.0
    right = (
        2.0 * offset_cells(5)
        - 13.0 * offset_cells(4)
        + 47.0 * offset_cells(3)
        + 27.0 * offset_cells(2)
        - 3.0 * offset_cells(1)
    ) / 60.0
    return left, right


def spread(values, rows, tracer_count):
    lanes = jnp.arange(rows * tracer_count, dtype=jnp.int32) // tracer_count
    pick = (jnp.arange(rows, dtype=jnp.int32)[:, None] == lanes[None, :]).astype(jnp.float32)
    return jnp.einsum("ljc,jm->lcm", values, pick, precision=EXACT_MODE)


def local(tracers, wind_field):
    levels, lon_cols, merged = tracers.shape
    lat_rows = wind_field.shape[2]
    tracer_count = merged // lat_rows
    lat_total = lat_rows * lax.axis_size("lat")
    band = lax.axis_index("lat")
    first_row = band * lat_rows
    row_ids = first_row + jnp.arange(lat_rows, dtype=jnp.int32)
    row_cosine = jnp.cos(
        (row_ids.astype(jnp.float32) + 0.5) * (math.pi / lat_total) - 0.5 * math.pi
    )
    flat_winds = wind_field.reshape(2 * levels * lat_rows, lon_cols)
    smoothed, zonal_speed, merid_speed, west, east, south, north = exchange_all(
        flat_winds, lat_rows, tracers
    )
    west = west[:, west.shape[1] - 3 :]
    east = east[:, :3]
    smoothed = smoothed.reshape(2, levels, lat_rows, lon_cols)
    zonal_rep = lax.optimization_barrier(spread(zonal_speed, lat_rows, tracer_count))
    merid_rep = lax.optimization_barrier(spread(merid_speed, lat_rows + 1, tracer_count))
    zonal_pad = jnp.concatenate([west, tracers, east], axis=1)
    left_x, right_x = stencil(zonal_pad, 1, lon_cols + 1, 1)
    zonal_flux = upwind(zonal_rep, left_x, right_x)
    merid_pad = jnp.concatenate([south, tracers, north], axis=2)
    left_y, right_y = stencil(merid_pad, 2, lat_rows + 1, tracer_count)
    merid_flux = upwind(merid_rep, left_y, right_y)
    metric = jnp.repeat(1.0 / jnp.maximum(row_cosine, COS_FLOOR), tracer_count)
    change = COURANT * (zonal_flux[:, 1:] - zonal_flux[:, :-1]) + COURANT * (
        merid_flux[:, :, tracer_count:] - merid_flux[:, :, :-tracer_count]
    )
    advected = tracers - metric[None, None, :] * change
    return (advected, smoothed)


def solution(mesh):
    placed = (P(None, "lon", "lat"), P(None, None, "lat", "lon"))
    return jax.shard_map(
        local,
        mesh=mesh,
        in_specs=placed,
        out_specs=(P(None, "lon", "lat"), P(None, None, "lat", "lon")),
        check_vma=False,
    )
```
